32 devices in a mesh: groups: 2 (over y), trades: 8 (over z, x), dates: 2 (over core).
Axes of the slice: x: 2, y: 2, z: 4, core: 2. Of those that a mesh axis runs over, the one named last changes fastest.
Arguments:
- basis_values: bfloat16 [8, 256, 256], P('dates', 'groups'), parts along dimension 1, may hold values from -6 to 6
- coefficients: bfloat16 [8192, 256], P('trades'), may hold values from -0.0625 to 0.0625
- set_map: int32 [8192], P('trades'), may hold values from 0 to 255, as said below
- trade_type: int32 [8192], P('trades'), may hold values from 0 to 15
- type_gain: float32 [8, 16], P('dates'), may hold values from 0.25 to 4
- set_lags: int32 [256], replicated, may hold values from 1 to 2
- thresholds: float32 [256], replicated, may hold values from -1 to 1
Outputs:
- coef_grad: float32 [16384, 256], P(('groups', 'trades'), 'dates'), parts along dimension 0
The draws below stay inside these ranges and needn't reach their ends.
There are 2 independent parts, one for each index of `groups`. The reference program is written for one: setup_inputs(seed, part) draws one part's arguments, and reference() takes and returns one part's arrays. A program takes and returns all parts, laid end to end along the dimension named above; an argument that names none is the same for every part. Nothing has to cross between parts.
Inputs may be any that keep to these rules, and one draw needn't show every extreme that they name: `set_map`: in every aligned block of 1024 trades, exactly 128 trades fall in each group of 32 consecutive netting sets (sets g * 32 to (g + 1) * 32 - 1).
All inputs are finite; a program needn't handle non-finite values.
Results may differ from the reference program's by a relative error of at most 0.0018.
Values may be sent and summed in bfloat16 or wider, within the bound.
A program may use at most 64 MiB of HBM per device.

```python
import math
import jax
import jax.numpy as jnp
from jax import lax

K = 256
NSETS = 256
NTYPE = 16
LAG_MAX = 2
TR_DEV = 1024
TRADES = 8192
PATHS = 128
DATES = 8


def draw_set_map(key, part):
    block_count = TRADES // TR_DEV
    per_group = TR_DEV // block_count
    group_sets = NSETS // block_count
    first_key = jax.random.fold_in(key, 11)
    second_key = jax.random.fold_in(key, 23)
    groups_base = jnp.tile(jnp.arange(block_count, dtype=jnp.int32), per_group)
    block_keys = jax.random.split(first_key, block_count)
    shuffled = jax.vmap(lambda one_key: jax.random.permutation(one_key, groups_base))(block_keys)
    within = jax.random.randint(second_key, (TRADES,), 0, group_sets, dtype=jnp.int32)
    return (shuffled.reshape(TRADES) * group_sets + within).astype(jnp.int32)


def place_ends(drawn, rng, least, high):
    index_at = [jax.random.randint(jax.random.fold_in(rng, axis), (), 0, length) for axis, length in enumerate(drawn.shape)]
    longest = drawn.shape.index(max(drawn.shape))
    next_to = index_at[:longest] + [(index_at[longest] + 1) % drawn.shape[longest]] + index_at[longest + 1:]
    return drawn.at[tuple(index_at)].set(least).at[tuple(next_to)].set(high)


def levels(rng, extent, cuts, low, high):
    factor_of, own = 1.0, jax.random.fold_in(rng, 6)
    for axis_at, blocks in cuts:
        steps = jnp.exp(jax.random.uniform(jax.random.fold_in(own, axis_at), (blocks,), jnp.float32, low / len(cuts), high / len(cuts)))
        factor_of = factor_of * jnp.repeat(steps, extent[axis_at] // blocks).reshape([-1 if axis == axis_at else 1 for axis in range(len(extent))])
    return factor_of


def normal_values(stream_key, shape, deviation, most, cuts=(), kind=jnp.bfloat16):
    result = jax.random.normal(stream_key, shape, jnp.float32) * deviation
    if len(cuts) > 0:
        result = levels(stream_key, shape, cuts, -0.22, 0.18) * result
    return jnp.clip(result, min=-most, max=most).astype(kind)


def setup_inputs(seed: int = 0, part: int = 0) -> dict:
    key_of = jax.random.split(jax.random.key(seed), 8)
    own_keys = jax.random.split(jax.random.fold_in(key_of[7], part), 8)
    return {
        "basis_values": normal_values(own_keys[0], (DATES, PATHS, K), 1.0, 6.0, ((0, 2),)),
        "coefficients": normal_values(key_of[1], (TRADES, K), (K * TRADES // NSETS) ** -0.5, 0.0625, ((0, 8),)),
        "set_map": draw_set_map(jax.random.fold_in(key_of[7], 71), part),
        "trade_type": place_ends(jax.random.randint(key_of[3], (TRADES,), 0, NTYPE), jax.random.fold_in(key_of[3], 1), 0, NTYPE - 1).astype(jnp.int32),
        "type_gain": jnp.clip(jnp.exp(math.log(4.0) - 2.7725887 * jax.random.uniform(key_of[4], (DATES, NTYPE), jnp.float32) ** levels(key_of[4], (DATES, NTYPE), ((0, 2),), -0.2, 0.2)), 0.25, 4.0),
        "set_lags": place_ends(jax.random.randint(key_of[5], (NSETS,), 1, LAG_MAX + 1), jax.random.fold_in(key_of[5], 1), 1, LAG_MAX).astype(jnp.int32),
        "thresholds": jnp.clip(jax.random.uniform(key_of[6], (NSETS,), jnp.float32, -1.0, 1.0), -1.0, 1.0),
    }


def reference(basis_values, coefficients, set_map, trade_type, type_gain, set_lags, thresholds):
    trade_count = coefficients.shape[0]
    block_count = trade_count // TR_DEV
    date_count = basis_values.shape[0]
    path_count = basis_values.shape[1]
    set_ids = jnp.arange(NSETS, dtype=jnp.int32)
    basis_wide = basis_values.astype(jnp.float32)

    def block_inputs(block_index):
        first_row = (block_index * TR_DEV).astype(jnp.int32)
        coef_block = lax.dynamic_slice_in_dim(coefficients, first_row, TR_DEV, 0).astype(jnp.float32)
        set_block = lax.dynamic_slice_in_dim(set_map, first_row, TR_DEV, 0)
        type_block = lax.dynamic_slice_in_dim(trade_type, first_row, TR_DEV, 0)
        trade_gain = jnp.take(type_gain, type_block, axis=1)
        return (coef_block, set_block, trade_gain)

    def add_block(block_index, netted):
        coef_block, set_block, trade_gain = block_inputs(block_index)
        raw_value = jnp.einsum('dpk,tk->dpt', basis_wide, coef_block)
        prices = (raw_value * trade_gain[:, None, :]).astype(jnp.bfloat16)
        prices = lax.optimization_barrier(prices)
        membership = (set_block[:, None] == set_ids[None, :]).astype(jnp.float32)
        return netted + jnp.einsum('dpt,ts->pds', prices.astype(jnp.float32), membership)
    netted = lax.fori_loop(0, block_count, add_block, jnp.zeros((path_count, date_count, NSETS), jnp.float32))
    padded = jnp.pad(netted, ((0, 0), (LAG_MAX, 0), (0, 0)))
    padded_back_zeros = jnp.zeros((path_count, LAG_MAX, NSETS), jnp.float32)
    collateral = jnp.zeros_like(netted)
    for lag_value in range(1, LAG_MAX + 1):
        lag_mask = (set_lags == lag_value).astype(jnp.float32)
        collateral = collateral + lag_mask * padded[:, LAG_MAX - lag_value:LAG_MAX - lag_value + date_count, :]
    exposure = jnp.maximum(netted - collateral - thresholds, 0.0)
    direct_term = exposure * (2.0 / math.sqrt(date_count * path_count))
    padded_back = jnp.concatenate([direct_term, padded_back_zeros], axis=1)
    adjoint = direct_term
    for lag_value in range(1, LAG_MAX + 1):
        lag_mask = (set_lags == lag_value).astype(jnp.float32)
        adjoint = adjoint - lag_mask * padded_back[:, lag_value:lag_value + date_count, :]
    adjoint = lax.optimization_barrier(adjoint.astype(jnp.bfloat16))
    adjoint_wide = adjoint.astype(jnp.float32)

    def grad_block(block_index):
        coef_block, set_block, trade_gain = block_inputs(block_index)
        spread = jnp.take(adjoint_wide, set_block, axis=2)
        scaled = (jnp.transpose(spread, (1, 0, 2)) * trade_gain[:, None, :]).astype(jnp.bfloat16)
        scaled = lax.optimization_barrier(scaled)
        return jnp.einsum('dpt,dpk->tk', scaled.astype(jnp.float32), basis_wide)
    grads = lax.map(grad_block, jnp.arange(block_count, dtype=jnp.int32))
    return grads.reshape(trade_count, K)
```

```python
import functools
import math

import jax
import jax.numpy as jnp
from jax import lax
from jax.experimental import pallas as pl
from jax.experimental.pallas import tpu as pltpu
from jax.sharding import PartitionSpec as P

LAG_MAX = 2
GROUP = 8
PIECES = 4
CODE_MAX = 32767.0
NT = (((1,), (1,)), ((), ()))


def kernel(
    trade_peers, date_peers, loss_scale,
    gain_in, basis_in, coef_in, set_in, type_in, lag_in, limit_in,
    out_ref,
    gain_ref, basis_ref, coef_ref, set_ref, type_ref, lag_ref, limit_ref, load_sem,
    code_send, code_recv, unit_send, unit_recv, adj_send, adj_recv,
    member_ref, gain_cols, basis_rows, total_ref, half_recv,
    code_ss, code_rs, unit_ss, unit_rs, adj_ss, adj_rs, half_ss, half_rs,
):
    peers = trade_peers * date_peers
    my_trade = lax.axis_index("trades")
    my_date = lax.axis_index("dates")
    me = my_date * trade_peers + my_trade
    local_dates, path_count, basis_count = basis_ref.shape
    trade_count = coef_ref.shape[0]
    set_count = limit_ref.shape[1]
    type_count = gain_ref.shape[1]
    own_paths = path_count // peers
    groups = peers // GROUP
    wave_groups = trade_peers // GROUP
    group_paths = GROUP * own_paths
    group_rows = local_dates * group_paths
    chunk_rows = local_dates * own_paths
    half = basis_count // date_peers
    unroll = peers <= 16

    def device(index):
        return {"trades": index % trade_peers, "dates": index // trade_peers}

    def partner(step):
        trade = 0
        for bit in range((trade_peers - 1).bit_length()):
            weight = 2 ** bit
            mine = (my_trade // weight) % 2
            flip = (step // weight) % 2
            trade += weight * (mine + flip - 2 * mine * flip)
        return trade

    barrier = pltpu.get_barrier_semaphore()

    def greet(step, carry):
        pl.semaphore_signal(
            barrier, inc=1, device_id=device(lax.rem(me + step, peers)),
            device_id_type=pl.DeviceIdType.MESH,
        )
        return carry

    lax.fori_loop(1, peers, greet, 0, unroll=unroll)
    loads = [
        pltpu.make_async_copy(source, target, load_sem.at[i])
        for i, (source, target) in enumerate((
            (type_in, type_ref), (gain_in, gain_ref), (set_in, set_ref), (basis_in, basis_ref),
            (coef_in, coef_ref), (lag_in, lag_ref), (limit_in, limit_ref),
        ))
    ]
    for load in loads:
        load.start()
    for load in loads[:3]:
        load.wait()

    def code_copy(index, slot_here, slot_there):
        return pltpu.make_async_remote_copy(
            src_ref=code_send.at[slot_here], dst_ref=code_recv.at[slot_there],
            send_sem=code_ss.at[slot_here], recv_sem=code_rs.at[slot_there],
            device_id=device(index), device_id_type=pl.DeviceIdType.MESH,
        )

    def unit_copy(index, slot_here, slot_there):
        return pltpu.make_async_remote_copy(
            src_ref=unit_send.at[slot_here], dst_ref=unit_recv.at[slot_there],
            send_sem=unit_ss.at[slot_here], recv_sem=unit_rs.at[slot_there],
            device_id=device(index), device_id_type=pl.DeviceIdType.MESH,
        )

    def adj_copy(index, slot_there):
        return pltpu.make_async_remote_copy(
            src_ref=adj_send.at[index // trade_peers], dst_ref=adj_recv.at[slot_there],
            send_sem=adj_ss.at[index], recv_sem=adj_rs.at[slot_there],
            device_id=device(index), device_id_type=pl.DeviceIdType.MESH,
        )

    types = type_ref[...]
    table = gain_ref[...]
    gains = []
    for d in range(local_dates):
        row = jnp.zeros_like(types, dtype=jnp.float32)
        for y in range(type_count):
            row = jnp.where(types == y, table[d:d + 1, y:y + 1], row)
        gains.append(row)
    set_ids = lax.broadcasted_iota(jnp.int32, (set_count, trade_count), 0)
    member_wide = jnp.where(set_ids == set_ref[...], 1.0, 0.0)
    member = member_wide.astype(jnp.bfloat16)

    for load in loads[3:]:
        load.wait()

    def forward(group, carry):
        rows = basis_ref[:, pl.ds(pl.multiple_of(group * group_paths, group_paths), group_paths), :]
        raw = lax.dot_general(
            rows.reshape(group_rows, basis_count), coef_ref[...], NT,
            preferred_element_type=jnp.float32,
        )
        prices = jnp.concatenate(
            [raw[d * group_paths:(d + 1) * group_paths] * gains[d] for d in range(local_dates)], axis=0
        ).astype(jnp.bfloat16)
        part = lax.dot_general(prices, member, NT, preferred_element_type=jnp.float32)
        part = part.reshape(local_dates, GROUP, own_paths, set_count)
        for i in range(GROUP):
            chunk = part[:, i].reshape(chunk_rows, set_count)
            top = jnp.maximum(jnp.max(jnp.abs(chunk), axis=0, keepdims=True), 1e-30)
            codes = jnp.round(chunk * (CODE_MAX / top)).astype(jnp.int32)
            code_send[group * GROUP + i] = codes.astype(jnp.int16)
            unit_send[group * GROUP + i] = top * (1.0 / CODE_MAX)

        return carry

    for wave in range(date_peers):
        lax.fori_loop(
            wave * wave_groups, (wave + 1) * wave_groups, forward, 0, unroll=wave_groups <= 1
        )
        if wave == 0:
            pl.semaphore_wait(barrier, peers - 1)

        def deal(step, carry):
            index = wave * trade_peers + partner(trade_peers - step)
            code_copy(index, index, me).start()
            unit_copy(index, index, me).start()
            return carry

        lax.fori_loop(1, trade_peers, deal, 0, unroll=unroll)

        @pl.when(my_date != wave)
        def _():
            index = wave * trade_peers + my_trade
            code_copy(index, index, me).start()
            unit_copy(index, index, me).start()

    code_recv[me] = code_send[me]
    unit_recv[me] = unit_send[me]
    member_ref[...] = jnp.transpose(member_wide).astype(jnp.bfloat16)
    gain_rows = jnp.concatenate(
        [jnp.broadcast_to(gains[d], (group_paths, trade_count)) for d in range(local_dates)], axis=0
    )
    gain_cols[...] = jnp.transpose(gain_rows)
    if groups > 2:
        total_ref[...] = jnp.zeros_like(total_ref)

    def order_rows(group, carry):
        rows = basis_ref[:, pl.ds(pl.multiple_of(group * group_paths, group_paths), group_paths), :]
        basis_rows[pl.ds(pl.multiple_of(group * group_rows, group_rows), group_rows), :] = (
            rows.reshape(group_rows, basis_count)
        )
        return carry

    lax.fori_loop(0, groups, order_rows, 0, unroll=groups <= 2)

    def arrived(step, carry):
        source = lax.rem(me + step, peers)
        code_copy(source, source, source).wait_recv()
        unit_copy(source, source, source).wait_recv()
        return carry

    lax.fori_loop(1, peers, arrived, 0, unroll=unroll)

    def add(trade, totals):
        result = []
        for q in range(date_peers):
            source = q * trade_peers + trade
            values = code_recv[source].astype(jnp.int32).astype(jnp.float32)
            result.append(totals[q] + values * unit_recv[source])
        return tuple(result)

    totals = lax.fori_loop(
        0, trade_peers, add,
        tuple(jnp.zeros((chunk_rows, set_count), jnp.float32) for _ in range(date_peers)),
        unroll=unroll,
    )
    netted = [
        totals[q][d * own_paths:(d + 1) * own_paths]
        for q in range(date_peers) for d in range(local_dates)
    ]
    date_count = len(netted)
    lags = lag_ref[...]
    direct = []
    for d in range(date_count):
        value = netted[d]
        for lag in range(1, LAG_MAX + 1):
            if d >= lag:
                value = value - jnp.where(lags == lag, netted[d - lag], 0.0)
        direct.append(jnp.maximum(value - limit_ref[...], 0.0) * loss_scale)
    for q in range(date_peers):
        parts = []
        for d in range(q * local_dates, (q + 1) * local_dates):
            value = direct[d]
            for lag in range(1, LAG_MAX + 1):
                if d + lag < date_count:
                    value = value - jnp.where(lags == lag, direct[d + lag], 0.0)
            parts.append(value)
        adj_send[q] = jnp.concatenate(parts, axis=0).astype(jnp.bfloat16)

    def spread_out(step, carry):
        trade = partner(trade_peers - step)
        for q in range(date_peers):
            adj_copy(q * trade_peers + trade, me).start()
        return carry

    lax.fori_loop(1, trade_peers, spread_out, 0, unroll=unroll)
    for step in range(1, date_peers):
        adj_copy(lax.rem(my_date + step, date_peers) * trade_peers + my_trade, me).start()
    adj_recv[me] = adj_send[my_date]

    def block_of(group):
        for i in range(GROUP):
            index = group * GROUP + i

            @pl.when(index != me)
            def _():
                adj_copy(index, index).wait_recv()

        block = adj_recv[pl.ds(pl.multiple_of(group * GROUP, GROUP), GROUP)].astype(jnp.float32)
        block = block.reshape(GROUP, local_dates, own_paths, set_count)
        return jnp.concatenate(
            [block[i, d] for d in range(local_dates) for i in range(GROUP)], axis=0
        ).astype(jnp.bfloat16)

    piece_rows = trade_count // PIECES

    def gradient(group, block, first, count):
        rows = pl.ds(first, count)
        spread = lax.dot_general(member_ref[rows], block, NT, preferred_element_type=jnp.float32)
        scaled = (spread * gain_cols[rows]).astype(jnp.bfloat16)
        return jnp.dot(
            scaled, basis_rows[pl.ds(pl.multiple_of(group * group_rows, group_rows), group_rows), :],
            preferred_element_type=jnp.float32,
        )

    def keep(rows, part, fresh):
        for q in range(date_peers):
            columns = part[:, q * half:(q + 1) * half]
            total_ref[q, rows] = columns if fresh else total_ref[q, rows] + columns

    def backward(group, carry):
        block = block_of(group)
        for piece in range(PIECES):
            part = gradient(group, block, piece * piece_rows, piece_rows)
            keep(pl.ds(piece * piece_rows, piece_rows), part, groups <= 2)
        return carry

    lax.fori_loop(0, groups - 1, backward, 0, unroll=groups <= 2)

    def half_copy(step, piece):
        rows = pl.ds(piece * piece_rows, piece_rows)
        q = lax.rem(my_date + step, date_peers)
        return pltpu.make_async_remote_copy(
            src_ref=total_ref.at[q, rows], dst_ref=half_recv.at[step - 1, rows],
            send_sem=half_ss.at[step - 1, piece], recv_sem=half_rs.at[step - 1, piece],
            device_id={"dates": q}, device_id_type=pl.DeviceIdType.MESH,
        )

    last = block_of(groups - 1)
    for piece in range(PIECES):
        part = gradient(groups - 1, last, piece * piece_rows, piece_rows)
        keep(pl.ds(piece * piece_rows, piece_rows), part, groups == 1)
        for step in range(1, date_peers):
            half_copy(step, piece).start()

    def sent(step, carry):
        index = lax.rem(me + step, peers)
        code_copy(index, index, me).wait_send()
        unit_copy(index, index, me).wait_send()
        adj_copy(index, me).wait_send()
        return carry

    lax.fori_loop(1, peers, sent, 0, unroll=unroll)
    for piece in range(PIECES):
        rows = pl.ds(piece * piece_rows, piece_rows)
        result = total_ref[my_date, rows]
        for step in range(1, date_peers):
            half_copy(step, piece).wait_recv()
            result += half_recv[step - 1, rows]
        out_ref[rows] = result

    for step in range(1, date_peers):
        for piece in range(PIECES):
            half_copy(step, piece).wait_send()


def on_device(
    trade_peers, date_peers,
    basis_values, coefficients, set_map, trade_type, type_gain, set_lags, thresholds,
):
    local_dates, path_count, basis_count = basis_values.shape
    trade_count = coefficients.shape[0]
    set_count = thresholds.shape[0]
    peers = trade_peers * date_peers
    own_paths = path_count // peers
    chunk = local_dates * own_paths
    group_rows = chunk * GROUP
    half = basis_count // date_peers
    loss_scale = 2.0 / math.sqrt(local_dates * date_peers * path_count)
    vmem_limit = min(60, 20 + 4 * local_dates * path_count // 512) * 1024 * 1024
    vmem = pl.BlockSpec(memory_space=pltpu.VMEM)
    dma = pltpu.SemaphoreType.DMA
    return pl.pallas_call(
        functools.partial(kernel, trade_peers, date_peers, loss_scale),
        out_shape=jax.ShapeDtypeStruct((trade_count, half), jnp.float32),
        in_specs=[pl.BlockSpec(memory_space=pltpu.HBM)] * 7,
        out_specs=vmem,
        scratch_shapes=[
            pltpu.VMEM(type_gain.shape, jnp.float32),
            pltpu.VMEM(basis_values.shape, jnp.bfloat16),
            pltpu.VMEM(coefficients.shape, jnp.bfloat16),
            pltpu.VMEM((1, trade_count), jnp.int32),
            pltpu.VMEM((1, trade_count), jnp.int32),
            pltpu.VMEM((1, set_count), jnp.int32),
            pltpu.VMEM((1, set_count), jnp.float32),
            dma((7,)),
            pltpu.VMEM((peers, chunk, set_count), jnp.int16),
            pltpu.VMEM((peers, chunk, set_count), jnp.int16),
            pltpu.VMEM((peers, 1, set_count), jnp.float32),
            pltpu.VMEM((peers, 1, set_count), jnp.float32),
            pltpu.VMEM((date_peers, chunk, set_count), jnp.bfloat16),
            pltpu.VMEM((peers, chunk, set_count), jnp.bfloat16),
            pltpu.VMEM((trade_count, set_count), jnp.bfloat16),
            pltpu.VMEM((trade_count, group_rows), jnp.float32),
            pltpu.VMEM((path_count * local_dates, basis_count), jnp.bfloat16),
            pltpu.VMEM((date_peers, trade_count, half), jnp.float32),
            pltpu.VMEM((date_peers - 1, trade_count, half), jnp.float32),
            dma((peers,)), dma((peers,)), dma((peers,)), dma((peers,)),
            dma((peers,)), dma((peers,)), dma((date_peers - 1, PIECES)), dma((date_peers - 1, PIECES)),
        ],
        compiler_params=pltpu.CompilerParams(
            collective_id=0, has_side_effects=True, vmem_limit_bytes=vmem_limit
        ),
    )(
        *[
            pltpu.with_memory_space_constraint(x, pltpu.HBM)
            for x in (
                type_gain, basis_values, coefficients, set_map.reshape(1, -1),
                trade_type.reshape(1, -1), set_lags.reshape(1, -1), thresholds.reshape(1, -1),
            )
        ]
    )


def solution(mesh):
    return jax.shard_map(
        functools.partial(on_device, mesh.shape["trades"], mesh.shape["dates"]),
        mesh=mesh,
        in_specs=(
            P("dates", "groups", None),
            P("trades", None),
            P("trades"),
            P("trades"),
            P("dates", None),
            P(),
            P(),
        ),
        out_specs=P(("groups", "trades"), "dates"),
        check_vma=False,
    )
```

```python
import functools
import math

import jax
import jax.numpy as jnp
from jax import lax
from jax.experimental import pallas as pl
from jax.experimental.pallas import tpu as pltpu
from jax.sharding import PartitionSpec as P

LAG_MAX = 2
GROUP = 8
PIECES = 2
WAVES = 2
CODE_MAX = 32767.0
NT = (((1,), (1,)), ((), ()))


def kernel(
    trade_peers, loss_scale,
    gain_in, basis_in, coef_in, set_in, type_in, lag_in, limit_in,
    out_ref,
    gain_ref, basis_ref, coef_ref, set_ref, type_ref, lag_ref, limit_ref, load_sem,
    code_send, code_recv, unit_send, unit_recv, edge_send, edge_recv, adj_send, adj_recv,
    member_ref, gain_cols, basis_rows, total_ref, half_recv,
    code_ss, code_rs, unit_ss, unit_rs, edge_ss, edge_rs, adj_ss, adj_rs, half_ss, half_rs,
):
    my_trade = lax.axis_index("trades")
    my_date = lax.axis_index("dates")
    local_dates, path_count, basis_count = basis_ref.shape
    trade_count = coef_ref.shape[0]
    set_count = limit_ref.shape[1]
    type_count = gain_ref.shape[1]
    others = trade_peers - 1
    own_paths = path_count // (WAVES * trade_peers)
    wave_groups = trade_peers // GROUP
    groups = WAVES * wave_groups
    group_paths = GROUP * own_paths
    group_rows = local_dates * group_paths
    chunk_rows = local_dates * own_paths
    edge_rows = LAG_MAX * own_paths
    half = basis_count // 2
    unroll = trade_peers <= 8

    def partner(step):
        trade = 0
        for bit in range(others.bit_length()):
            weight = 2 ** bit
            mine = (my_trade // weight) % 2
            flip = (step // weight) % 2
            trade += weight * (mine + flip - 2 * mine * flip)
        return trade

    barrier = pltpu.get_barrier_semaphore()

    def greet(step, carry):
        pl.semaphore_signal(
            barrier, inc=1, device_id={"trades": partner(trade_peers - step)},
            device_id_type=pl.DeviceIdType.MESH,
        )
        return carry

    lax.fori_loop(1, trade_peers, greet, 0, unroll=unroll)
    pl.semaphore_signal(
        barrier, inc=1, device_id={"dates": 1 - my_date}, device_id_type=pl.DeviceIdType.MESH
    )
    loads = [
        pltpu.make_async_copy(source, target, load_sem.at[i])
        for i, (source, target) in enumerate((
            (type_in, type_ref), (gain_in, gain_ref), (set_in, set_ref), (basis_in, basis_ref),
            (coef_in, coef_ref), (lag_in, lag_ref), (limit_in, limit_ref),
        ))
    ]
    for load in loads:
        load.start()
    for load in loads[:3]:
        load.wait()

    def to_trade(source, target, send_sem, recv_sem, trade):
        return pltpu.make_async_remote_copy(
            src_ref=source, dst_ref=target, send_sem=send_sem, recv_sem=recv_sem,
            device_id={"trades": trade}, device_id_type=pl.DeviceIdType.MESH,
        )

    def to_core(source, target, send_sem, recv_sem):
        return pltpu.make_async_remote_copy(
            src_ref=source, dst_ref=target, send_sem=send_sem, recv_sem=recv_sem,
            device_id={"dates": 1 - my_date}, device_id_type=pl.DeviceIdType.MESH,
        )

    def code_copy(wave, here, there, trade):
        return to_trade(code_send.at[here], code_recv.at[there], code_ss.at[0], code_rs.at[wave], trade)

    def unit_copy(wave, here, there, trade):
        return to_trade(unit_send.at[here], unit_recv.at[there], unit_ss.at[0], unit_rs.at[wave], trade)

    def adj_copy(wave, here, there, trade):
        return to_trade(adj_send.at[here], adj_recv.at[there], adj_ss.at[0], adj_rs.at[wave], trade)

    def all_of(buffer, send_sem, recv_sem, count):
        slots = buffer.at[pl.ds(0, count)]
        return to_trade(slots, slots, send_sem, recv_sem, my_trade)

    types = type_ref[...]
    table = gain_ref[...]
    gains = []
    for d in range(local_dates):
        row = jnp.zeros_like(types, dtype=jnp.float32)
        for y in range(type_count):
            row = jnp.where(types == y, table[d:d + 1, y:y + 1], row)
        gains.append(row)
    set_ids = lax.broadcasted_iota(jnp.int32, (set_count, trade_count), 0)
    member_wide = jnp.where(set_ids == set_ref[...], 1.0, 0.0)
    member = member_wide.astype(jnp.bfloat16)

    for load in loads[3:]:
        load.wait()

    def forward(group, carry):
        rows = basis_ref[:, pl.ds(pl.multiple_of(group * group_paths, group_paths), group_paths), :]
        raw = lax.dot_general(
            rows.reshape(group_rows, basis_count), coef_ref[...], NT,
            preferred_element_type=jnp.float32,
        )
        prices = jnp.concatenate(
            [raw[d * group_paths:(d + 1) * group_paths] * gains[d] for d in range(local_dates)], axis=0
        ).astype(jnp.bfloat16)
        part = lax.dot_general(prices, member, NT, preferred_element_type=jnp.float32)
        part = part.reshape(local_dates, GROUP, own_paths, set_count)
        for i in range(GROUP):
            chunk = part[:, i].reshape(chunk_rows, set_count)
            top = jnp.maximum(jnp.max(jnp.abs(chunk), axis=0, keepdims=True), 1e-30)
            codes = jnp.round(chunk * (CODE_MAX / top)).astype(jnp.int32)
            code_send[group * GROUP + i] = codes.astype(jnp.int16)
            unit_send[group * GROUP + i] = top * (1.0 / CODE_MAX)

        return carry

    for wave in range(WAVES):
        lax.fori_loop(
            wave * wave_groups, (wave + 1) * wave_groups, forward, 0, unroll=wave_groups <= 1
        )
        if wave == 0:
            pl.semaphore_wait(barrier, trade_peers)

        def deal(step, carry):
            trade = partner(trade_peers - step)
            code_copy(wave, wave * trade_peers + trade, wave * trade_peers + my_trade, trade).start()
            unit_copy(wave, wave * trade_peers + trade, wave * trade_peers + my_trade, trade).start()
            return carry

        lax.fori_loop(1, trade_peers, deal, 0, unroll=unroll)
        mine = wave * trade_peers + my_trade
        code_recv[mine] = code_send[mine]
        unit_recv[mine] = unit_send[mine]

    member_ref[...] = jnp.transpose(member_wide).astype(jnp.bfloat16)
    gain_rows = jnp.concatenate(
        [jnp.broadcast_to(gains[d], (group_paths, trade_count)) for d in range(local_dates)], axis=0
    )
    gain_cols[...] = jnp.transpose(gain_rows)
    if groups > 2:
        total_ref[...] = jnp.zeros_like(total_ref)

    def order_rows(group, carry):
        rows = basis_ref[:, pl.ds(pl.multiple_of(group * group_paths, group_paths), group_paths), :]
        basis_rows[pl.ds(pl.multiple_of(group * group_rows, group_rows), group_rows), :] = (
            rows.reshape(group_rows, basis_count)
        )
        return carry

    lax.fori_loop(0, groups, order_rows, 0, unroll=groups <= 2)

    lags = lag_ref[...]
    first_core = my_date == 0

    def edge_copy(wave):
        return to_core(edge_send.at[wave], edge_recv.at[wave], edge_ss.at[wave], edge_rs.at[wave])

    for wave in range(WAVES):
        all_of(code_recv, code_ss.at[0], code_rs.at[wave], others).wait_recv()
        all_of(unit_recv, unit_ss.at[0], unit_rs.at[wave], others).wait_recv()

        def add(trade, total):
            source = wave * trade_peers + trade
            values = code_recv[source].astype(jnp.int32).astype(jnp.float32)
            return total + values * unit_recv[source]

        total = lax.fori_loop(
            0, trade_peers, add, jnp.zeros((chunk_rows, set_count), jnp.float32), unroll=unroll
        )
        edge_send[wave] = jnp.where(first_core, total[chunk_rows - edge_rows:], total[:edge_rows])
        edge_copy(wave).start()
        edge_copy(wave).wait_recv()
        edge = edge_recv[wave]
        before = jnp.where(first_core, 0.0, edge)
        netted = [before[i * own_paths:(i + 1) * own_paths] for i in range(LAG_MAX)]
        netted += [total[d * own_paths:(d + 1) * own_paths] for d in range(local_dates)]
        netted += [edge[i * own_paths:(i + 1) * own_paths] for i in range(LAG_MAX)]
        direct = []
        for d in range(LAG_MAX, len(netted)):
            value = netted[d]
            for lag in range(1, LAG_MAX + 1):
                value = value - jnp.where(lags == lag, netted[d - lag], 0.0)
            value = jnp.maximum(value - limit_ref[...], 0.0) * loss_scale
            if d >= LAG_MAX + local_dates:
                value = jnp.where(first_core, value, 0.0)
            direct.append(value)
        parts = []
        for d in range(local_dates):
            value = direct[d]
            for lag in range(1, LAG_MAX + 1):
                value = value - jnp.where(lags == lag, direct[d + lag], 0.0)
            parts.append(value)
        adj_send[wave] = jnp.concatenate(parts, axis=0).astype(jnp.bfloat16)

        def spread_out(step, carry):
            adj_copy(wave, wave, wave * trade_peers + my_trade, partner(trade_peers - step)).start()
            return carry

        lax.fori_loop(1, trade_peers, spread_out, 0, unroll=unroll)
        adj_recv[wave * trade_peers + my_trade] = adj_send[wave]

    def block_of(group):
        block = adj_recv[pl.ds(pl.multiple_of(group * GROUP, GROUP), GROUP)].astype(jnp.float32)
        block = block.reshape(GROUP, local_dates, own_paths, set_count)
        return jnp.concatenate(
            [block[i, d] for d in range(local_dates) for i in range(GROUP)], axis=0
        ).astype(jnp.bfloat16)

    piece_rows = trade_count // PIECES

    def gradient(group, block, first, count):
        rows = pl.ds(first, count)
        spread = lax.dot_general(member_ref[rows], block, NT, preferred_element_type=jnp.float32)
        scaled = (spread * gain_cols[rows]).astype(jnp.bfloat16)
        return jnp.dot(
            scaled, basis_rows[pl.ds(pl.multiple_of(group * group_rows, group_rows), group_rows), :],
            preferred_element_type=jnp.float32,
        )

    def keep(rows, part, fresh):
        for q in range(2):
            columns = part[:, q * half:(q + 1) * half]
            total_ref[q, rows] = columns if fresh else total_ref[q, rows] + columns

    def backward(group, carry):
        block = block_of(group)
        for piece in range(PIECES):
            part = gradient(group, block, piece * piece_rows, piece_rows)
            keep(pl.ds(piece * piece_rows, piece_rows), part, groups <= 2)
        return carry

    def half_copy(piece):
        rows = pl.ds(piece * piece_rows, piece_rows)
        return to_core(
            total_ref.at[1 - my_date, rows], half_recv.at[rows], half_ss.at[piece], half_rs.at[piece]
        )

    for wave in range(WAVES):
        all_of(adj_recv, adj_ss.at[0], adj_rs.at[wave], others).wait_recv()
        last = wave == WAVES - 1
        lax.fori_loop(
            wave * wave_groups, (wave + 1) * wave_groups - last, backward, 0, unroll=groups <= 2
        )

    last_block = block_of(groups - 1)
    for piece in range(PIECES):
        part = gradient(groups - 1, last_block, piece * piece_rows, piece_rows)
        keep(pl.ds(piece * piece_rows, piece_rows), part, False)
        half_copy(piece).start()

    all_of(code_send, code_ss.at[0], code_rs.at[0], WAVES * others).wait_send()
    all_of(unit_send, unit_ss.at[0], unit_rs.at[0], WAVES * others).wait_send()
    all_of(adj_recv, adj_ss.at[0], adj_rs.at[0], WAVES * others).wait_send()
    for wave in range(WAVES):
        edge_copy(wave).wait_send()
    for piece in range(PIECES):
        rows = pl.ds(piece * piece_rows, piece_rows)
        half_copy(piece).wait_recv()
        out_ref[rows] = total_ref[my_date, rows] + half_recv[rows]

    for piece in range(PIECES):
        half_copy(piece).wait_send()


def on_device(
    trade_peers, date_peers,
    basis_values, coefficients, set_map, trade_type, type_gain, set_lags, thresholds,
):
    local_dates, path_count, basis_count = basis_values.shape
    trade_count = coefficients.shape[0]
    set_count = thresholds.shape[0]
    slots = WAVES * trade_peers
    own_paths = path_count // slots
    chunk = local_dates * own_paths
    edge = LAG_MAX * own_paths
    group_rows = chunk * GROUP
    half = basis_count // 2
    loss_scale = 2.0 / math.sqrt(local_dates * date_peers * path_count)
    vmem_limit = min(60, 20 + 4 * local_dates * path_count // 512) * 1024 * 1024
    vmem = pl.BlockSpec(memory_space=pltpu.VMEM)
    dma = pltpu.SemaphoreType.DMA
    assert date_peers == 2 and local_dates >= LAG_MAX and trade_peers % GROUP == 0
    return pl.pallas_call(
        functools.partial(kernel, trade_peers, loss_scale),
        out_shape=jax.ShapeDtypeStruct((trade_count, half), jnp.float32),
        in_specs=[pl.BlockSpec(memory_space=pltpu.HBM)] * 7,
        out_specs=vmem,
        scratch_shapes=[
            pltpu.VMEM(type_gain.shape, jnp.float32),
            pltpu.VMEM(basis_values.shape, jnp.bfloat16),
            pltpu.VMEM(coefficients.shape, jnp.bfloat16),
            pltpu.VMEM((1, trade_count), jnp.int32),
            pltpu.VMEM((1, trade_count), jnp.int32),
            pltpu.VMEM((1, set_count), jnp.int32),
            pltpu.VMEM((1, set_count), jnp.float32),
            dma((7,)),
            pltpu.VMEM((slots, chunk, set_count), jnp.int16),
            pltpu.VMEM((slots, chunk, set_count), jnp.int16),
            pltpu.VMEM((slots, 1, set_count), jnp.float32),
            pltpu.VMEM((slots, 1, set_count), jnp.float32),
            pltpu.VMEM((WAVES, edge, set_count), jnp.float32),
            pltpu.VMEM((WAVES, edge, set_count), jnp.float32),
            pltpu.VMEM((WAVES, chunk, set_count), jnp.bfloat16),
            pltpu.VMEM((slots, chunk, set_count), jnp.bfloat16),
            pltpu.VMEM((trade_count, set_count), jnp.bfloat16),
            pltpu.VMEM((trade_count, group_rows), jnp.float32),
            pltpu.VMEM((path_count * local_dates, basis_count), jnp.bfloat16),
            pltpu.VMEM((2, trade_count, half), jnp.float32),
            pltpu.VMEM((trade_count, half), jnp.float32),
            dma((1,)), dma((WAVES,)), dma((1,)), dma((WAVES,)), dma((WAVES,)), dma((WAVES,)),
            dma((1,)), dma((WAVES,)), dma((PIECES,)), dma((PIECES,)),
        ],
        compiler_params=pltpu.CompilerParams(
            collective_id=0, has_side_effects=True, vmem_limit_bytes=vmem_limit
        ),
    )(
        *[
            pltpu.with_memory_space_constraint(x, pltpu.HBM)
            for x in (
                type_gain, basis_values, coefficients, set_map.reshape(1, -1),
                trade_type.reshape(1, -1), set_lags.reshape(1, -1), thresholds.reshape(1, -1),
            )
        ]
    )


def solution(mesh):
    return jax.shard_map(
        functools.partial(on_device, mesh.shape["trades"], mesh.shape["dates"]),
        mesh=mesh,
        in_specs=(
            P("dates", "groups", None),
            P("trades", None),
            P("trades"),
            P("trades"),
            P("dates", None),
            P(),
            P(),
        ),
        out_specs=P(("groups", "trades"), "dates"),
        check_vma=False,
    )
```

```python
import functools
import math

import jax
import jax.numpy as jnp
from jax import lax
from jax.experimental import pallas as pl
from jax.experimental.pallas import tpu as pltpu
from jax.sharding import PartitionSpec as P

LAG_MAX = 2
GROUP = 8
PIECES = 2
CODE_MAX = 32767.0
NT = (((1,), (1,)), ((), ()))


def kernel(
    trade_peers, loss_scale,
    gain_in, basis_in, coef_in, set_in, type_in, lag_in, limit_in,
    out_ref,
    gain_ref, basis_ref, coef_ref, set_ref, type_ref, lag_ref, limit_ref, load_sem,
    code_send, code_pass, code_recv, unit_send, unit_pass, unit_recv, gain_far, basis_far,
    adj_send, adj_recv, member_ref, gain_cols, basis_rows, total_ref, half_recv,
    code_ss, code_rs, unit_ss, unit_rs, pass_ss, pass_rs, adj_ss, adj_rs, half_ss, half_rs,
):
    my_trade = lax.axis_index("trades")
    my_core = lax.axis_index("dates")
    other_core = 1 - my_core
    local_dates, path_count, basis_count = basis_ref.shape
    trade_count = coef_ref.shape[0]
    set_count = limit_ref.shape[1]
    type_count = gain_ref.shape[1]
    others = trade_peers - 1
    core_paths = path_count // 2
    own_paths = core_paths // trade_peers
    core_groups = trade_peers // GROUP
    group_paths = GROUP * own_paths
    group_rows = local_dates * group_paths
    chunk_rows = local_dates * own_paths
    half = basis_count // 2
    unroll = trade_peers <= 8

    def partner(step):
        trade = 0
        for bit in range(others.bit_length()):
            weight = 2 ** bit
            mine = (my_trade // weight) % 2
            flip = (step // weight) % 2
            trade += weight * (mine + flip - 2 * mine * flip)
        return trade

    barrier = pltpu.get_barrier_semaphore()

    def greet(step, carry):
        pl.semaphore_signal(
            barrier, inc=1, device_id={"trades": partner(trade_peers - step)},
            device_id_type=pl.DeviceIdType.MESH,
        )
        return carry

    lax.fori_loop(1, trade_peers, greet, 0, unroll=unroll)
    pl.semaphore_signal(
        barrier, inc=1, device_id={"dates": other_core}, device_id_type=pl.DeviceIdType.MESH
    )
    loads = [
        pltpu.make_async_copy(source, target, load_sem.at[i])
        for i, (source, target) in enumerate((
            (type_in, type_ref), (gain_in, gain_ref), (set_in, set_ref), (basis_in, basis_ref),
            (coef_in, coef_ref), (lag_in, lag_ref), (limit_in, limit_ref),
        ))
    ]
    for load in loads:
        load.start()
    for load in loads[:3]:
        load.wait()

    def to_trade(source, target, send_sem, recv_sem, trade):
        return pltpu.make_async_remote_copy(
            src_ref=source, dst_ref=target, send_sem=send_sem, recv_sem=recv_sem,
            device_id={"trades": trade}, device_id_type=pl.DeviceIdType.MESH,
        )

    def to_core(source, target, send_sem, recv_sem):
        return pltpu.make_async_remote_copy(
            src_ref=source, dst_ref=target, send_sem=send_sem, recv_sem=recv_sem,
            device_id={"dates": other_core}, device_id_type=pl.DeviceIdType.MESH,
        )

    def all_of(buffer, send_sem, recv_sem, count):
        slots = buffer.at[pl.ds(0, count)]
        return to_trade(slots, slots, send_sem, recv_sem, my_trade)

    types = type_ref[...]

    def gains_of(table):
        gains = []
        for d in range(local_dates):
            row = jnp.zeros_like(types, dtype=jnp.float32)
            for y in range(type_count):
                row = jnp.where(types == y, table[d:d + 1, y:y + 1], row)
            gains.append(row)
        return gains

    gains = gains_of(gain_ref[...])
    set_ids = lax.broadcasted_iota(jnp.int32, (set_count, trade_count), 0)
    member_wide = jnp.where(set_ids == set_ref[...], 1.0, 0.0)
    member = member_wide.astype(jnp.bfloat16)

    for load in loads[3:]:
        load.wait()

    def forward(group, carry):
        rows = basis_ref[:, pl.ds(pl.multiple_of(group * group_paths, group_paths), group_paths), :]
        raw = lax.dot_general(
            rows.reshape(group_rows, basis_count), coef_ref[...], NT,
            preferred_element_type=jnp.float32,
        )
        prices = jnp.concatenate(
            [raw[d * group_paths:(d + 1) * group_paths] * gains[d] for d in range(local_dates)], axis=0
        ).astype(jnp.bfloat16)
        part = lax.dot_general(prices, member, NT, preferred_element_type=jnp.float32)
        part = part.reshape(local_dates, GROUP, own_paths, set_count)
        for i in range(GROUP):
            chunk = part[:, i].reshape(chunk_rows, set_count)
            top = jnp.maximum(jnp.max(jnp.abs(chunk), axis=0, keepdims=True), 1e-30)
            codes = jnp.round(chunk * (CODE_MAX / top)).astype(jnp.int32)
            code_send[group * GROUP + i] = codes.astype(jnp.int16)
            unit_send[group * GROUP + i] = top * (1.0 / CODE_MAX)

        return carry

    lax.fori_loop(0, 2 * core_groups, forward, 0, unroll=core_groups <= 1)
    pl.semaphore_wait(barrier, trade_peers)
    theirs = pl.ds(other_core * trade_peers, trade_peers)
    their_paths = pl.ds(pl.multiple_of(other_core * core_paths, core_paths), core_paths)
    code_over = to_core(code_send.at[theirs], code_pass, pass_ss.at[0], pass_rs.at[0])
    unit_over = to_core(unit_send.at[theirs], unit_pass, pass_ss.at[1], pass_rs.at[1])
    gain_over = to_core(gain_ref, gain_far, pass_ss.at[2], pass_rs.at[2])
    basis_over = to_core(basis_ref.at[:, their_paths], basis_far, pass_ss.at[3], pass_rs.at[3])
    code_over.start()
    unit_over.start()

    def deal(codes, units, first, dates):
        def one(step, carry):
            trade = partner(trade_peers - step)
            slot = dates * trade_peers + my_trade
            to_trade(
                codes.at[first + trade], code_recv.at[slot], code_ss.at[0], code_rs.at[0], trade
            ).start()
            to_trade(
                units.at[first + trade], unit_recv.at[slot], unit_ss.at[0], unit_rs.at[0], trade
            ).start()
            return carry

        lax.fori_loop(1, trade_peers, one, 0, unroll=unroll)

    mine = my_core * trade_peers
    deal(code_send, unit_send, mine, my_core)
    code_recv[mine + my_trade] = code_send[mine + my_trade]
    unit_recv[mine + my_trade] = unit_send[mine + my_trade]
    member_ref[...] = jnp.transpose(member_wide).astype(jnp.bfloat16)
    code_over.wait_recv()
    unit_over.wait_recv()
    deal(code_pass, unit_pass, 0, other_core)
    gain_over.start()
    basis_over.start()
    far = other_core * trade_peers
    code_recv[far + my_trade] = code_pass[my_trade]
    unit_recv[far + my_trade] = unit_pass[my_trade]

    def widen(gains, dates):
        wide = jnp.concatenate(
            [jnp.broadcast_to(gains[d], (group_paths, trade_count)) for d in range(local_dates)], axis=0
        )
        gain_cols[dates] = jnp.transpose(wide)

    def order_rows(source, first, dates):
        def one(group, carry):
            start = pl.multiple_of(first + group * group_paths, group_paths)
            basis_rows[dates * core_groups + group] = (
                source[:, pl.ds(start, group_paths), :].reshape(group_rows, basis_count)
            )
            return carry

        lax.fori_loop(0, core_groups, one, 0, unroll=core_groups <= 1)

    widen(gains, my_core)
    order_rows(basis_ref, my_core * core_paths, my_core)
    if core_groups > 1:
        total_ref[...] = jnp.zeros_like(total_ref)

    all_of(code_recv, code_ss.at[0], code_rs.at[0], 2 * others).wait_recv()
    all_of(unit_recv, unit_ss.at[0], unit_rs.at[0], 2 * others).wait_recv()

    def add(trade, totals):
        result = []
        for q in range(2):
            source = q * trade_peers + trade
            values = code_recv[source].astype(jnp.int32).astype(jnp.float32)
            result.append(totals[q] + values * unit_recv[source])
        return tuple(result)

    totals = lax.fori_loop(
        0, trade_peers, add,
        tuple(jnp.zeros((chunk_rows, set_count), jnp.float32) for _ in range(2)), unroll=unroll,
    )
    netted = [
        totals[q][d * own_paths:(d + 1) * own_paths] for q in range(2) for d in range(local_dates)
    ]
    date_count = len(netted)
    lags = lag_ref[...]
    direct = []
    for d in range(date_count):
        value = netted[d]
        for lag in range(1, LAG_MAX + 1):
            if d >= lag:
                value = value - jnp.where(lags == lag, netted[d - lag], 0.0)
        direct.append(jnp.maximum(value - limit_ref[...], 0.0) * loss_scale)
    for q in range(2):
        parts = []
        for d in range(q * local_dates, (q + 1) * local_dates):
            value = direct[d]
            for lag in range(1, LAG_MAX + 1):
                if d + lag < date_count:
                    value = value - jnp.where(lags == lag, direct[d + lag], 0.0)
            parts.append(value)
        adj_send[q] = jnp.concatenate(parts, axis=0).astype(jnp.bfloat16)

    for q in range(2):
        def spread_out(step, carry):
            trade = partner(trade_peers - step)
            to_trade(
                adj_send.at[q], adj_recv.at[q * trade_peers + my_trade], adj_ss.at[0], adj_rs.at[q], trade
            ).start()
            return carry

        lax.fori_loop(1, trade_peers, spread_out, 0, unroll=unroll)
        adj_recv[q * trade_peers + my_trade] = adj_send[q]

    gain_over.wait_recv()
    basis_over.wait_recv()
    widen(gains_of(gain_far[...]), other_core)
    order_rows(basis_far, 0, other_core)

    def block_of(group):
        block = adj_recv[pl.ds(pl.multiple_of(group * GROUP, GROUP), GROUP)].astype(jnp.float32)
        block = block.reshape(GROUP, local_dates, own_paths, set_count)
        return jnp.concatenate(
            [block[i, d] for d in range(local_dates) for i in range(GROUP)], axis=0
        ).astype(jnp.bfloat16)

    piece_rows = trade_count // PIECES

    def gradient(dates, group, block, piece):
        rows = pl.ds(piece * piece_rows, piece_rows)
        spread = lax.dot_general(member_ref[rows], block, NT, preferred_element_type=jnp.float32)
        scaled = (spread * gain_cols[dates, rows]).astype(jnp.bfloat16)
        return jnp.dot(scaled, basis_rows[group], preferred_element_type=jnp.float32)

    def keep(piece, part, fresh):
        rows = pl.ds(piece * piece_rows, piece_rows)
        for q in range(2):
            columns = part[:, q * half:(q + 1) * half]
            total_ref[q, rows] = columns if fresh else total_ref[q, rows] + columns

    def half_copy(piece):
        rows = pl.ds(piece * piece_rows, piece_rows)
        return to_core(
            total_ref.at[other_core, rows], half_recv.at[rows], half_ss.at[piece], half_rs.at[piece]
        )

    for dates in range(2):
        def backward(group, carry):
            block = block_of(group)
            for piece in range(PIECES):
                keep(piece, gradient(dates, group, block, piece), core_groups == 1)
            return carry

        all_of(adj_recv, adj_ss.at[0], adj_rs.at[dates], others).wait_recv()
        lax.fori_loop(
            dates * core_groups, (dates + 1) * core_groups - dates, backward, 0,
            unroll=core_groups <= 1,
        )

    final = 2 * core_groups - 1
    block = block_of(final)
    for piece in range(PIECES):
        keep(piece, gradient(1, final, block, piece), False)
        half_copy(piece).start()

    all_of(code_send, code_ss.at[0], code_rs.at[0], 2 * others).wait_send()
    all_of(unit_send, unit_ss.at[0], unit_rs.at[0], 2 * others).wait_send()
    all_of(adj_recv, adj_ss.at[0], adj_rs.at[0], 2 * others).wait_send()
    for copy in (code_over, unit_over, gain_over, basis_over):
        copy.wait_send()
    for piece in range(PIECES):
        rows = pl.ds(piece * piece_rows, piece_rows)
        half_copy(piece).wait_recv()
        out_ref[rows] = total_ref[my_core, rows] + half_recv[rows]

    for piece in range(PIECES):
        half_copy(piece).wait_send()


def on_device(
    trade_peers, date_peers,
    basis_values, coefficients, set_map, trade_type, type_gain, set_lags, thresholds,
):
    local_dates, path_count, basis_count = basis_values.shape
    trade_count = coefficients.shape[0]
    set_count = thresholds.shape[0]
    slots = 2 * trade_peers
    chunk = local_dates * path_count // slots
    group_rows = chunk * GROUP
    half = basis_count // 2
    loss_scale = 2.0 / math.sqrt(local_dates * date_peers * path_count)
    vmem_limit = min(60, 20 + 4 * local_dates * path_count // 512) * 1024 * 1024
    vmem = pl.BlockSpec(memory_space=pltpu.VMEM)
    dma = pltpu.SemaphoreType.DMA
    assert date_peers == 2 and trade_peers % GROUP == 0
    return pl.pallas_call(
        functools.partial(kernel, trade_peers, loss_scale),
        out_shape=jax.ShapeDtypeStruct((trade_count, half), jnp.float32),
        in_specs=[pl.BlockSpec(memory_space=pltpu.HBM)] * 7,
        out_specs=vmem,
        scratch_shapes=[
            pltpu.VMEM(type_gain.shape, jnp.float32),
            pltpu.VMEM(basis_values.shape, jnp.bfloat16),
            pltpu.VMEM(coefficients.shape, jnp.bfloat16),
            pltpu.VMEM((1, trade_count), jnp.int32),
            pltpu.VMEM((1, trade_count), jnp.int32),
            pltpu.VMEM((1, set_count), jnp.int32),
            pltpu.VMEM((1, set_count), jnp.float32),
            dma((7,)),
            pltpu.VMEM((slots, chunk, set_count), jnp.int16),
            pltpu.VMEM((trade_peers, chunk, set_count), jnp.int16),
            pltpu.VMEM((slots, chunk, set_count), jnp.int16),
            pltpu.VMEM((slots, 1, set_count), jnp.float32),
            pltpu.VMEM((trade_peers, 1, set_count), jnp.float32),
            pltpu.VMEM((slots, 1, set_count), jnp.float32),
            pltpu.VMEM(type_gain.shape, jnp.float32),
            pltpu.VMEM((local_dates, path_count // 2, basis_count), jnp.bfloat16),
            pltpu.VMEM((2, chunk, set_count), jnp.bfloat16),
            pltpu.VMEM((slots, chunk, set_count), jnp.bfloat16),
            pltpu.VMEM((trade_count, set_count), jnp.bfloat16),
            pltpu.VMEM((2, trade_count, group_rows), jnp.float32),
            pltpu.VMEM((slots // GROUP, group_rows, basis_count), jnp.bfloat16),
            pltpu.VMEM((2, trade_count, half), jnp.float32),
            pltpu.VMEM((trade_count, half), jnp.float32),
            dma((1,)), dma((1,)), dma((1,)), dma((1,)), dma((4,)), dma((4,)),
            dma((1,)), dma((2,)), dma((PIECES,)), dma((PIECES,)),
        ],
        compiler_params=pltpu.CompilerParams(
            collective_id=0, has_side_effects=True, vmem_limit_bytes=vmem_limit
        ),
    )(
        *[
            pltpu.with_memory_space_constraint(x, pltpu.HBM)
            for x in (
                type_gain, basis_values, coefficients, set_map.reshape(1, -1),
                trade_type.reshape(1, -1), set_lags.reshape(1, -1), thresholds.reshape(1, -1),
            )
        ]
    )


def solution(mesh):
    return jax.shard_map(
        functools.partial(on_device, mesh.shape["trades"], mesh.shape["dates"]),
        mesh=mesh,
        in_specs=(
            P("dates", "groups", None),
            P("trades", None),
            P("trades"),
            P("trades"),
            P("dates", None),
            P(),
            P(),
        ),
        out_specs=P(("groups", "trades"), "dates"),
        check_vma=False,
    )
```

```python
import functools
import math

import jax
import jax.numpy as jnp
from jax import lax
from jax.experimental import pallas as pl
from jax.experimental.pallas import tpu as pltpu
from jax.sharding import PartitionSpec as P

LAG_MAX = 2
GROUP = 8
PIECES = 2
CODE_MAX = 32767.0
NT = (((1,), (1,)), ((), ()))


def kernel(
    trade_peers, loss_scale,
    gain_in, basis_in, coef_in, set_in, type_in, lag_in, limit_in,
    out_ref,
    gain_ref, basis_ref, coef_ref, set_ref, type_ref, lag_ref, limit_ref, load_sem,
    code_send, code_pass, code_recv, unit_send, unit_pass, unit_recv, gain_far, basis_far,
    adj_send, adj_recv, member_ref, gain_cols, basis_rows, total_ref, half_recv,
    code_ss, code_rs, unit_ss, unit_rs, pass_ss, pass_rs, adj_ss, adj_rs, cross_rs, half_ss, half_rs,
):
    my_trade = lax.axis_index("trades")
    my_core = lax.axis_index("dates")
    other_core = 1 - my_core
    local_dates, path_count, basis_count = basis_ref.shape
    trade_count = coef_ref.shape[0]
    set_count = limit_ref.shape[1]
    type_count = gain_ref.shape[1]
    others = trade_peers - 1
    core_paths = path_count // 2
    own_paths = core_paths // trade_peers
    core_groups = trade_peers // GROUP
    group_paths = GROUP * own_paths
    group_rows = local_dates * group_paths
    chunk_rows = local_dates * own_paths
    half = basis_count // 2
    unroll = trade_peers <= 8

    def partner(step):
        trade = 0
        for bit in range(others.bit_length()):
            weight = 2 ** bit
            mine = (my_trade // weight) % 2
            flip = (step // weight) % 2
            trade += weight * (mine + flip - 2 * mine * flip)
        return trade

    barrier = pltpu.get_barrier_semaphore()

    def greet(step, carry):
        pl.semaphore_signal(
            barrier, inc=1, device_id={"trades": partner(trade_peers - step)},
            device_id_type=pl.DeviceIdType.MESH,
        )
        return carry

    lax.fori_loop(1, trade_peers, greet, 0, unroll=unroll)
    pl.semaphore_signal(
        barrier, inc=1, device_id={"dates": other_core}, device_id_type=pl.DeviceIdType.MESH
    )
    loads = [
        pltpu.make_async_copy(source, target, load_sem.at[i])
        for i, (source, target) in enumerate((
            (type_in, type_ref), (gain_in, gain_ref), (set_in, set_ref), (basis_in, basis_ref),
            (coef_in, coef_ref), (lag_in, lag_ref), (limit_in, limit_ref),
        ))
    ]
    for load in loads:
        load.start()
    for load in loads[:3]:
        load.wait()

    def to_trade(source, target, send_sem, recv_sem, trade):
        return pltpu.make_async_remote_copy(
            src_ref=source, dst_ref=target, send_sem=send_sem, recv_sem=recv_sem,
            device_id={"trades": trade}, device_id_type=pl.DeviceIdType.MESH,
        )

    def to_core(source, target, send_sem, recv_sem):
        return pltpu.make_async_remote_copy(
            src_ref=source, dst_ref=target, send_sem=send_sem, recv_sem=recv_sem,
            device_id={"dates": other_core}, device_id_type=pl.DeviceIdType.MESH,
        )

    def all_of(buffer, send_sem, recv_sem, count):
        slots = buffer.at[pl.ds(0, count)]
        return to_trade(slots, slots, send_sem, recv_sem, my_trade)

    types = type_ref[...]

    def gains_of(table):
        gains = []
        for d in range(local_dates):
            row = jnp.zeros_like(types, dtype=jnp.float32)
            for y in range(type_count):
                row = jnp.where(types == y, table[d:d + 1, y:y + 1], row)
            gains.append(row)
        return gains

    gains = gains_of(gain_ref[...])
    set_ids = lax.broadcasted_iota(jnp.int32, (set_count, trade_count), 0)
    member_wide = jnp.where(set_ids == set_ref[...], 1.0, 0.0)
    member = member_wide.astype(jnp.bfloat16)

    for load in loads[3:]:
        load.wait()

    def forward(group, carry):
        rows = basis_ref[:, pl.ds(pl.multiple_of(group * group_paths, group_paths), group_paths), :]
        raw = lax.dot_general(
            rows.reshape(group_rows, basis_count), coef_ref[...], NT,
            preferred_element_type=jnp.float32,
        )
        prices = jnp.concatenate(
            [raw[d * group_paths:(d + 1) * group_paths] * gains[d] for d in range(local_dates)], axis=0
        ).astype(jnp.bfloat16)
        part = lax.dot_general(prices, member, NT, preferred_element_type=jnp.float32)
        part = part.reshape(local_dates, GROUP, own_paths, set_count)
        for i in range(GROUP):
            chunk = part[:, i].reshape(chunk_rows, set_count)
            top = jnp.maximum(jnp.max(jnp.abs(chunk), axis=0, keepdims=True), 1e-30)
            codes = jnp.round(chunk * (CODE_MAX / top)).astype(jnp.int32)
            code_send[group * GROUP + i] = codes.astype(jnp.int16)
            unit_send[group * GROUP + i] = top * (1.0 / CODE_MAX)

        return carry

    lax.fori_loop(0, 2 * core_groups, forward, 0, unroll=core_groups <= 1)
    pl.semaphore_wait(barrier, trade_peers)
    theirs = pl.ds(other_core * trade_peers, trade_peers)
    their_paths = pl.ds(pl.multiple_of(other_core * core_paths, core_paths), core_paths)
    code_over = to_core(code_send.at[theirs], code_pass, pass_ss.at[0], pass_rs.at[0])
    unit_over = to_core(unit_send.at[theirs], unit_pass, pass_ss.at[1], pass_rs.at[1])
    gain_over = to_core(gain_ref, gain_far, pass_ss.at[2], pass_rs.at[2])
    basis_over = to_core(basis_ref.at[:, their_paths], basis_far, pass_ss.at[3], pass_rs.at[3])
    code_over.start()
    unit_over.start()

    def deal(codes, units, first, dates):
        def one(step, carry):
            trade = partner(trade_peers - step)
            slot = dates * trade_peers + my_trade
            to_trade(
                codes.at[first + trade], code_recv.at[slot], code_ss.at[0], code_rs.at[0], trade
            ).start()
            to_trade(
                units.at[first + trade], unit_recv.at[slot], unit_ss.at[0], unit_rs.at[0], trade
            ).start()
            return carry

        lax.fori_loop(1, trade_peers, one, 0, unroll=unroll)

    mine = my_core * trade_peers
    deal(code_send, unit_send, mine, my_core)
    code_recv[mine + my_trade] = code_send[mine + my_trade]
    unit_recv[mine + my_trade] = unit_send[mine + my_trade]
    member_ref[...] = jnp.transpose(member_wide).astype(jnp.bfloat16)
    code_over.wait_recv()
    unit_over.wait_recv()
    deal(code_pass, unit_pass, 0, other_core)
    gain_over.start()
    basis_over.start()
    far = other_core * trade_peers
    code_recv[far + my_trade] = code_pass[my_trade]
    unit_recv[far + my_trade] = unit_pass[my_trade]

    def widen(gains, dates):
        wide = jnp.concatenate(
            [jnp.broadcast_to(gains[d], (group_paths, trade_count)) for d in range(local_dates)], axis=0
        )
        gain_cols[dates] = jnp.transpose(wide)

    def order_rows(source, first, dates):
        def one(group, carry):
            start = pl.multiple_of(first + group * group_paths, group_paths)
            basis_rows[dates * core_groups + group] = (
                source[:, pl.ds(start, group_paths), :].reshape(group_rows, basis_count)
            )
            return carry

        lax.fori_loop(0, core_groups, one, 0, unroll=core_groups <= 1)

    widen(gains, my_core)
    order_rows(basis_ref, my_core * core_paths, my_core)
    if core_groups > 1:
        total_ref[...] = jnp.zeros_like(total_ref)

    all_of(code_recv, code_ss.at[0], code_rs.at[0], 2 * others).wait_recv()
    all_of(unit_recv, unit_ss.at[0], unit_rs.at[0], 2 * others).wait_recv()

    def add(trade, totals):
        result = []
        for q in range(2):
            source = q * trade_peers + trade
            values = code_recv[source].astype(jnp.int32).astype(jnp.float32)
            result.append(totals[q] + values * unit_recv[source])
        return tuple(result)

    totals = lax.fori_loop(
        0, trade_peers, add,
        tuple(jnp.zeros((chunk_rows, set_count), jnp.float32) for _ in range(2)), unroll=unroll,
    )
    netted = [
        totals[q][d * own_paths:(d + 1) * own_paths] for q in range(2) for d in range(local_dates)
    ]
    date_count = len(netted)
    lags = lag_ref[...]
    direct = []
    for d in range(date_count):
        value = netted[d]
        for lag in range(1, LAG_MAX + 1):
            if d >= lag:
                value = value - jnp.where(lags == lag, netted[d - lag], 0.0)
        direct.append(jnp.maximum(value - limit_ref[...], 0.0) * loss_scale)
    for q in range(2):
        parts = []
        for d in range(q * local_dates, (q + 1) * local_dates):
            value = direct[d]
            for lag in range(1, LAG_MAX + 1):
                if d + lag < date_count:
                    value = value - jnp.where(lags == lag, direct[d + lag], 0.0)
            parts.append(value)
        adj_send[q] = jnp.concatenate(parts, axis=0).astype(jnp.bfloat16)

    forwards = my_core == 1
    neighbour = partner(1)
    pairs = trade_peers // 2

    def adj_copy(q, trade, sems):
        return to_trade(
            adj_send.at[q], adj_recv.at[q * trade_peers + my_trade], adj_ss.at[0], sems.at[q], trade
        )

    for q in range(2):
        def spread_out(pair, carry):
            @pl.when(jnp.logical_not(forwards))
            def _():
                adj_copy(q, partner(trade_peers + 1 - 2 * pair), cross_rs).start()

            adj_copy(q, partner(trade_peers - 2 * pair), adj_rs).start()
            return carry

        lax.fori_loop(1, pairs, spread_out, 0, unroll=unroll)
        adj_copy(q, neighbour, cross_rs).start()
        adj_recv[q * trade_peers + my_trade] = adj_send[q]

    gain_over.wait_recv()
    basis_over.wait_recv()
    widen(gains_of(gain_far[...]), other_core)
    order_rows(basis_far, 0, other_core)

    def column_arrived(q):
        all_of(adj_recv, adj_ss.at[0], adj_rs.at[q], pairs - 1).wait_recv()

    @pl.when(forwards)
    def _():
        for q in range(2):
            column_arrived(q)

            def forward_block(pair, carry):
                block = adj_recv.at[q * trade_peers + partner(trade_peers - 2 * pair)]
                to_trade(block, block, adj_ss.at[0], cross_rs.at[q], neighbour).start()
                return carry

            lax.fori_loop(1, pairs, forward_block, 0, unroll=unroll)

    @pl.when(jnp.logical_not(forwards))
    def _():
        for q in range(2):
            column_arrived(q)

    def block_of(group):
        block = adj_recv[pl.ds(pl.multiple_of(group * GROUP, GROUP), GROUP)].astype(jnp.float32)
        block = block.reshape(GROUP, local_dates, own_paths, set_count)
        return jnp.concatenate(
            [block[i, d] for d in range(local_dates) for i in range(GROUP)], axis=0
        ).astype(jnp.bfloat16)

    piece_rows = trade_count // PIECES

    def gradient(dates, group, block, piece):
        rows = pl.ds(piece * piece_rows, piece_rows)
        spread = lax.dot_general(member_ref[rows], block, NT, preferred_element_type=jnp.float32)
        scaled = (spread * gain_cols[dates, rows]).astype(jnp.bfloat16)
        return jnp.dot(scaled, basis_rows[group], preferred_element_type=jnp.float32)

    def keep(piece, part, fresh):
        rows = pl.ds(piece * piece_rows, piece_rows)
        for q in range(2):
            columns = part[:, q * half:(q + 1) * half]
            total_ref[q, rows] = columns if fresh else total_ref[q, rows] + columns

    def half_copy(piece):
        rows = pl.ds(piece * piece_rows, piece_rows)
        return to_core(
            total_ref.at[other_core, rows], half_recv.at[rows], half_ss.at[piece], half_rs.at[piece]
        )

    for dates in range(2):
        def backward(group, carry):
            block = block_of(group)
            for piece in range(PIECES):
                keep(piece, gradient(dates, group, block, piece), core_groups == 1)
            return carry

        all_of(adj_recv, adj_ss.at[0], cross_rs.at[dates], pairs).wait_recv()
        lax.fori_loop(
            dates * core_groups, (dates + 1) * core_groups - dates, backward, 0,
            unroll=core_groups <= 1,
        )

    final = 2 * core_groups - 1
    block = block_of(final)
    for piece in range(PIECES):
        keep(piece, gradient(1, final, block, piece), False)
        half_copy(piece).start()

    all_of(code_send, code_ss.at[0], code_rs.at[0], 2 * others).wait_send()
    all_of(unit_send, unit_ss.at[0], unit_rs.at[0], 2 * others).wait_send()
    all_of(adj_recv, adj_ss.at[0], adj_rs.at[0], 2 * others).wait_send()
    for copy in (code_over, unit_over, gain_over, basis_over):
        copy.wait_send()
    for piece in range(PIECES):
        rows = pl.ds(piece * piece_rows, piece_rows)
        half_copy(piece).wait_recv()
        out_ref[rows] = total_ref[my_core, rows] + half_recv[rows]

    for piece in range(PIECES):
        half_copy(piece).wait_send()


def on_device(
    trade_peers, date_peers,
    basis_values, coefficients, set_map, trade_type, type_gain, set_lags, thresholds,
):
    local_dates, path_count, basis_count = basis_values.shape
    trade_count = coefficients.shape[0]
    set_count = thresholds.shape[0]
    slots = 2 * trade_peers
    chunk = local_dates * path_count // slots
    group_rows = chunk * GROUP
    half = basis_count // 2
    loss_scale = 2.0 / math.sqrt(local_dates * date_peers * path_count)
    vmem_limit = min(60, 20 + 4 * local_dates * path_count // 512) * 1024 * 1024
    vmem = pl.BlockSpec(memory_space=pltpu.VMEM)
    dma = pltpu.SemaphoreType.DMA
    assert date_peers == 2 and trade_peers % GROUP == 0
    return pl.pallas_call(
        functools.partial(kernel, trade_peers, loss_scale),
        out_shape=jax.ShapeDtypeStruct((trade_count, half), jnp.float32),
        in_specs=[pl.BlockSpec(memory_space=pltpu.HBM)] * 7,
        out_specs=vmem,
        scratch_shapes=[
            pltpu.VMEM(type_gain.shape, jnp.float32),
            pltpu.VMEM(basis_values.shape, jnp.bfloat16),
            pltpu.VMEM(coefficients.shape, jnp.bfloat16),
            pltpu.VMEM((1, trade_count), jnp.int32),
            pltpu.VMEM((1, trade_count), jnp.int32),
            pltpu.VMEM((1, set_count), jnp.int32),
            pltpu.VMEM((1, set_count), jnp.float32),
            dma((7,)),
            pltpu.VMEM((slots, chunk, set_count), jnp.int16),
            pltpu.VMEM((trade_peers, chunk, set_count), jnp.int16),
            pltpu.VMEM((slots, chunk, set_count), jnp.int16),
            pltpu.VMEM((slots, 1, set_count), jnp.float32),
            pltpu.VMEM((trade_peers, 1, set_count), jnp.float32),
            pltpu.VMEM((slots, 1, set_count), jnp.float32),
            pltpu.VMEM(type_gain.shape, jnp.float32),
            pltpu.VMEM((local_dates, path_count // 2, basis_count), jnp.bfloat16),
            pltpu.VMEM((2, chunk, set_count), jnp.bfloat16),
            pltpu.VMEM((slots, chunk, set_count), jnp.bfloat16),
            pltpu.VMEM((trade_count, set_count), jnp.bfloat16),
            pltpu.VMEM((2, trade_count, group_rows), jnp.float32),
            pltpu.VMEM((slots // GROUP, group_rows, basis_count), jnp.bfloat16),
            pltpu.VMEM((2, trade_count, half), jnp.float32),
            pltpu.VMEM((trade_count, half), jnp.float32),
            dma((1,)), dma((1,)), dma((1,)), dma((1,)), dma((4,)), dma((4,)),
            dma((1,)), dma((2,)), dma((2,)), dma((PIECES,)), dma((PIECES,)),
        ],
        compiler_params=pltpu.CompilerParams(
            collective_id=0, has_side_effects=True, vmem_limit_bytes=vmem_limit
        ),
    )(
        *[
            pltpu.with_memory_space_constraint(x, pltpu.HBM)
            for x in (
                type_gain, basis_values, coefficients, set_map.reshape(1, -1),
                trade_type.reshape(1, -1), set_lags.reshape(1, -1), thresholds.reshape(1, -1),
            )
        ]
    )


def solution(mesh):
    return jax.shard_map(
        functools.partial(on_device, mesh.shape["trades"], mesh.shape["dates"]),
        mesh=mesh,
        in_specs=(
            P("dates", "groups", None),
            P("trades", None),
            P("trades"),
            P("trades"),
            P("dates", None),
            P(),
            P(),
        ),
        out_specs=P(("groups", "trades"), "dates"),
        check_vma=False,
    )
```

```python
import functools
import math

import jax
import jax.numpy as jnp
from jax import lax
from jax.experimental import pallas as pl
from jax.experimental.pallas import tpu as pltpu
from jax.sharding import PartitionSpec as P

LAG_MAX = 2
GROUP = 8
SPAN = 4
PIECES = 4
CODE_MAX = 32767.0
NT = (((1,), (1,)), ((), ()))


def kernel(
    trade_peers, loss_scale,
    gain_in, basis_in, coef_in, set_in, type_in, lag_in, limit_in,
    out_ref,
    gain_ref, basis_ref, coef_ref, set_ref, type_ref, lag_ref, limit_ref, load_sem,
    code_send, code_pass, code_recv, unit_send, unit_pass, unit_recv, gain_far, basis_far,
    adj_send, adj_recv, member_ref, gain_cols, basis_rows, scaled_ref, total_ref, half_recv,
    code_ss, code_rs, unit_ss, unit_rs, pass_ss, pass_rs, adj_ss, adj_rs, half_ss, half_rs,
):
    my_trade = lax.axis_index("trades")
    my_core = lax.axis_index("dates")
    other_core = 1 - my_core
    local_dates, path_count, basis_count = basis_ref.shape
    trade_count = coef_ref.shape[0]
    set_count = limit_ref.shape[1]
    type_count = gain_ref.shape[1]
    others = trade_peers - 1
    core_paths = path_count // 2
    own_paths = core_paths // trade_peers
    core_groups = trade_peers // GROUP
    group_paths = GROUP * own_paths
    group_rows = local_dates * group_paths
    chunk_rows = local_dates * own_paths
    spans = trade_peers // SPAN
    span_paths = SPAN * own_paths
    half_rows = local_dates * span_paths
    half = basis_count // 2
    unroll = trade_peers <= 8

    def partner(step):
        trade = 0
        for bit in range(others.bit_length()):
            weight = 2 ** bit
            mine = (my_trade // weight) % 2
            flip = (step // weight) % 2
            trade += weight * (mine + flip - 2 * mine * flip)
        return trade

    barrier = pltpu.get_barrier_semaphore()

    def greet(step, carry):
        pl.semaphore_signal(
            barrier, inc=1, device_id={"trades": partner(trade_peers - step)},
            device_id_type=pl.DeviceIdType.MESH,
        )
        return carry

    lax.fori_loop(1, trade_peers, greet, 0, unroll=unroll)
    pl.semaphore_signal(
        barrier, inc=1, device_id={"dates": other_core}, device_id_type=pl.DeviceIdType.MESH
    )
    loads = [
        pltpu.make_async_copy(source, target, load_sem.at[i])
        for i, (source, target) in enumerate((
            (type_in, type_ref), (gain_in, gain_ref), (set_in, set_ref), (basis_in, basis_ref),
            (coef_in, coef_ref), (lag_in, lag_ref), (limit_in, limit_ref),
        ))
    ]
    for load in loads:
        load.start()
    for load in loads[:3]:
        load.wait()

    def to_trade(source, target, send_sem, recv_sem, trade):
        return pltpu.make_async_remote_copy(
            src_ref=source, dst_ref=target, send_sem=send_sem, recv_sem=recv_sem,
            device_id={"trades": trade}, device_id_type=pl.DeviceIdType.MESH,
        )

    def to_core(source, target, send_sem, recv_sem):
        return pltpu.make_async_remote_copy(
            src_ref=source, dst_ref=target, send_sem=send_sem, recv_sem=recv_sem,
            device_id={"dates": other_core}, device_id_type=pl.DeviceIdType.MESH,
        )

    def all_of(buffer, send_sem, recv_sem, count):
        slots = buffer.at[pl.ds(0, count)]
        return to_trade(slots, slots, send_sem, recv_sem, my_trade)

    types = type_ref[...]

    def gains_of(table):
        gains = []
        for d in range(local_dates):
            row = jnp.zeros_like(types, dtype=jnp.float32)
            for y in range(type_count):
                row = jnp.where(types == y, table[d:d + 1, y:y + 1], row)
            gains.append(row)
        return gains

    gains = gains_of(gain_ref[...])
    set_ids = lax.broadcasted_iota(jnp.int32, (set_count, trade_count), 0)
    member_wide = jnp.where(set_ids == set_ref[...], 1.0, 0.0)
    member = member_wide.astype(jnp.bfloat16)

    for load in loads[3:]:
        load.wait()

    def forward(group, carry):
        rows = basis_ref[:, pl.ds(pl.multiple_of(group * group_paths, group_paths), group_paths), :]
        raw = lax.dot_general(
            rows.reshape(group_rows, basis_count), coef_ref[...], NT,
            preferred_element_type=jnp.float32,
        )
        prices = jnp.concatenate(
            [raw[d * group_paths:(d + 1) * group_paths] * gains[d] for d in range(local_dates)], axis=0
        ).astype(jnp.bfloat16)
        part = lax.dot_general(prices, member, NT, preferred_element_type=jnp.float32)
        part = part.reshape(local_dates, GROUP, own_paths, set_count)
        for i in range(GROUP):
            chunk = part[:, i].reshape(chunk_rows, set_count)
            top = jnp.maximum(jnp.max(jnp.abs(chunk), axis=0, keepdims=True), 1e-30)
            codes = jnp.round(chunk * (CODE_MAX / top)).astype(jnp.int32)
            code_send[group * GROUP + i] = codes.astype(jnp.int16)
            unit_send[group * GROUP + i] = top * (1.0 / CODE_MAX)

        return carry

    lax.fori_loop(0, 2 * core_groups, forward, 0, unroll=core_groups <= 1)
    pl.semaphore_wait(barrier, trade_peers)
    theirs = pl.ds(other_core * trade_peers, trade_peers)
    their_paths = pl.ds(pl.multiple_of(other_core * core_paths, core_paths), core_paths)
    code_over = to_core(code_send.at[theirs], code_pass, pass_ss.at[0], pass_rs.at[0])
    unit_over = to_core(unit_send.at[theirs], unit_pass, pass_ss.at[1], pass_rs.at[1])
    gain_over = to_core(gain_ref, gain_far, pass_ss.at[2], pass_rs.at[2])
    basis_over = to_core(basis_ref.at[:, their_paths], basis_far, pass_ss.at[3], pass_rs.at[3])
    code_over.start()
    unit_over.start()

    def deal(codes, units, first, dates):
        def one(step, carry):
            trade = partner(trade_peers - step)
            slot = dates * trade_peers + my_trade
            to_trade(
                codes.at[first + trade], code_recv.at[slot], code_ss.at[0], code_rs.at[0], trade
            ).start()
            to_trade(
                units.at[first + trade], unit_recv.at[slot], unit_ss.at[0], unit_rs.at[0], trade
            ).start()
            return carry

        lax.fori_loop(1, trade_peers, one, 0, unroll=unroll)

    mine = my_core * trade_peers
    deal(code_send, unit_send, mine, my_core)
    code_recv[mine + my_trade] = code_send[mine + my_trade]
    unit_recv[mine + my_trade] = unit_send[mine + my_trade]
    member_ref[...] = jnp.transpose(member_wide).astype(jnp.bfloat16)
    code_over.wait_recv()
    unit_over.wait_recv()
    deal(code_pass, unit_pass, 0, other_core)
    gain_over.start()
    basis_over.start()
    far = other_core * trade_peers
    code_recv[far + my_trade] = code_pass[my_trade]
    unit_recv[far + my_trade] = unit_pass[my_trade]

    def widen(gains, dates):
        wide = jnp.concatenate(
            [jnp.broadcast_to(gains[d], (span_paths, trade_count)) for d in range(local_dates)], axis=0
        )
        columns = pl.ds(pl.multiple_of(dates * half_rows, half_rows), half_rows)
        gain_cols[:, columns] = jnp.transpose(wide)

    def order_rows(source, first, dates):
        def one(span, carry):
            start = pl.multiple_of(first + span * span_paths, span_paths)
            basis_rows[span, dates] = (
                source[:, pl.ds(start, span_paths), :].reshape(half_rows, basis_count)
            )
            return carry

        lax.fori_loop(0, spans, one, 0, unroll=spans <= 2)

    widen(gains, my_core)
    order_rows(basis_ref, my_core * core_paths, my_core)
    if spans > 2:
        total_ref[...] = jnp.zeros_like(total_ref)

    all_of(code_recv, code_ss.at[0], code_rs.at[0], 2 * others).wait_recv()
    all_of(unit_recv, unit_ss.at[0], unit_rs.at[0], 2 * others).wait_recv()

    def add(trade, totals):
        result = []
        for q in range(2):
            source = q * trade_peers + trade
            values = code_recv[source].astype(jnp.int32).astype(jnp.float32)
            result.append(totals[q] + values * unit_recv[source])
        return tuple(result)

    totals = lax.fori_loop(
        0, trade_peers, add,
        tuple(jnp.zeros((chunk_rows, set_count), jnp.float32) for _ in range(2)), unroll=unroll,
    )
    netted = [
        totals[q][d * own_paths:(d + 1) * own_paths] for q in range(2) for d in range(local_dates)
    ]
    date_count = len(netted)
    lags = lag_ref[...]
    direct = []
    for d in range(date_count):
        value = netted[d]
        for lag in range(1, LAG_MAX + 1):
            if d >= lag:
                value = value - jnp.where(lags == lag, netted[d - lag], 0.0)
        direct.append(jnp.maximum(value - limit_ref[...], 0.0) * loss_scale)
    parts = []
    for d in range(date_count):
        value = direct[d]
        for lag in range(1, LAG_MAX + 1):
            if d + lag < date_count:
                value = value - jnp.where(lags == lag, direct[d + lag], 0.0)
        parts.append(value)
    adj_send[...] = jnp.concatenate(parts, axis=0).astype(jnp.bfloat16)

    side = trade_peers // 2
    my_side = my_trade // side

    def adj_copy(trade):
        far = my_side + trade // side - 2 * my_side * (trade // side)
        return to_trade(adj_send, adj_recv.at[my_trade], adj_ss.at[0], adj_rs.at[far], trade)

    def spread_out(step, carry):
        adj_copy(step + (step + trade_peers - my_trade) // trade_peers).start()
        return carry

    lax.fori_loop(0, others, spread_out, 0, unroll=unroll)
    adj_recv[my_trade] = adj_send[...]

    gain_over.wait_recv()
    basis_over.wait_recv()
    widen(gains_of(gain_far[...]), other_core)
    order_rows(basis_far, 0, other_core)

    def block_of(span):
        block = adj_recv[pl.ds(span * SPAN, SPAN)].astype(jnp.float32)
        block = block.reshape(SPAN, date_count, own_paths, set_count)
        return jnp.concatenate(
            [block[i, d] for d in range(date_count) for i in range(SPAN)], axis=0
        ).astype(jnp.bfloat16)

    def scaled_of(span):
        spread = lax.dot_general(
            member_ref[...], block_of(span), NT, preferred_element_type=jnp.float32
        )
        return (spread * gain_cols[...]).astype(jnp.bfloat16)

    def gradient(span, scaled):
        rows = basis_rows[span].reshape(2 * half_rows, basis_count)
        return jnp.dot(scaled, rows, preferred_element_type=jnp.float32)

    def backward(step, carry):
        span = lax.rem(my_side * (spans // 2) + step, spans)
        part = gradient(span, scaled_of(span))
        for q in range(2):
            columns = part[:, q * half:(q + 1) * half]
            total_ref[q] = columns if spans <= 2 else total_ref[q] + columns
        return carry

    piece_rows = trade_count // PIECES

    def half_copy(piece):
        rows = pl.ds(piece * piece_rows, piece_rows)
        return to_core(
            total_ref.at[other_core, rows], half_recv.at[rows], half_ss.at[piece], half_rs.at[piece]
        )

    all_of(adj_recv, adj_ss.at[0], adj_rs.at[0], side - 1).wait_recv()
    lax.fori_loop(0, spans // 2, backward, 0, unroll=spans <= 2)
    all_of(adj_recv, adj_ss.at[0], adj_rs.at[1], side).wait_recv()
    lax.fori_loop(spans // 2, spans - 1, backward, 0, unroll=spans <= 2)
    final = lax.rem(my_side * (spans // 2) + spans - 1, spans)
    scaled_ref[...] = scaled_of(final)
    for piece in range(PIECES):
        rows = pl.ds(piece * piece_rows, piece_rows)
        part = gradient(final, scaled_ref[rows])
        for q in range(2):
            total_ref[q, rows] += part[:, q * half:(q + 1) * half]
        half_copy(piece).start()

    all_of(code_send, code_ss.at[0], code_rs.at[0], 2 * others).wait_send()
    all_of(unit_send, unit_ss.at[0], unit_rs.at[0], 2 * others).wait_send()
    all_of(adj_recv, adj_ss.at[0], adj_rs.at[0], others).wait_send()
    for copy in (code_over, unit_over, gain_over, basis_over):
        copy.wait_send()
    for piece in range(PIECES):
        rows = pl.ds(piece * piece_rows, piece_rows)
        half_copy(piece).wait_recv()
        out_ref[rows] = total_ref[my_core, rows] + half_recv[rows]

    for piece in range(PIECES):
        half_copy(piece).wait_send()


def on_device(
    trade_peers, date_peers,
    basis_values, coefficients, set_map, trade_type, type_gain, set_lags, thresholds,
):
    local_dates, path_count, basis_count = basis_values.shape
    trade_count = coefficients.shape[0]
    set_count = thresholds.shape[0]
    slots = 2 * trade_peers
    chunk = local_dates * path_count // slots
    half_rows = chunk * SPAN
    half = basis_count // 2
    loss_scale = 2.0 / math.sqrt(local_dates * date_peers * path_count)
    vmem_limit = min(60, 20 + 4 * local_dates * path_count // 512) * 1024 * 1024
    vmem = pl.BlockSpec(memory_space=pltpu.VMEM)
    dma = pltpu.SemaphoreType.DMA
    assert date_peers == 2 and trade_peers % GROUP == 0 and trade_peers % (2 * SPAN) == 0
    return pl.pallas_call(
        functools.partial(kernel, trade_peers, loss_scale),
        out_shape=jax.ShapeDtypeStruct((trade_count, half), jnp.float32),
        in_specs=[pl.BlockSpec(memory_space=pltpu.HBM)] * 7,
        out_specs=vmem,
        scratch_shapes=[
            pltpu.VMEM(type_gain.shape, jnp.float32),
            pltpu.VMEM(basis_values.shape, jnp.bfloat16),
            pltpu.VMEM(coefficients.shape, jnp.bfloat16),
            pltpu.VMEM((1, trade_count), jnp.int32),
            pltpu.VMEM((1, trade_count), jnp.int32),
            pltpu.VMEM((1, set_count), jnp.int32),
            pltpu.VMEM((1, set_count), jnp.float32),
            dma((7,)),
            pltpu.VMEM((slots, chunk, set_count), jnp.int16),
            pltpu.VMEM((trade_peers, chunk, set_count), jnp.int16),
            pltpu.VMEM((slots, chunk, set_count), jnp.int16),
            pltpu.VMEM((slots, 1, set_count), jnp.float32),
            pltpu.VMEM((trade_peers, 1, set_count), jnp.float32),
            pltpu.VMEM((slots, 1, set_count), jnp.float32),
            pltpu.VMEM(type_gain.shape, jnp.float32),
            pltpu.VMEM((local_dates, path_count // 2, basis_count), jnp.bfloat16),
            pltpu.VMEM((2 * chunk, set_count), jnp.bfloat16),
            pltpu.VMEM((trade_peers, 2 * chunk, set_count), jnp.bfloat16),
            pltpu.VMEM((trade_count, set_count), jnp.bfloat16),
            pltpu.VMEM((trade_count, 2 * half_rows), jnp.float32),
            pltpu.VMEM((trade_peers // SPAN, 2, half_rows, basis_count), jnp.bfloat16),
            pltpu.VMEM((trade_count, 2 * half_rows), jnp.bfloat16),
            pltpu.VMEM((2, trade_count, half), jnp.float32),
            pltpu.VMEM((trade_count, half), jnp.float32),
            dma((1,)), dma((1,)), dma((1,)), dma((1,)), dma((4,)), dma((4,)),
            dma((1,)), dma((2,)), dma((PIECES,)), dma((PIECES,)),
        ],
        compiler_params=pltpu.CompilerParams(
            collective_id=0, has_side_effects=True, vmem_limit_bytes=vmem_limit
        ),
    )(
        *[
            pltpu.with_memory_space_constraint(x, pltpu.HBM)
            for x in (
                type_gain, basis_values, coefficients, set_map.reshape(1, -1),
                trade_type.reshape(1, -1), set_lags.reshape(1, -1), thresholds.reshape(1, -1),
            )
        ]
    )


def solution(mesh):
    return jax.shard_map(
        functools.partial(on_device, mesh.shape["trades"], mesh.shape["dates"]),
        mesh=mesh,
        in_specs=(
            P("dates", "groups", None),
            P("trades", None),
            P("trades"),
            P("trades"),
            P("dates", None),
            P(),
            P(),
        ),
        out_specs=P(("groups", "trades"), "dates"),
        check_vma=False,
    )
```

```python
import functools
import math

import jax
import jax.numpy as jnp
from jax import lax
from jax.experimental import pallas as pl
from jax.experimental.pallas import tpu as pltpu
from jax.sharding import PartitionSpec as P

LAG_MAX = 2
GROUP = 8
SPAN = 4
PIECES = 2
CODE_MAX = 32767.0
NT = (((1,), (1,)), ((), ()))


def kernel(
    trade_peers, loss_scale,
    gain_in, basis_in, coef_in, set_in, type_in, lag_in, limit_in,
    out_ref,
    gain_ref, basis_ref, coef_ref, set_ref, type_ref, lag_ref, limit_ref, load_sem,
    code_send, code_pass, code_recv, unit_send, unit_pass, unit_recv, gain_far, basis_far,
    adj_send, adj_recv, member_ref, gain_cols, basis_rows, total_ref, half_recv,
    code_ss, code_rs, unit_ss, unit_rs, pass_ss, pass_rs, adj_ss, adj_rs, half_ss, half_rs,
):
    my_trade = lax.axis_index("trades")
    my_core = lax.axis_index("dates")
    other_core = 1 - my_core
    local_dates, path_count, basis_count = basis_ref.shape
    trade_count = coef_ref.shape[0]
    set_count = limit_ref.shape[1]
    type_count = gain_ref.shape[1]
    others = trade_peers - 1
    core_paths = path_count // 2
    own_paths = core_paths // trade_peers
    core_groups = trade_peers // GROUP
    group_paths = GROUP * own_paths
    group_rows = local_dates * group_paths
    chunk_rows = local_dates * own_paths
    spans = trade_peers // SPAN
    span_paths = SPAN * own_paths
    half_rows = local_dates * span_paths
    half = basis_count // 2
    unroll = trade_peers <= 8

    def partner(step):
        trade = 0
        for bit in range(others.bit_length()):
            weight = 2 ** bit
            mine = (my_trade // weight) % 2
            flip = (step // weight) % 2
            trade += weight * (mine + flip - 2 * mine * flip)
        return trade

    barrier = pltpu.get_barrier_semaphore()

    def greet(step, carry):
        pl.semaphore_signal(
            barrier, inc=1, device_id={"trades": partner(trade_peers - step)},
            device_id_type=pl.DeviceIdType.MESH,
        )
        return carry

    lax.fori_loop(1, trade_peers, greet, 0, unroll=unroll)
    pl.semaphore_signal(
        barrier, inc=1, device_id={"dates": other_core}, device_id_type=pl.DeviceIdType.MESH
    )
    loads = [
        pltpu.make_async_copy(source, target, load_sem.at[i])
        for i, (source, target) in enumerate((
            (type_in, type_ref), (gain_in, gain_ref), (set_in, set_ref), (basis_in, basis_ref),
            (coef_in, coef_ref), (lag_in, lag_ref), (limit_in, limit_ref),
        ))
    ]
    for load in loads:
        load.start()
    for load in loads[:3]:
        load.wait()

    def to_trade(source, target, send_sem, recv_sem, trade):
        return pltpu.make_async_remote_copy(
            src_ref=source, dst_ref=target, send_sem=send_sem, recv_sem=recv_sem,
            device_id={"trades": trade}, device_id_type=pl.DeviceIdType.MESH,
        )

    def to_core(source, target, send_sem, recv_sem):
        return pltpu.make_async_remote_copy(
            src_ref=source, dst_ref=target, send_sem=send_sem, recv_sem=recv_sem,
            device_id={"dates": other_core}, device_id_type=pl.DeviceIdType.MESH,
        )

    def all_of(buffer, send_sem, recv_sem, count):
        slots = buffer.at[pl.ds(0, count)]
        return to_trade(slots, slots, send_sem, recv_sem, my_trade)

    types = type_ref[...]

    def gains_of(table):
        gains = []
        for d in range(local_dates):
            row = jnp.zeros_like(types, dtype=jnp.float32)
            for y in range(type_count):
                row = jnp.where(types == y, table[d:d + 1, y:y + 1], row)
            gains.append(row)
        return gains

    gains = gains_of(gain_ref[...])
    set_ids = lax.broadcasted_iota(jnp.int32, (set_count, trade_count), 0)
    member_wide = jnp.where(set_ids == set_ref[...], 1.0, 0.0)
    member = member_wide.astype(jnp.bfloat16)

    for load in loads[3:]:
        load.wait()

    def forward(group, carry):
        rows = basis_ref[:, pl.ds(pl.multiple_of(group * group_paths, group_paths), group_paths), :]
        raw = lax.dot_general(
            rows.reshape(group_rows, basis_count), coef_ref[...], NT,
            preferred_element_type=jnp.float32,
        )
        prices = jnp.concatenate(
            [raw[d * group_paths:(d + 1) * group_paths] * gains[d] for d in range(local_dates)], axis=0
        ).astype(jnp.bfloat16)
        part = lax.dot_general(prices, member, NT, preferred_element_type=jnp.float32)
        part = part.reshape(local_dates, GROUP, own_paths, set_count)
        for i in range(GROUP):
            chunk = part[:, i].reshape(chunk_rows, set_count)
            top = jnp.maximum(jnp.max(jnp.abs(chunk), axis=0, keepdims=True), 1e-30)
            codes = jnp.round(chunk * (CODE_MAX / top)).astype(jnp.int32)
            code_send[group * GROUP + i] = codes.astype(jnp.int16)
            unit_send[group * GROUP + i] = top * (1.0 / CODE_MAX)

        return carry

    lax.fori_loop(0, 2 * core_groups, forward, 0, unroll=core_groups <= 1)
    pl.semaphore_wait(barrier, trade_peers)
    theirs = pl.ds(other_core * trade_peers, trade_peers)
    their_paths = pl.ds(pl.multiple_of(other_core * core_paths, core_paths), core_paths)
    code_over = to_core(code_send.at[theirs], code_pass, pass_ss.at[0], pass_rs.at[0])
    unit_over = to_core(unit_send.at[theirs], unit_pass, pass_ss.at[1], pass_rs.at[1])
    gain_over = to_core(gain_ref, gain_far, pass_ss.at[2], pass_rs.at[2])
    basis_over = to_core(basis_ref.at[:, their_paths], basis_far, pass_ss.at[3], pass_rs.at[3])
    code_over.start()
    unit_over.start()

    def deal(codes, units, first, dates):
        def one(step, carry):
            trade = partner(trade_peers - step)
            slot = dates * trade_peers + my_trade
            to_trade(
                codes.at[first + trade], code_recv.at[slot], code_ss.at[0], code_rs.at[0], trade
            ).start()
            to_trade(
                units.at[first + trade], unit_recv.at[slot], unit_ss.at[0], unit_rs.at[0], trade
            ).start()
            return carry

        lax.fori_loop(1, trade_peers, one, 0, unroll=unroll)

    mine = my_core * trade_peers
    deal(code_send, unit_send, mine, my_core)
    code_recv[mine + my_trade] = code_send[mine + my_trade]
    unit_recv[mine + my_trade] = unit_send[mine + my_trade]
    member_ref[...] = jnp.transpose(member_wide).astype(jnp.bfloat16)
    code_over.wait_recv()
    unit_over.wait_recv()
    deal(code_pass, unit_pass, 0, other_core)
    gain_over.start()
    basis_over.start()
    far = other_core * trade_peers
    code_recv[far + my_trade] = code_pass[my_trade]
    unit_recv[far + my_trade] = unit_pass[my_trade]

    def widen(gains, dates):
        wide = jnp.concatenate(
            [jnp.broadcast_to(gains[d], (span_paths, trade_count)) for d in range(local_dates)], axis=0
        )
        columns = pl.ds(pl.multiple_of(dates * half_rows, half_rows), half_rows)
        gain_cols[:, columns] = jnp.transpose(wide)

    def order_rows(source, first, dates):
        def one(span, carry):
            start = pl.multiple_of(first + span * span_paths, span_paths)
            basis_rows[span, dates] = (
                source[:, pl.ds(start, span_paths), :].reshape(half_rows, basis_count)
            )
            return carry

        lax.fori_loop(0, spans, one, 0, unroll=spans <= 2)

    widen(gains, my_core)
    order_rows(basis_ref, my_core * core_paths, my_core)
    if spans > 2:
        total_ref[...] = jnp.zeros_like(total_ref)

    all_of(code_recv, code_ss.at[0], code_rs.at[0], 2 * others).wait_recv()
    all_of(unit_recv, unit_ss.at[0], unit_rs.at[0], 2 * others).wait_recv()

    def add(trade, totals):
        result = []
        for q in range(2):
            source = q * trade_peers + trade
            values = code_recv[source].astype(jnp.int32).astype(jnp.float32)
            result.append(totals[q] + values * unit_recv[source])
        return tuple(result)

    totals = lax.fori_loop(
        0, trade_peers, add,
        tuple(jnp.zeros((chunk_rows, set_count), jnp.float32) for _ in range(2)), unroll=unroll,
    )
    netted = [
        totals[q][d * own_paths:(d + 1) * own_paths] for q in range(2) for d in range(local_dates)
    ]
    date_count = len(netted)
    lags = lag_ref[...]
    direct = []
    for d in range(date_count):
        value = netted[d]
        for lag in range(1, LAG_MAX + 1):
            if d >= lag:
                value = value - jnp.where(lags == lag, netted[d - lag], 0.0)
        direct.append(jnp.maximum(value - limit_ref[...], 0.0) * loss_scale)
    parts = []
    for d in range(date_count):
        value = direct[d]
        for lag in range(1, LAG_MAX + 1):
            if d + lag < date_count:
                value = value - jnp.where(lags == lag, direct[d + lag], 0.0)
        parts.append(value)
    adj_send[...] = jnp.concatenate(parts, axis=0).astype(jnp.bfloat16)

    side = trade_peers // 2
    my_side = my_trade // side

    def adj_copy(trade):
        far = my_side + trade // side - 2 * my_side * (trade // side)
        return to_trade(adj_send, adj_recv.at[my_trade], adj_ss.at[0], adj_rs.at[far], trade)

    def spread_out(step, carry):
        adj_copy(step + (step + trade_peers - my_trade) // trade_peers).start()
        return carry

    lax.fori_loop(0, others, spread_out, 0, unroll=unroll)
    adj_recv[my_trade] = adj_send[...]

    gain_over.wait_recv()
    basis_over.wait_recv()
    widen(gains_of(gain_far[...]), other_core)
    order_rows(basis_far, 0, other_core)

    def block_of(span):
        block = adj_recv[pl.ds(span * SPAN, SPAN)].astype(jnp.float32)
        block = block.reshape(SPAN, date_count, own_paths, set_count)
        return jnp.concatenate(
            [block[i, d] for d in range(date_count) for i in range(SPAN)], axis=0
        ).astype(jnp.bfloat16)

    def gradient(span, block, rows):
        spread = lax.dot_general(member_ref[rows], block, NT, preferred_element_type=jnp.float32)
        scaled = (spread * gain_cols[rows]).astype(jnp.bfloat16)
        basis = basis_rows[span].reshape(2 * half_rows, basis_count)
        return jnp.dot(scaled, basis, preferred_element_type=jnp.float32)

    def backward(step, carry):
        span = lax.rem(my_side * (spans // 2) + step, spans)
        part = gradient(span, block_of(span), pl.ds(0, trade_count))
        for q in range(2):
            columns = part[:, q * half:(q + 1) * half]
            total_ref[q] = columns if spans <= 2 else total_ref[q] + columns
        return carry

    piece_rows = trade_count // PIECES

    def half_copy(piece):
        rows = pl.ds(piece * piece_rows, piece_rows)
        return to_core(
            total_ref.at[other_core, rows], half_recv.at[rows], half_ss.at[piece], half_rs.at[piece]
        )

    all_of(adj_recv, adj_ss.at[0], adj_rs.at[0], side - 1).wait_recv()
    lax.fori_loop(0, spans // 2, backward, 0, unroll=spans <= 2)
    all_of(adj_recv, adj_ss.at[0], adj_rs.at[1], side).wait_recv()
    lax.fori_loop(spans // 2, spans - 1, backward, 0, unroll=spans <= 2)
    final = lax.rem(my_side * (spans // 2) + spans - 1, spans)
    block = block_of(final)
    for piece in range(PIECES):
        rows = pl.ds(piece * piece_rows, piece_rows)
        part = gradient(final, block, rows)
        for q in range(2):
            total_ref[q, rows] += part[:, q * half:(q + 1) * half]
        half_copy(piece).start()

    all_of(code_send, code_ss.at[0], code_rs.at[0], 2 * others).wait_send()
    all_of(unit_send, unit_ss.at[0], unit_rs.at[0], 2 * others).wait_send()
    all_of(adj_recv, adj_ss.at[0], adj_rs.at[0], others).wait_send()
    for copy in (code_over, unit_over, gain_over, basis_over):
        copy.wait_send()
    for piece in range(PIECES):
        rows = pl.ds(piece * piece_rows, piece_rows)
        half_copy(piece).wait_recv()
        out_ref[rows] = total_ref[my_core, rows] + half_recv[rows]

    for piece in range(PIECES):
        half_copy(piece).wait_send()


def on_device(
    trade_peers, date_peers,
    basis_values, coefficients, set_map, trade_type, type_gain, set_lags, thresholds,
):
    local_dates, path_count, basis_count = basis_values.shape
    trade_count = coefficients.shape[0]
    set_count = thresholds.shape[0]
    slots = 2 * trade_peers
    chunk = local_dates * path_count // slots
    half_rows = chunk * SPAN
    half = basis_count // 2
    loss_scale = 2.0 / math.sqrt(local_dates * date_peers * path_count)
    vmem_limit = min(60, 20 + 4 * local_dates * path_count // 512) * 1024 * 1024
    vmem = pl.BlockSpec(memory_space=pltpu.VMEM)
    dma = pltpu.SemaphoreType.DMA
    assert date_peers == 2 and trade_peers % GROUP == 0 and trade_peers % (2 * SPAN) == 0
    return pl.pallas_call(
        functools.partial(kernel, trade_peers, loss_scale),
        out_shape=jax.ShapeDtypeStruct((trade_count, half), jnp.float32),
        in_specs=[pl.BlockSpec(memory_space=pltpu.HBM)] * 7,
        out_specs=vmem,
        scratch_shapes=[
            pltpu.VMEM(type_gain.shape, jnp.float32),
            pltpu.VMEM(basis_values.shape, jnp.bfloat16),
            pltpu.VMEM(coefficients.shape, jnp.bfloat16),
            pltpu.VMEM((1, trade_count), jnp.int32),
            pltpu.VMEM((1, trade_count), jnp.int32),
            pltpu.VMEM((1, set_count), jnp.int32),
            pltpu.VMEM((1, set_count), jnp.float32),
            dma((7,)),
            pltpu.VMEM((slots, chunk, set_count), jnp.int16),
            pltpu.VMEM((trade_peers, chunk, set_count), jnp.int16),
            pltpu.VMEM((slots, chunk, set_count), jnp.int16),
            pltpu.VMEM((slots, 1, set_count), jnp.float32),
            pltpu.VMEM((trade_peers, 1, set_count), jnp.float32),
            pltpu.VMEM((slots, 1, set_count), jnp.float32),
            pltpu.VMEM(type_gain.shape, jnp.float32),
            pltpu.VMEM((local_dates, path_count // 2, basis_count), jnp.bfloat16),
            pltpu.VMEM((2 * chunk, set_count), jnp.bfloat16),
            pltpu.VMEM((trade_peers, 2 * chunk, set_count), jnp.bfloat16),
            pltpu.VMEM((trade_count, set_count), jnp.bfloat16),
            pltpu.VMEM((trade_count, 2 * half_rows), jnp.float32),
            pltpu.VMEM((trade_peers // SPAN, 2, half_rows, basis_count), jnp.bfloat16),
            pltpu.VMEM((2, trade_count, half), jnp.float32),
            pltpu.VMEM((trade_count, half), jnp.float32),
            dma((1,)), dma((1,)), dma((1,)), dma((1,)), dma((4,)), dma((4,)),
            dma((1,)), dma((2,)), dma((PIECES,)), dma((PIECES,)),
        ],
        compiler_params=pltpu.CompilerParams(
            collective_id=0, has_side_effects=True, vmem_limit_bytes=vmem_limit
        ),
    )(
        *[
            pltpu.with_memory_space_constraint(x, pltpu.HBM)
            for x in (
                type_gain, basis_values, coefficients, set_map.reshape(1, -1),
                trade_type.reshape(1, -1), set_lags.reshape(1, -1), thresholds.reshape(1, -1),
            )
        ]
    )


def solution(mesh):
    return jax.shard_map(
        functools.partial(on_device, mesh.shape["trades"], mesh.shape["dates"]),
        mesh=mesh,
        in_specs=(
            P("dates", "groups", None),
            P("trades", None),
            P("trades"),
            P("trades"),
            P("dates", None),
            P(),
            P(),
        ),
        out_specs=P(("groups", "trades"), "dates"),
        check_vma=False,
    )
```

```python
import functools
import math

import jax
import jax.numpy as jnp
from jax import lax
from jax.experimental import pallas as pl
from jax.experimental.pallas import tpu as pltpu
from jax.sharding import PartitionSpec as P

LAG_MAX = 2
GROUP = 8
SPAN = 4
CODE_MAX = 32767.0
NT = (((1,), (1,)), ((), ()))


def kernel(
    trade_peers, loss_scale,
    gain_in, basis_in, coef_in, set_in, type_in, lag_in, limit_in,
    out_ref,
    gain_ref, basis_ref, coef_ref, set_ref, type_ref, lag_ref, limit_ref, load_sem,
    code_send, code_pass, code_recv, unit_send, unit_both, unit_recv, gain_far, basis_far,
    adj_send, adj_recv, member_ref, gain_cols, basis_rows, total_ref, half_recv,
    code_ss, code_rs, unit_ss, unit_rs, pass_ss, pass_rs, adj_ss, adj_rs, half_ss, half_rs,
):
    my_trade = lax.axis_index("trades")
    my_core = lax.axis_index("dates")
    other_core = 1 - my_core
    local_dates, path_count, basis_count = basis_ref.shape
    trade_count = coef_ref.shape[0]
    set_count = limit_ref.shape[1]
    type_count = gain_ref.shape[1]
    others = trade_peers - 1
    core_paths = path_count // 2
    own_paths = core_paths // trade_peers
    core_groups = trade_peers // GROUP
    group_paths = GROUP * own_paths
    group_rows = local_dates * group_paths
    chunk_rows = local_dates * own_paths
    spans = trade_peers // SPAN
    span_paths = SPAN * own_paths
    half_rows = local_dates * span_paths
    half = basis_count // 2
    unroll = trade_peers <= 8

    def partner(step):
        trade = 0
        for bit in range(others.bit_length()):
            weight = 2 ** bit
            mine = (my_trade // weight) % 2
            flip = (step // weight) % 2
            trade += weight * (mine + flip - 2 * mine * flip)
        return trade

    barrier = pltpu.get_barrier_semaphore()

    def greet(step, carry):
        pl.semaphore_signal(
            barrier, inc=1, device_id={"trades": partner(trade_peers - step)},
            device_id_type=pl.DeviceIdType.MESH,
        )
        return carry

    lax.fori_loop(1, trade_peers, greet, 0, unroll=unroll)
    pl.semaphore_signal(
        barrier, inc=1, device_id={"dates": other_core}, device_id_type=pl.DeviceIdType.MESH
    )
    loads = [
        pltpu.make_async_copy(source, target, load_sem.at[i])
        for i, (source, target) in enumerate((
            (type_in, type_ref), (gain_in, gain_ref), (set_in, set_ref), (basis_in, basis_ref),
            (coef_in, coef_ref), (lag_in, lag_ref), (limit_in, limit_ref),
        ))
    ]
    for load in loads:
        load.start()
    for load in loads[:3]:
        load.wait()

    def to_trade(source, target, send_sem, recv_sem, trade):
        return pltpu.make_async_remote_copy(
            src_ref=source, dst_ref=target, send_sem=send_sem, recv_sem=recv_sem,
            device_id={"trades": trade}, device_id_type=pl.DeviceIdType.MESH,
        )

    def to_core(source, target, send_sem, recv_sem):
        return pltpu.make_async_remote_copy(
            src_ref=source, dst_ref=target, send_sem=send_sem, recv_sem=recv_sem,
            device_id={"dates": other_core}, device_id_type=pl.DeviceIdType.MESH,
        )

    def all_of(buffer, send_sem, recv_sem, count):
        slots = buffer.at[pl.ds(0, count)]
        return to_trade(slots, slots, send_sem, recv_sem, my_trade)

    types = type_ref[...]

    def gains_of(table):
        gains = []
        for d in range(local_dates):
            row = jnp.zeros_like(types, dtype=jnp.float32)
            for y in range(type_count):
                row = jnp.where(types == y, table[d:d + 1, y:y + 1], row)
            gains.append(row)
        return gains

    gains = gains_of(gain_ref[...])
    set_ids = lax.broadcasted_iota(jnp.int32, (set_count, trade_count), 0)
    member_wide = jnp.where(set_ids == set_ref[...], 1.0, 0.0)
    member = member_wide.astype(jnp.bfloat16)

    for load in loads[3:]:
        load.wait()

    def forward(group, carry):
        rows = basis_ref[:, pl.ds(pl.multiple_of(group * group_paths, group_paths), group_paths), :]
        raw = lax.dot_general(
            rows.reshape(group_rows, basis_count), coef_ref[...], NT,
            preferred_element_type=jnp.float32,
        )
        prices = jnp.concatenate(
            [raw[d * group_paths:(d + 1) * group_paths] * gains[d] for d in range(local_dates)], axis=0
        ).astype(jnp.bfloat16)
        part = lax.dot_general(prices, member, NT, preferred_element_type=jnp.float32)
        part = part.reshape(local_dates, GROUP, own_paths, set_count)
        for i in range(GROUP):
            chunk = part[:, i].reshape(chunk_rows, set_count)
            top = jnp.maximum(jnp.max(jnp.abs(chunk), axis=0, keepdims=True), 1e-30)
            codes = jnp.round(chunk * (CODE_MAX / top)).astype(jnp.int32)
            code_send[group * GROUP + i] = codes.astype(jnp.int16)
            unit_send[group * GROUP + i] = top * (1.0 / CODE_MAX)

        return carry

    lax.fori_loop(0, 2 * core_groups, forward, 0, unroll=core_groups <= 1)
    pl.semaphore_wait(barrier, trade_peers)
    theirs = pl.ds(other_core * trade_peers, trade_peers)
    code_over = to_core(code_send.at[theirs], code_pass, pass_ss.at[0], pass_rs.at[0])
    unit_over = to_core(
        unit_send.at[theirs], unit_both.at[my_core], pass_ss.at[1], pass_rs.at[1]
    )
    gain_over = to_core(gain_ref, gain_far, pass_ss.at[2], pass_rs.at[2])
    basis_over = to_core(basis_ref, basis_far, pass_ss.at[3], pass_rs.at[3])
    code_over.start()
    unit_over.start()

    def deal(codes, first, dates, units):
        def one(step, carry):
            trade = partner(trade_peers - step)
            slot = dates * trade_peers + my_trade
            to_trade(
                codes.at[first + trade], code_recv.at[slot], code_ss.at[0], code_rs.at[0], trade
            ).start()
            if units:
                to_trade(
                    unit_both.at[:, trade], unit_recv.at[my_trade], unit_ss.at[0], unit_rs.at[0], trade
                ).start()
            return carry

        lax.fori_loop(1, trade_peers, one, 0, unroll=unroll)

    leads = my_core == 1
    mine = my_core * trade_peers
    deal(code_send, mine, my_core, False)
    code_recv[mine + my_trade] = code_send[mine + my_trade]
    unit_both[my_core] = unit_send[pl.ds(mine, trade_peers)]
    member_ref[...] = jnp.transpose(member_wide).astype(jnp.bfloat16)
    code_over.wait_recv()
    unit_over.wait_recv()
    deal(code_pass, 0, other_core, True)
    code_recv[other_core * trade_peers + my_trade] = code_pass[my_trade]
    unit_recv[my_trade] = unit_both[:, my_trade]
    gain_over.start()
    basis_over.start()

    def widen(gains, dates):
        wide = jnp.concatenate(
            [jnp.broadcast_to(gains[d], (span_paths, trade_count)) for d in range(local_dates)], axis=0
        )
        columns = pl.ds(pl.multiple_of(dates * half_rows, half_rows), half_rows)
        gain_cols[:, columns] = jnp.transpose(wide)

    def order_rows(source, dates):
        def one(span, start):
            basis_rows[span, dates] = (
                source[:, pl.ds(pl.multiple_of(start, span_paths), span_paths), :]
                .reshape(half_rows, basis_count)
            )

        def each(span, carry):
            one(span, my_core * core_paths + span * span_paths)
            return carry

        lax.fori_loop(0, spans, each, 0, unroll=spans <= 2)
        one(spans, other_core * core_paths + final * span_paths)

    side = trade_peers // 2
    my_side = my_trade // side
    final = lax.rem(my_side * (spans // 2) + spans - 1, spans)
    widen(gains, my_core)
    order_rows(basis_ref, my_core)

    all_of(code_recv, code_ss.at[0], code_rs.at[0], 2 * others).wait_recv()
    all_of(unit_recv, unit_ss.at[0], unit_rs.at[0], others).wait_recv()

    def add(trade, totals):
        result = []
        for q in range(2):
            source = q * trade_peers + trade
            values = code_recv[source].astype(jnp.int32).astype(jnp.float32)
            result.append(totals[q] + values * unit_recv[trade, q])
        return tuple(result)

    totals = lax.fori_loop(
        0, trade_peers, add,
        tuple(jnp.zeros((chunk_rows, set_count), jnp.float32) for _ in range(2)), unroll=unroll,
    )
    netted = [
        totals[q][d * own_paths:(d + 1) * own_paths] for q in range(2) for d in range(local_dates)
    ]
    date_count = len(netted)
    lags = lag_ref[...]
    direct = []
    for d in range(date_count):
        value = netted[d]
        for lag in range(1, LAG_MAX + 1):
            if d >= lag:
                value = value - jnp.where(lags == lag, netted[d - lag], 0.0)
        direct.append(jnp.maximum(value - limit_ref[...], 0.0) * loss_scale)
    parts = []
    for d in range(date_count):
        value = direct[d]
        for lag in range(1, LAG_MAX + 1):
            if d + lag < date_count:
                value = value - jnp.where(lags == lag, direct[d + lag], 0.0)
        parts.append(value)
    adj_send[...] = jnp.concatenate(parts, axis=0).astype(jnp.bfloat16)

    def adj_copy(trade):
        far = my_side + trade // side - 2 * my_side * (trade // side)
        return to_trade(adj_send, adj_recv.at[my_trade], adj_ss.at[0], adj_rs.at[far], trade)

    def spread_out(step, carry):
        adj_copy(step + (step + trade_peers - my_trade) // trade_peers).start()
        return carry

    lax.fori_loop(0, others, spread_out, 0, unroll=unroll)
    adj_recv[my_trade] = adj_send[...]

    gain_over.wait_recv()
    basis_over.wait_recv()
    widen(gains_of(gain_far[...]), other_core)
    order_rows(basis_far, other_core)

    def scaled_of(first):
        block = adj_recv[pl.ds(first, SPAN)].astype(jnp.float32)
        block = block.reshape(SPAN, date_count, own_paths, set_count)
        block = jnp.concatenate(
            [block[i, d] for d in range(date_count) for i in range(SPAN)], axis=0
        ).astype(jnp.bfloat16)
        spread = lax.dot_general(member_ref[...], block, NT, preferred_element_type=jnp.float32)
        return (spread * gain_cols[...]).astype(jnp.bfloat16)

    def backward(step, carry, fresh=False):
        span = lax.rem(my_side * (spans // 2) + step, spans)
        rows = basis_rows[span].reshape(2 * half_rows, basis_count)
        part = jnp.dot(scaled_of(span * SPAN), rows, preferred_element_type=jnp.float32)
        for q in range(2):
            columns = part[:, q * half:(q + 1) * half]
            total_ref[q] = total_ref[q] + columns if fresh is False else columns
        return carry

    def far_arrived():
        all_of(adj_recv, adj_ss.at[0], adj_rs.at[1], side).wait_recv()

    half_over = to_core(total_ref.at[other_core], half_recv, half_ss.at[0], half_rs.at[0])
    blocks_over = to_core(
        adj_recv.at[pl.ds(final * SPAN, SPAN)], adj_recv.at[pl.ds(trade_peers, SPAN)],
        half_ss.at[1], half_rs.at[1],
    )
    all_of(adj_recv, adj_ss.at[0], adj_rs.at[0], side - 1).wait_recv()
    backward(0, 0, True)
    if spans > 2:
        lax.fori_loop(1, spans // 2, backward, 0)

    @pl.when(leads)
    def _():
        far_arrived()
        lax.fori_loop(spans // 2, spans, backward, 0, unroll=spans <= 2)
        half_over.start()
        blocks_over.wait_recv()

    @pl.when(jnp.logical_not(leads))
    def _():
        if spans > 2:
            far_arrived()
            lax.fori_loop(spans // 2, spans - 1, backward, 0)
        half_over.start()
        if spans <= 2:
            far_arrived()
        blocks_over.start()

    half_over.wait_recv()
    scaled = scaled_of((1 - my_core) * final * SPAN + my_core * trade_peers)
    my_columns = pl.ds(pl.multiple_of(my_core * half, half), half)
    rows = basis_rows[(1 - my_core) * final + my_core * spans, :, :, my_columns]
    part = jnp.dot(
        scaled, rows.reshape(2 * half_rows, half), preferred_element_type=jnp.float32
    )
    out_ref[...] = total_ref[my_core] + half_recv[...] + part

    all_of(code_send, code_ss.at[0], code_rs.at[0], 2 * others).wait_send()
    all_of(unit_recv, unit_ss.at[0], unit_rs.at[0], others).wait_send()
    all_of(adj_recv, adj_ss.at[0], adj_rs.at[0], others).wait_send()
    for copy in (code_over, unit_over, gain_over, basis_over, half_over):
        copy.wait_send()

    @pl.when(jnp.logical_not(leads))
    def _():
        blocks_over.wait_send()


def on_device(
    trade_peers, date_peers,
    basis_values, coefficients, set_map, trade_type, type_gain, set_lags, thresholds,
):
    local_dates, path_count, basis_count = basis_values.shape
    trade_count = coefficients.shape[0]
    set_count = thresholds.shape[0]
    slots = 2 * trade_peers
    chunk = local_dates * path_count // slots
    half_rows = chunk * SPAN
    half = basis_count // 2
    loss_scale = 2.0 / math.sqrt(local_dates * date_peers * path_count)
    vmem_limit = min(60, 20 + 4 * local_dates * path_count // 512) * 1024 * 1024
    vmem = pl.BlockSpec(memory_space=pltpu.VMEM)
    dma = pltpu.SemaphoreType.DMA
    assert date_peers == 2 and trade_peers % GROUP == 0 and trade_peers % (2 * SPAN) == 0
    return pl.pallas_call(
        functools.partial(kernel, trade_peers, loss_scale),
        out_shape=jax.ShapeDtypeStruct((trade_count, half), jnp.float32),
        in_specs=[pl.BlockSpec(memory_space=pltpu.HBM)] * 7,
        out_specs=vmem,
        scratch_shapes=[
            pltpu.VMEM(type_gain.shape, jnp.float32),
            pltpu.VMEM(basis_values.shape, jnp.bfloat16),
            pltpu.VMEM(coefficients.shape, jnp.bfloat16),
            pltpu.VMEM((1, trade_count), jnp.int32),
            pltpu.VMEM((1, trade_count), jnp.int32),
            pltpu.VMEM((1, set_count), jnp.int32),
            pltpu.VMEM((1, set_count), jnp.float32),
            dma((7,)),
            pltpu.VMEM((slots, chunk, set_count), jnp.int16),
            pltpu.VMEM((trade_peers, chunk, set_count), jnp.int16),
            pltpu.VMEM((slots, chunk, set_count), jnp.int16),
            pltpu.VMEM((slots, 1, set_count), jnp.float32),
            pltpu.VMEM((2, trade_peers, 1, set_count), jnp.float32),
            pltpu.VMEM((trade_peers, 2, 1, set_count), jnp.float32),
            pltpu.VMEM(type_gain.shape, jnp.float32),
            pltpu.VMEM(basis_values.shape, jnp.bfloat16),
            pltpu.VMEM((2 * chunk, set_count), jnp.bfloat16),
            pltpu.VMEM((trade_peers + SPAN, 2 * chunk, set_count), jnp.bfloat16),
            pltpu.VMEM((trade_count, set_count), jnp.bfloat16),
            pltpu.VMEM((trade_count, 2 * half_rows), jnp.float32),
            pltpu.VMEM((trade_peers // SPAN + 1, 2, half_rows, basis_count), jnp.bfloat16),
            pltpu.VMEM((2, trade_count, half), jnp.float32),
            pltpu.VMEM((trade_count, half), jnp.float32),
            dma((1,)), dma((1,)), dma((1,)), dma((1,)), dma((4,)), dma((4,)),
            dma((1,)), dma((2,)), dma((2,)), dma((2,)),
        ],
        compiler_params=pltpu.CompilerParams(
            collective_id=0, has_side_effects=True, vmem_limit_bytes=vmem_limit
        ),
    )(
        *[
            pltpu.with_memory_space_constraint(x, pltpu.HBM)
            for x in (
                type_gain, basis_values, coefficients, set_map.reshape(1, -1),
                trade_type.reshape(1, -1), set_lags.reshape(1, -1), thresholds.reshape(1, -1),
            )
        ]
    )


def solution(mesh):
    return jax.shard_map(
        functools.partial(on_device, mesh.shape["trades"], mesh.shape["dates"]),
        mesh=mesh,
        in_specs=(
            P("dates", "groups", None),
            P("trades", None),
            P("trades"),
            P("trades"),
            P("dates", None),
            P(),
            P(),
        ),
        out_specs=P(("groups", "trades"), "dates"),
        check_vma=False,
    )
```

```python
import functools
import math

import jax
import jax.numpy as jnp
from jax import lax
from jax.experimental import pallas as pl
from jax.experimental.pallas import tpu as pltpu
from jax.sharding import PartitionSpec as P

LAG_MAX = 2
GROUP = 8
SPAN = 4
CODE_MAX = 32767.0
NT = (((1,), (1,)), ((), ()))


def kernel(
    trade_peers, loss_scale,
    gain_in, basis_in, coef_in, set_in, type_in, lag_in, limit_in,
    out_ref,
    gain_ref, basis_ref, coef_ref, set_ref, type_ref, lag_ref, limit_ref, load_sem,
    code_send, code_pass, code_recv, unit_send, unit_both, unit_recv, gain_far, basis_far,
    adj_send, adj_recv, member_ref, gain_cols, basis_rows,
    code_ss, code_rs, unit_ss, unit_rs, pass_ss, pass_rs, adj_ss, adj_rs, half_ss, half_rs,
):
    my_trade = lax.axis_index("trades")
    my_core = lax.axis_index("dates")
    other_core = 1 - my_core
    local_dates, path_count, basis_count = basis_ref.shape
    trade_count = coef_ref.shape[0]
    set_count = limit_ref.shape[1]
    type_count = gain_ref.shape[1]
    others = trade_peers - 1
    core_paths = path_count // 2
    own_paths = core_paths // trade_peers
    core_groups = trade_peers // GROUP
    group_paths = GROUP * own_paths
    group_rows = local_dates * group_paths
    chunk_rows = local_dates * own_paths
    spans = trade_peers // SPAN
    span_paths = SPAN * own_paths
    half_rows = local_dates * span_paths
    half = basis_count // 2
    unroll = trade_peers <= 8

    def partner(step):
        trade = 0
        for bit in range(others.bit_length()):
            weight = 2 ** bit
            mine = (my_trade // weight) % 2
            flip = (step // weight) % 2
            trade += weight * (mine + flip - 2 * mine * flip)
        return trade

    barrier = pltpu.get_barrier_semaphore()

    def greet(step, carry):
        pl.semaphore_signal(
            barrier, inc=1, device_id={"trades": partner(trade_peers - step)},
            device_id_type=pl.DeviceIdType.MESH,
        )
        return carry

    lax.fori_loop(1, trade_peers, greet, 0, unroll=unroll)
    pl.semaphore_signal(
        barrier, inc=1, device_id={"dates": other_core}, device_id_type=pl.DeviceIdType.MESH
    )
    loads = [
        pltpu.make_async_copy(source, target, load_sem.at[i])
        for i, (source, target) in enumerate((
            (type_in, type_ref), (gain_in, gain_ref), (set_in, set_ref), (basis_in, basis_ref),
            (coef_in, coef_ref), (lag_in, lag_ref), (limit_in, limit_ref),
        ))
    ]
    for load in loads:
        load.start()
    for load in loads[:3]:
        load.wait()

    def to_trade(source, target, send_sem, recv_sem, trade):
        return pltpu.make_async_remote_copy(
            src_ref=source, dst_ref=target, send_sem=send_sem, recv_sem=recv_sem,
            device_id={"trades": trade}, device_id_type=pl.DeviceIdType.MESH,
        )

    def to_core(source, target, send_sem, recv_sem):
        return pltpu.make_async_remote_copy(
            src_ref=source, dst_ref=target, send_sem=send_sem, recv_sem=recv_sem,
            device_id={"dates": other_core}, device_id_type=pl.DeviceIdType.MESH,
        )

    def all_of(buffer, send_sem, recv_sem, count):
        slots = buffer.at[pl.ds(0, count)]
        return to_trade(slots, slots, send_sem, recv_sem, my_trade)

    types = type_ref[...]

    def gains_of(table):
        gains = []
        for d in range(local_dates):
            row = jnp.zeros_like(types, dtype=jnp.float32)
            for y in range(type_count):
                row = jnp.where(types == y, table[d:d + 1, y:y + 1], row)
            gains.append(row)
        return gains

    gains = gains_of(gain_ref[...])
    set_ids = lax.broadcasted_iota(jnp.int32, (set_count, trade_count), 0)
    member_wide = jnp.where(set_ids == set_ref[...], 1.0, 0.0)
    member = member_wide.astype(jnp.bfloat16)

    for load in loads[3:]:
        load.wait()

    def forward(group, carry):
        rows = basis_ref[:, pl.ds(pl.multiple_of(group * group_paths, group_paths), group_paths), :]
        raw = lax.dot_general(
            rows.reshape(group_rows, basis_count), coef_ref[...], NT,
            preferred_element_type=jnp.float32,
        )
        prices = jnp.concatenate(
            [raw[d * group_paths:(d + 1) * group_paths] * gains[d] for d in range(local_dates)], axis=0
        ).astype(jnp.bfloat16)
        part = lax.dot_general(prices, member, NT, preferred_element_type=jnp.float32)
        part = part.reshape(local_dates, GROUP, own_paths, set_count)
        for i in range(GROUP):
            chunk = part[:, i].reshape(chunk_rows, set_count)
            top = jnp.maximum(jnp.max(jnp.abs(chunk), axis=0, keepdims=True), 1e-30)
            codes = jnp.round(chunk * (CODE_MAX / top)).astype(jnp.int32)
            code_send[group * GROUP + i] = codes.astype(jnp.int16)
            unit_send[group * GROUP + i] = top * (1.0 / CODE_MAX)

        return carry

    lax.fori_loop(0, 2 * core_groups, forward, 0, unroll=core_groups <= 1)
    pl.semaphore_wait(barrier, trade_peers)
    theirs = pl.ds(other_core * trade_peers, trade_peers)
    code_over = to_core(code_send.at[theirs], code_pass, pass_ss.at[0], pass_rs.at[0])
    unit_over = to_core(
        unit_send.at[theirs], unit_both.at[my_core], pass_ss.at[1], pass_rs.at[1]
    )
    gain_over = to_core(gain_ref, gain_far, pass_ss.at[2], pass_rs.at[2])
    basis_over = to_core(basis_ref, basis_far, pass_ss.at[3], pass_rs.at[3])
    code_over.start()
    unit_over.start()

    def deal(codes, first, dates, units):
        def one(step, carry):
            trade = partner(trade_peers - step)
            slot = dates * trade_peers + my_trade
            to_trade(
                codes.at[first + trade], code_recv.at[slot], code_ss.at[0], code_rs.at[0], trade
            ).start()
            if units:
                to_trade(
                    unit_both.at[:, trade], unit_recv.at[my_trade], unit_ss.at[0], unit_rs.at[0], trade
                ).start()
            return carry

        lax.fori_loop(1, trade_peers, one, 0, unroll=unroll)

    leads = my_core == 1
    mine = my_core * trade_peers
    deal(code_send, mine, my_core, False)
    code_recv[mine + my_trade] = code_send[mine + my_trade]
    unit_both[my_core] = unit_send[pl.ds(mine, trade_peers)]
    member_ref[...] = jnp.transpose(member_wide).astype(jnp.bfloat16)
    code_over.wait_recv()
    unit_over.wait_recv()
    deal(code_pass, 0, other_core, True)
    code_recv[other_core * trade_peers + my_trade] = code_pass[my_trade]
    unit_recv[my_trade] = unit_both[:, my_trade]
    gain_over.start()
    basis_over.start()

    def widen(gains, dates):
        wide = jnp.concatenate(
            [jnp.broadcast_to(gains[d], (span_paths, trade_count)) for d in range(local_dates)], axis=0
        )
        columns = pl.ds(pl.multiple_of(dates * half_rows, half_rows), half_rows)
        gain_cols[:, columns] = jnp.transpose(wide)

    my_columns = pl.ds(pl.multiple_of(my_core * half, half), half)

    def order_rows(source, dates):
        def one(span, carry):
            start = my_core * core_paths + span * span_paths
            start -= (span // spans) * (2 * my_core * core_paths)
            rows = source[:, pl.ds(pl.multiple_of(start, span_paths), span_paths), my_columns]
            basis_rows[span, dates] = rows.reshape(half_rows, half)
            return carry

        lax.fori_loop(0, 2 * spans, one, 0, unroll=spans <= 2)

    side = trade_peers // 2
    my_side = my_trade // side
    widen(gains, my_core)
    order_rows(basis_ref, my_core)

    all_of(code_recv, code_ss.at[0], code_rs.at[0], 2 * others).wait_recv()
    all_of(unit_recv, unit_ss.at[0], unit_rs.at[0], others).wait_recv()

    def add(trade, totals):
        result = []
        for q in range(2):
            source = q * trade_peers + trade
            values = code_recv[source].astype(jnp.int32).astype(jnp.float32)
            result.append(totals[q] + values * unit_recv[trade, q])
        return tuple(result)

    totals = lax.fori_loop(
        0, trade_peers, add,
        tuple(jnp.zeros((chunk_rows, set_count), jnp.float32) for _ in range(2)), unroll=unroll,
    )
    netted = [
        totals[q][d * own_paths:(d + 1) * own_paths] for q in range(2) for d in range(local_dates)
    ]
    date_count = len(netted)
    lags = lag_ref[...]
    direct = []
    for d in range(date_count):
        value = netted[d]
        for lag in range(1, LAG_MAX + 1):
            if d >= lag:
                value = value - jnp.where(lags == lag, netted[d - lag], 0.0)
        direct.append(jnp.maximum(value - limit_ref[...], 0.0) * loss_scale)
    parts = []
    for d in range(date_count):
        value = direct[d]
        for lag in range(1, LAG_MAX + 1):
            if d + lag < date_count:
                value = value - jnp.where(lags == lag, direct[d + lag], 0.0)
        parts.append(value)
    adj_send[...] = jnp.concatenate(parts, axis=0).astype(jnp.bfloat16)

    def adj_copy(trade):
        far = my_side + trade // side - 2 * my_side * (trade // side)
        return to_trade(adj_send, adj_recv.at[my_trade], adj_ss.at[0], adj_rs.at[far], trade)

    def spread_out(step, carry):
        adj_copy(step + (step + trade_peers - my_trade) // trade_peers).start()
        return carry

    lax.fori_loop(0, others, spread_out, 0, unroll=unroll)
    adj_recv[my_trade] = adj_send[...]

    gain_over.wait_recv()
    basis_over.wait_recv()
    widen(gains_of(gain_far[...]), other_core)
    order_rows(basis_far, other_core)

    def scaled_of(first):
        block = adj_recv[pl.ds(first, SPAN)].astype(jnp.float32)
        block = block.reshape(SPAN, date_count, own_paths, set_count)
        block = jnp.concatenate(
            [block[i, d] for d in range(date_count) for i in range(SPAN)], axis=0
        ).astype(jnp.bfloat16)
        spread = lax.dot_general(member_ref[...], block, NT, preferred_element_type=jnp.float32)
        return (spread * gain_cols[...]).astype(jnp.bfloat16)

    def backward(system, far, fresh=False):
        which = my_side + far - 2 * my_side * far

        def one(step, carry):
            span = which * (spans // 2) + step
            rows = basis_rows[system * spans + span].reshape(2 * half_rows, half)
            scaled = scaled_of(system * trade_peers + span * SPAN)
            part = jnp.dot(scaled, rows, preferred_element_type=jnp.float32)
            out_ref[...] = part if fresh else out_ref[...] + part
            return carry

        if fresh and spans > 2:
            out_ref[...] = jnp.zeros_like(out_ref)
            fresh = False
        lax.fori_loop(0, spans // 2, one, 0, unroll=spans <= 2)

    def blocks_over(far):
        first = (my_side + far - 2 * my_side * far) * side
        return to_core(
            adj_recv.at[pl.ds(first, side)], adj_recv.at[pl.ds(trade_peers + first, side)],
            half_ss.at[far], half_rs.at[far],
        )

    def own_arrived(far):
        all_of(adj_recv, adj_ss.at[0], adj_rs.at[far], side - 1 + far).wait_recv()
        blocks_over(far).start()

    @pl.when(leads)
    def _():
        own_arrived(0)

    @pl.when(jnp.logical_not(leads))
    def _():
        blocks_over(0).wait_recv()

    backward(1 - my_core, 0, True)

    @pl.when(leads)
    def _():
        own_arrived(1)

    @pl.when(jnp.logical_not(leads))
    def _():
        own_arrived(0)

    backward(0, my_core)

    @pl.when(leads)
    def _():
        blocks_over(0).wait_recv()

    @pl.when(jnp.logical_not(leads))
    def _():
        blocks_over(1).wait_recv()

    backward(1, 1 - my_core)

    @pl.when(leads)
    def _():
        blocks_over(1).wait_recv()

    @pl.when(jnp.logical_not(leads))
    def _():
        own_arrived(1)

    backward(my_core, 1)

    all_of(code_send, code_ss.at[0], code_rs.at[0], 2 * others).wait_send()
    all_of(unit_recv, unit_ss.at[0], unit_rs.at[0], others).wait_send()
    all_of(adj_recv, adj_ss.at[0], adj_rs.at[0], others).wait_send()
    for copy in (code_over, unit_over, gain_over, basis_over, blocks_over(0), blocks_over(1)):
        copy.wait_send()


def on_device(
    trade_peers, date_peers,
    basis_values, coefficients, set_map, trade_type, type_gain, set_lags, thresholds,
):
    local_dates, path_count, basis_count = basis_values.shape
    trade_count = coefficients.shape[0]
    set_count = thresholds.shape[0]
    slots = 2 * trade_peers
    chunk = local_dates * path_count // slots
    half_rows = chunk * SPAN
    half = basis_count // 2
    loss_scale = 2.0 / math.sqrt(local_dates * date_peers * path_count)
    vmem_limit = min(60, 20 + 4 * local_dates * path_count // 512) * 1024 * 1024
    vmem = pl.BlockSpec(memory_space=pltpu.VMEM)
    dma = pltpu.SemaphoreType.DMA
    assert date_peers == 2 and trade_peers % GROUP == 0 and trade_peers % (2 * SPAN) == 0
    return pl.pallas_call(
        functools.partial(kernel, trade_peers, loss_scale),
        out_shape=jax.ShapeDtypeStruct((trade_count, half), jnp.float32),
        in_specs=[pl.BlockSpec(memory_space=pltpu.HBM)] * 7,
        out_specs=vmem,
        scratch_shapes=[
            pltpu.VMEM(type_gain.shape, jnp.float32),
            pltpu.VMEM(basis_values.shape, jnp.bfloat16),
            pltpu.VMEM(coefficients.shape, jnp.bfloat16),
            pltpu.VMEM((1, trade_count), jnp.int32),
            pltpu.VMEM((1, trade_count), jnp.int32),
            pltpu.VMEM((1, set_count), jnp.int32),
            pltpu.VMEM((1, set_count), jnp.float32),
            dma((7,)),
            pltpu.VMEM((slots, chunk, set_count), jnp.int16),
            pltpu.VMEM((trade_peers, chunk, set_count), jnp.int16),
            pltpu.VMEM((slots, chunk, set_count), jnp.int16),
            pltpu.VMEM((slots, 1, set_count), jnp.float32),
            pltpu.VMEM((2, trade_peers, 1, set_count), jnp.float32),
            pltpu.VMEM((trade_peers, 2, 1, set_count), jnp.float32),
            pltpu.VMEM(type_gain.shape, jnp.float32),
            pltpu.VMEM(basis_values.shape, jnp.bfloat16),
            pltpu.VMEM((2 * chunk, set_count), jnp.bfloat16),
            pltpu.VMEM((slots, 2 * chunk, set_count), jnp.bfloat16),
            pltpu.VMEM((trade_count, set_count), jnp.bfloat16),
            pltpu.VMEM((trade_count, 2 * half_rows), jnp.float32),
            pltpu.VMEM((slots // SPAN, 2, half_rows, half), jnp.bfloat16),
            dma((1,)), dma((1,)), dma((1,)), dma((1,)), dma((4,)), dma((4,)),
            dma((1,)), dma((2,)), dma((2,)), dma((2,)),
        ],
        compiler_params=pltpu.CompilerParams(
            collective_id=0, has_side_effects=True, vmem_limit_bytes=vmem_limit
        ),
    )(
        *[
            pltpu.with_memory_space_constraint(x, pltpu.HBM)
            for x in (
                type_gain, basis_values, coefficients, set_map.reshape(1, -1),
                trade_type.reshape(1, -1), set_lags.reshape(1, -1), thresholds.reshape(1, -1),
            )
        ]
    )


def solution(mesh):
    return jax.shard_map(
        functools.partial(on_device, mesh.shape["trades"], mesh.shape["dates"]),
        mesh=mesh,
        in_specs=(
            P("dates", "groups", None),
            P("trades", None),
            P("trades"),
            P("trades"),
            P("dates", None),
            P(),
            P(),
        ),
        out_specs=P(("groups", "trades"), "dates"),
        check_vma=False,
    )
```

```python
import functools
import math

import jax
import jax.numpy as jnp
from jax import lax
from jax.experimental import pallas as pl
from jax.experimental.pallas import tpu as pltpu
from jax.sharding import PartitionSpec as P

LAG_MAX = 2
GROUP = 8
SPAN = 4
CODE_MAX = 32767.0
NT = (((1,), (1,)), ((), ()))


def kernel(
    trade_peers, loss_scale,
    gain_in, basis_in, coef_in, set_in, type_in, lag_in, limit_in,
    out_ref,
    gain_ref, basis_ref, coef_ref, set_ref, type_ref, lag_ref, limit_ref, load_sem,
    code_send, code_pass, code_recv, unit_send, unit_both, unit_recv, gain_far, basis_far,
    adj_send, adj_recv, member_ref, gain_cols, basis_rows,
    code_ss, code_rs, unit_ss, unit_rs, pass_ss, pass_rs, adj_ss, adj_rs, half_ss, half_rs,
):
    my_trade = lax.axis_index("trades")
    my_core = lax.axis_index("dates")
    other_core = 1 - my_core
    local_dates, path_count, basis_count = basis_ref.shape
    trade_count = coef_ref.shape[0]
    set_count = limit_ref.shape[1]
    type_count = gain_ref.shape[1]
    others = trade_peers - 1
    core_paths = path_count // 2
    own_paths = core_paths // trade_peers
    core_groups = trade_peers // GROUP
    group_paths = GROUP * own_paths
    group_rows = local_dates * group_paths
    chunk_rows = local_dates * own_paths
    spans = trade_peers // SPAN
    span_paths = SPAN * own_paths
    half_rows = local_dates * span_paths
    half = basis_count // 2
    unroll = trade_peers <= 8

    def partner(step):
        trade = 0
        for bit in range(others.bit_length()):
            weight = 2 ** bit
            mine = (my_trade // weight) % 2
            flip = (step // weight) % 2
            trade += weight * (mine + flip - 2 * mine * flip)
        return trade

    barrier = pltpu.get_barrier_semaphore()

    def greet(step, carry):
        pl.semaphore_signal(
            barrier, inc=1, device_id={"trades": partner(trade_peers - step)},
            device_id_type=pl.DeviceIdType.MESH,
        )
        return carry

    lax.fori_loop(1, trade_peers, greet, 0, unroll=unroll)
    pl.semaphore_signal(
        barrier, inc=1, device_id={"dates": other_core}, device_id_type=pl.DeviceIdType.MESH
    )
    loads = [
        pltpu.make_async_copy(source, target, load_sem.at[i])
        for i, (source, target) in enumerate((
            (type_in, type_ref), (gain_in, gain_ref), (set_in, set_ref), (basis_in, basis_ref),
            (coef_in, coef_ref), (lag_in, lag_ref), (limit_in, limit_ref),
        ))
    ]
    for load in loads:
        load.start()
    for load in loads[:3]:
        load.wait()

    def to_trade(source, target, send_sem, recv_sem, trade):
        return pltpu.make_async_remote_copy(
            src_ref=source, dst_ref=target, send_sem=send_sem, recv_sem=recv_sem,
            device_id={"trades": trade}, device_id_type=pl.DeviceIdType.MESH,
        )

    def to_core(source, target, send_sem, recv_sem):
        return pltpu.make_async_remote_copy(
            src_ref=source, dst_ref=target, send_sem=send_sem, recv_sem=recv_sem,
            device_id={"dates": other_core}, device_id_type=pl.DeviceIdType.MESH,
        )

    def all_of(buffer, send_sem, recv_sem, count):
        slots = buffer.at[pl.ds(0, count)]
        return to_trade(slots, slots, send_sem, recv_sem, my_trade)

    types = type_ref[...]

    def gains_of(table):
        gains = []
        for d in range(local_dates):
            row = jnp.zeros_like(types, dtype=jnp.float32)
            for y in range(type_count):
                row = jnp.where(types == y, table[d:d + 1, y:y + 1], row)
            gains.append(row)
        return gains

    gains = gains_of(gain_ref[...])
    set_ids = lax.broadcasted_iota(jnp.int32, (set_count, trade_count), 0)
    member_wide = jnp.where(set_ids == set_ref[...], 1.0, 0.0)
    member = member_wide.astype(jnp.bfloat16)

    for load in loads[3:]:
        load.wait()

    def forward(group, carry):
        rows = basis_ref[:, pl.ds(pl.multiple_of(group * group_paths, group_paths), group_paths), :]
        raw = lax.dot_general(
            rows.reshape(group_rows, basis_count), coef_ref[...], NT,
            preferred_element_type=jnp.float32,
        )
        prices = jnp.concatenate(
            [raw[d * group_paths:(d + 1) * group_paths] * gains[d] for d in range(local_dates)], axis=0
        ).astype(jnp.bfloat16)
        part = lax.dot_general(prices, member, NT, preferred_element_type=jnp.float32)
        part = part.reshape(local_dates, GROUP, own_paths, set_count)
        for i in range(GROUP):
            chunk = part[:, i].reshape(chunk_rows, set_count)
            top = jnp.maximum(jnp.max(jnp.abs(chunk), axis=0, keepdims=True), 1e-30)
            codes = jnp.round(chunk * (CODE_MAX / top)).astype(jnp.int32)
            code_send[group * GROUP + i] = codes.astype(jnp.int16)
            unit_send[group * GROUP + i] = top * (1.0 / CODE_MAX)

        return carry

    lax.fori_loop(0, 2 * core_groups, forward, 0, unroll=core_groups <= 1)
    pl.semaphore_wait(barrier, trade_peers)
    theirs = pl.ds(other_core * trade_peers, trade_peers)
    code_over = to_core(code_send.at[theirs], code_pass, pass_ss.at[0], pass_rs.at[0])
    unit_over = to_core(
        unit_send.at[theirs], unit_both.at[my_core], pass_ss.at[1], pass_rs.at[1]
    )
    gain_over = to_core(gain_ref, gain_far, pass_ss.at[2], pass_rs.at[2])
    basis_over = to_core(basis_ref, basis_far, pass_ss.at[3], pass_rs.at[3])
    code_over.start()
    unit_over.start()

    def deal(codes, first, dates, units):
        def one(step, carry):
            trade = partner(trade_peers - step)
            slot = dates * trade_peers + my_trade
            to_trade(
                codes.at[first + trade], code_recv.at[slot], code_ss.at[0], code_rs.at[0], trade
            ).start()
            if units:
                to_trade(
                    unit_both.at[:, trade], unit_recv.at[my_trade], unit_ss.at[0], unit_rs.at[0], trade
                ).start()
            return carry

        lax.fori_loop(1, trade_peers, one, 0, unroll=unroll)

    leads = my_core == 1
    mine = my_core * trade_peers
    deal(code_send, mine, my_core, False)
    code_recv[mine + my_trade] = code_send[mine + my_trade]
    unit_both[my_core] = unit_send[pl.ds(mine, trade_peers)]
    member_ref[...] = jnp.transpose(member_wide).astype(jnp.bfloat16)
    code_over.wait_recv()
    unit_over.wait_recv()
    deal(code_pass, 0, other_core, True)
    code_recv[other_core * trade_peers + my_trade] = code_pass[my_trade]
    unit_recv[my_trade] = unit_both[:, my_trade]
    gain_over.start()
    basis_over.start()

    def widen(gains, dates):
        wide = jnp.concatenate(
            [jnp.broadcast_to(gains[d], (span_paths, trade_count)) for d in range(local_dates)], axis=0
        )
        columns = pl.ds(pl.multiple_of(dates * half_rows, half_rows), half_rows)
        gain_cols[:, columns] = jnp.transpose(wide)

    my_columns = pl.ds(pl.multiple_of(my_core * half, half), half)

    def order_rows(source, dates):
        def one(span, carry):
            start = my_core * core_paths + span * span_paths
            start -= (span // spans) * (2 * my_core * core_paths)
            rows = source[:, pl.ds(pl.multiple_of(start, span_paths), span_paths), my_columns]
            basis_rows[span, dates] = rows.reshape(half_rows, half)
            return carry

        lax.fori_loop(0, 2 * spans, one, 0, unroll=spans <= 2)

    side = trade_peers // 2
    my_side = my_trade // side
    widen(gains, my_core)
    order_rows(basis_ref, my_core)

    all_of(code_recv, code_ss.at[0], code_rs.at[0], 2 * others).wait_recv()
    all_of(unit_recv, unit_ss.at[0], unit_rs.at[0], others).wait_recv()

    def add(trade, totals):
        result = []
        for q in range(2):
            source = q * trade_peers + trade
            values = code_recv[source].astype(jnp.int32).astype(jnp.float32)
            result.append(totals[q] + values * unit_recv[trade, q])
        return tuple(result)

    totals = lax.fori_loop(
        0, trade_peers, add,
        tuple(jnp.zeros((chunk_rows, set_count), jnp.float32) for _ in range(2)), unroll=unroll,
    )
    netted = [
        totals[q][d * own_paths:(d + 1) * own_paths] for q in range(2) for d in range(local_dates)
    ]
    date_count = len(netted)
    lags = lag_ref[...]
    direct = []
    for d in range(date_count):
        value = netted[d]
        for lag in range(1, LAG_MAX + 1):
            if d >= lag:
                value = value - jnp.where(lags == lag, netted[d - lag], 0.0)
        direct.append(jnp.maximum(value - limit_ref[...], 0.0) * loss_scale)
    parts = []
    for d in range(date_count):
        value = direct[d]
        for lag in range(1, LAG_MAX + 1):
            if d + lag < date_count:
                value = value - jnp.where(lags == lag, direct[d + lag], 0.0)
        parts.append(value)
    adj_send[...] = jnp.concatenate(parts, axis=0).astype(jnp.bfloat16)

    def adj_copy(trade):
        far = my_side + trade // side - 2 * my_side * (trade // side)
        return to_trade(adj_send, adj_recv.at[my_trade], adj_ss.at[0], adj_rs.at[far], trade)

    quarter = trade_peers // 4
    is_last = my_trade // (3 * quarter)

    def spread_out(step, carry):
        part = step // quarter
        trade = step + is_last * quarter * ((part + 3) // 4 - 3 * (part // 3))

        @pl.when(trade != my_trade)
        def _():
            adj_copy(trade).start()

        return carry

    lax.fori_loop(0, trade_peers, spread_out, 0, unroll=unroll)
    adj_recv[my_trade] = adj_send[...]

    gain_over.wait_recv()
    basis_over.wait_recv()
    widen(gains_of(gain_far[...]), other_core)
    order_rows(basis_far, other_core)

    def scaled_of(first):
        block = adj_recv[pl.ds(first, SPAN)].astype(jnp.float32)
        block = block.reshape(SPAN, date_count, own_paths, set_count)
        block = jnp.concatenate(
            [block[i, d] for d in range(date_count) for i in range(SPAN)], axis=0
        ).astype(jnp.bfloat16)
        spread = lax.dot_general(member_ref[...], block, NT, preferred_element_type=jnp.float32)
        return (spread * gain_cols[...]).astype(jnp.bfloat16)

    def backward(system, far, fresh=False):
        which = my_side + far - 2 * my_side * far

        def one(step, carry):
            span = which * (spans // 2) + step
            rows = basis_rows[system * spans + span].reshape(2 * half_rows, half)
            scaled = scaled_of(system * trade_peers + span * SPAN)
            part = jnp.dot(scaled, rows, preferred_element_type=jnp.float32)
            out_ref[...] = part if fresh else out_ref[...] + part
            return carry

        if fresh and spans > 2:
            out_ref[...] = jnp.zeros_like(out_ref)
            fresh = False
        lax.fori_loop(0, spans // 2, one, 0, unroll=spans <= 2)

    def blocks_over(far):
        first = (my_side + far - 2 * my_side * far) * side
        return to_core(
            adj_recv.at[pl.ds(first, side)], adj_recv.at[pl.ds(trade_peers + first, side)],
            half_ss.at[far], half_rs.at[far],
        )

    def own_arrived(far):
        all_of(adj_recv, adj_ss.at[0], adj_rs.at[far], side - 1 + far).wait_recv()
        blocks_over(far).start()

    @pl.when(leads)
    def _():
        own_arrived(0)

    @pl.when(jnp.logical_not(leads))
    def _():
        blocks_over(0).wait_recv()

    backward(1 - my_core, 0, True)

    @pl.when(leads)
    def _():
        own_arrived(1)

    @pl.when(jnp.logical_not(leads))
    def _():
        own_arrived(0)

    backward(0, my_core)

    @pl.when(leads)
    def _():
        blocks_over(0).wait_recv()

    @pl.when(jnp.logical_not(leads))
    def _():
        blocks_over(1).wait_recv()

    backward(1, 1 - my_core)

    @pl.when(leads)
    def _():
        blocks_over(1).wait_recv()

    @pl.when(jnp.logical_not(leads))
    def _():
        own_arrived(1)

    backward(my_core, 1)

    all_of(code_send, code_ss.at[0], code_rs.at[0], 2 * others).wait_send()
    all_of(unit_recv, unit_ss.at[0], unit_rs.at[0], others).wait_send()
    all_of(adj_recv, adj_ss.at[0], adj_rs.at[0], others).wait_send()
    for copy in (code_over, unit_over, gain_over, basis_over, blocks_over(0), blocks_over(1)):
        copy.wait_send()


def on_device(
    trade_peers, date_peers,
    basis_values, coefficients, set_map, trade_type, type_gain, set_lags, thresholds,
):
    local_dates, path_count, basis_count = basis_values.shape
    trade_count = coefficients.shape[0]
    set_count = thresholds.shape[0]
    slots = 2 * trade_peers
    chunk = local_dates * path_count // slots
    half_rows = chunk * SPAN
    half = basis_count // 2
    loss_scale = 2.0 / math.sqrt(local_dates * date_peers * path_count)
    vmem_limit = min(60, 20 + 4 * local_dates * path_count // 512) * 1024 * 1024
    vmem = pl.BlockSpec(memory_space=pltpu.VMEM)
    dma = pltpu.SemaphoreType.DMA
    assert date_peers == 2 and trade_peers % GROUP == 0 and trade_peers % (2 * SPAN) == 0
    return pl.pallas_call(
        functools.partial(kernel, trade_peers, loss_scale),
        out_shape=jax.ShapeDtypeStruct((trade_count, half), jnp.float32),
        in_specs=[pl.BlockSpec(memory_space=pltpu.HBM)] * 7,
        out_specs=vmem,
        scratch_shapes=[
            pltpu.VMEM(type_gain.shape, jnp.float32),
            pltpu.VMEM(basis_values.shape, jnp.bfloat16),
            pltpu.VMEM(coefficients.shape, jnp.bfloat16),
            pltpu.VMEM((1, trade_count), jnp.int32),
            pltpu.VMEM((1, trade_count), jnp.int32),
            pltpu.VMEM((1, set_count), jnp.int32),
            pltpu.VMEM((1, set_count), jnp.float32),
            dma((7,)),
            pltpu.VMEM((slots, chunk, set_count), jnp.int16),
            pltpu.VMEM((trade_peers, chunk, set_count), jnp.int16),
            pltpu.VMEM((slots, chunk, set_count), jnp.int16),
            pltpu.VMEM((slots, 1, set_count), jnp.float32),
            pltpu.VMEM((2, trade_peers, 1, set_count), jnp.float32),
            pltpu.VMEM((trade_peers, 2, 1, set_count), jnp.float32),
            pltpu.VMEM(type_gain.shape, jnp.float32),
            pltpu.VMEM(basis_values.shape, jnp.bfloat16),
            pltpu.VMEM((2 * chunk, set_count), jnp.bfloat16),
            pltpu.VMEM((slots, 2 * chunk, set_count), jnp.bfloat16),
            pltpu.VMEM((trade_count, set_count), jnp.bfloat16),
            pltpu.VMEM((trade_count, 2 * half_rows), jnp.float32),
            pltpu.VMEM((slots // SPAN, 2, half_rows, half), jnp.bfloat16),
            dma((1,)), dma((1,)), dma((1,)), dma((1,)), dma((4,)), dma((4,)),
            dma((1,)), dma((2,)), dma((2,)), dma((2,)),
        ],
        compiler_params=pltpu.CompilerParams(
            collective_id=0, has_side_effects=True, vmem_limit_bytes=vmem_limit
        ),
    )(
        *[
            pltpu.with_memory_space_constraint(x, pltpu.HBM)
            for x in (
                type_gain, basis_values, coefficients, set_map.reshape(1, -1),
                trade_type.reshape(1, -1), set_lags.reshape(1, -1), thresholds.reshape(1, -1),
            )
        ]
    )


def solution(mesh):
    return jax.shard_map(
        functools.partial(on_device, mesh.shape["trades"], mesh.shape["dates"]),
        mesh=mesh,
        in_specs=(
            P("dates", "groups", None),
            P("trades", None),
            P("trades"),
            P("trades"),
            P("dates", None),
            P(),
            P(),
        ),
        out_specs=P(("groups", "trades"), "dates"),
        check_vma=False,
    )
```

```python
import functools
import math

import jax
import jax.numpy as jnp
from jax import lax
from jax.experimental import pallas as pl
from jax.experimental.pallas import tpu as pltpu
from jax.sharding import PartitionSpec as P

LAG_MAX = 2
GROUP = 8
SPAN = 4
CODE_MAX = 32767.0
NT = (((1,), (1,)), ((), ()))


def kernel(
    trade_peers, loss_scale,
    gain_in, basis_in, coef_in, set_in, type_in, lag_in, limit_in,
    out_ref,
    gain_ref, basis_ref, coef_ref, set_ref, type_ref, lag_ref, limit_ref, load_sem,
    code_send, code_pass, code_recv, unit_send, unit_both, unit_recv, gain_far, basis_far,
    adj_send, adj_recv, member_ref, gain_cols, basis_rows,
    code_ss, code_rs, unit_ss, unit_rs, pass_ss, pass_rs, adj_ss, adj_rs, half_ss, half_rs,
):
    my_trade = lax.axis_index("trades")
    my_core = lax.axis_index("dates")
    other_core = 1 - my_core
    local_dates, path_count, basis_count = basis_ref.shape
    trade_count = coef_ref.shape[0]
    set_count = limit_ref.shape[1]
    type_count = gain_ref.shape[1]
    others = trade_peers - 1
    core_paths = path_count // 2
    own_paths = core_paths // trade_peers
    core_groups = trade_peers // GROUP
    group_paths = GROUP * own_paths
    group_rows = local_dates * group_paths
    chunk_rows = local_dates * own_paths
    spans = trade_peers // SPAN
    span_paths = SPAN * own_paths
    half_rows = local_dates * span_paths
    half = basis_count // 2
    unroll = trade_peers <= 8

    def partner(step):
        trade = 0
        for bit in range(others.bit_length()):
            weight = 2 ** bit
            mine = (my_trade // weight) % 2
            flip = (step // weight) % 2
            trade += weight * (mine + flip - 2 * mine * flip)
        return trade

    barrier = pltpu.get_barrier_semaphore()

    def greet(step, carry):
        pl.semaphore_signal(
            barrier, inc=1, device_id={"trades": partner(trade_peers - step)},
            device_id_type=pl.DeviceIdType.MESH,
        )
        return carry

    lax.fori_loop(1, trade_peers, greet, 0, unroll=unroll)
    pl.semaphore_signal(
        barrier, inc=1, device_id={"dates": other_core}, device_id_type=pl.DeviceIdType.MESH
    )
    loads = [
        pltpu.make_async_copy(source, target, load_sem.at[i])
        for i, (source, target) in enumerate((
            (type_in, type_ref), (gain_in, gain_ref), (set_in, set_ref), (basis_in, basis_ref),
            (coef_in, coef_ref), (lag_in, lag_ref), (limit_in, limit_ref),
        ))
    ]
    for load in loads:
        load.start()
    for load in loads[:3]:
        load.wait()

    def to_trade(source, target, send_sem, recv_sem, trade):
        return pltpu.make_async_remote_copy(
            src_ref=source, dst_ref=target, send_sem=send_sem, recv_sem=recv_sem,
            device_id={"trades": trade}, device_id_type=pl.DeviceIdType.MESH,
        )

    def to_core(source, target, send_sem, recv_sem):
        return pltpu.make_async_remote_copy(
            src_ref=source, dst_ref=target, send_sem=send_sem, recv_sem=recv_sem,
            device_id={"dates": other_core}, device_id_type=pl.DeviceIdType.MESH,
        )

    def all_of(buffer, send_sem, recv_sem, count):
        slots = buffer.at[pl.ds(0, count)]
        return to_trade(slots, slots, send_sem, recv_sem, my_trade)

    types = type_ref[...]

    def gains_of(table):
        gains = []
        for d in range(local_dates):
            row = jnp.zeros_like(types, dtype=jnp.float32)
            for y in range(type_count):
                row = jnp.where(types == y, table[d:d + 1, y:y + 1], row)
            gains.append(row)
        return gains

    gains = gains_of(gain_ref[...])
    set_ids = lax.broadcasted_iota(jnp.int32, (set_count, trade_count), 0)
    member_wide = jnp.where(set_ids == set_ref[...], 1.0, 0.0)
    member = member_wide.astype(jnp.bfloat16)

    for load in loads[3:]:
        load.wait()

    def forward(group, carry):
        rows = basis_ref[:, pl.ds(pl.multiple_of(group * group_paths, group_paths), group_paths), :]
        raw = lax.dot_general(
            rows.reshape(group_rows, basis_count), coef_ref[...], NT,
            preferred_element_type=jnp.float32,
        )
        prices = jnp.concatenate(
            [raw[d * group_paths:(d + 1) * group_paths] * gains[d] for d in range(local_dates)], axis=0
        ).astype(jnp.bfloat16)
        part = lax.dot_general(prices, member, NT, preferred_element_type=jnp.float32)
        part = part.reshape(local_dates, GROUP, own_paths, set_count)
        for i in range(GROUP):
            chunk = part[:, i].reshape(chunk_rows, set_count)
            top = jnp.maximum(jnp.max(jnp.abs(chunk), axis=0, keepdims=True), 1e-30)
            codes = jnp.round(chunk * (CODE_MAX / top)).astype(jnp.int32)
            code_send[group * GROUP + i] = codes.astype(jnp.int16)
            unit_send[group * GROUP + i] = top * (1.0 / CODE_MAX)

        return carry

    lax.fori_loop(0, 2 * core_groups, forward, 0, unroll=core_groups <= 1)
    pl.semaphore_wait(barrier, trade_peers)
    theirs = pl.ds(other_core * trade_peers, trade_peers)
    code_over = to_core(code_send.at[theirs], code_pass, pass_ss.at[0], pass_rs.at[0])
    unit_over = to_core(
        unit_send.at[theirs], unit_both.at[my_core], pass_ss.at[1], pass_rs.at[1]
    )
    gain_over = to_core(gain_ref, gain_far, pass_ss.at[2], pass_rs.at[2])
    basis_over = to_core(basis_ref, basis_far, pass_ss.at[3], pass_rs.at[3])
    code_over.start()
    unit_over.start()

    def deal(codes, first, dates, units):
        def one(step, carry):
            trade = partner(trade_peers - step)
            slot = dates * trade_peers + my_trade
            to_trade(
                codes.at[first + trade], code_recv.at[slot], code_ss.at[0], code_rs.at[0], trade
            ).start()
            if units:
                to_trade(
                    unit_both.at[:, trade], unit_recv.at[my_trade], unit_ss.at[0], unit_rs.at[0], trade
                ).start()
            return carry

        lax.fori_loop(1, trade_peers, one, 0, unroll=unroll)

    leads = my_core == 1
    mine = my_core * trade_peers
    deal(code_send, mine, my_core, False)
    code_recv[mine + my_trade] = code_send[mine + my_trade]
    unit_both[my_core] = unit_send[pl.ds(mine, trade_peers)]
    member_ref[...] = jnp.transpose(member_wide).astype(jnp.bfloat16)
    code_over.wait_recv()
    unit_over.wait_recv()
    deal(code_pass, 0, other_core, True)
    code_recv[other_core * trade_peers + my_trade] = code_pass[my_trade]
    unit_recv[my_trade] = unit_both[:, my_trade]
    gain_over.start()
    basis_over.start()

    my_columns = pl.ds(pl.multiple_of(my_core * half, half), half)

    def order_rows(source, dates):
        def one(span, carry):
            start = my_core * core_paths + span * span_paths
            start -= (span // spans) * (2 * my_core * core_paths)
            rows = source[:, pl.ds(pl.multiple_of(start, span_paths), span_paths), my_columns]
            rows = rows.astype(jnp.float32)
            for i in range(SPAN):
                block = rows[:, i * own_paths:(i + 1) * own_paths].reshape(chunk_rows, half)
                basis_rows[span, i, dates] = block.astype(jnp.bfloat16)
            return carry

        lax.fori_loop(0, 2 * spans, one, 0, unroll=spans <= 2)

    side = trade_peers // 2
    my_side = my_trade // side
    order_rows(basis_ref, my_core)

    all_of(code_recv, code_ss.at[0], code_rs.at[0], 2 * others).wait_recv()
    all_of(unit_recv, unit_ss.at[0], unit_rs.at[0], others).wait_recv()

    def add(trade, totals):
        result = []
        for q in range(2):
            source = q * trade_peers + trade
            values = code_recv[source].astype(jnp.int32).astype(jnp.float32)
            result.append(totals[q] + values * unit_recv[trade, q])
        return tuple(result)

    totals = lax.fori_loop(
        0, trade_peers, add,
        tuple(jnp.zeros((chunk_rows, set_count), jnp.float32) for _ in range(2)), unroll=unroll,
    )
    netted = [
        totals[q][d * own_paths:(d + 1) * own_paths] for q in range(2) for d in range(local_dates)
    ]
    date_count = len(netted)
    lags = lag_ref[...]
    direct = []
    for d in range(date_count):
        value = netted[d]
        for lag in range(1, LAG_MAX + 1):
            if d >= lag:
                value = value - jnp.where(lags == lag, netted[d - lag], 0.0)
        direct.append(jnp.maximum(value - limit_ref[...], 0.0) * loss_scale)
    parts = []
    for d in range(date_count):
        value = direct[d]
        for lag in range(1, LAG_MAX + 1):
            if d + lag < date_count:
                value = value - jnp.where(lags == lag, direct[d + lag], 0.0)
        parts.append(value)
    adj_send[...] = jnp.concatenate(parts, axis=0).astype(jnp.bfloat16)

    def adj_copy(trade):
        far = my_side + trade // side - 2 * my_side * (trade // side)
        return to_trade(adj_send, adj_recv.at[my_trade], adj_ss.at[0], adj_rs.at[far], trade)

    quarter = trade_peers // 4
    is_last = my_trade // (3 * quarter)

    def spread_out(step, carry):
        part = step // quarter
        trade = step + is_last * quarter * ((part + 3) // 4 - 3 * (part // 3))

        @pl.when(trade != my_trade)
        def _():
            adj_copy(trade).start()

        return carry

    lax.fori_loop(0, trade_peers, spread_out, 0, unroll=unroll)
    adj_recv[my_trade] = adj_send[...]

    gain_over.wait_recv()
    basis_over.wait_recv()
    gains_far = gains_of(gain_far[...])
    gains_all = [jnp.where(my_core == 0, near, far) for near, far in zip(gains, gains_far)]
    gains_all += [jnp.where(my_core == 0, far, near) for near, far in zip(gains, gains_far)]
    wide = [jnp.broadcast_to(row, (own_paths, trade_count)) for row in gains_all]
    gain_cols[...] = jnp.transpose(jnp.concatenate(wide * SPAN, axis=0))
    order_rows(basis_far, other_core)

    def scaled_of(first):
        block = adj_recv[pl.ds(first, SPAN)].reshape(2 * half_rows, set_count)
        spread = lax.dot_general(member_ref[...], block, NT, preferred_element_type=jnp.float32)
        return (spread * gain_cols[...]).astype(jnp.bfloat16)

    def backward(system, far, fresh=False):
        which = my_side + far - 2 * my_side * far

        def one(step, carry):
            span = which * (spans // 2) + step
            rows = basis_rows[system * spans + span].reshape(2 * half_rows, half)
            scaled = scaled_of(system * trade_peers + span * SPAN)
            part = jnp.dot(scaled, rows, preferred_element_type=jnp.float32)
            out_ref[...] = part if fresh else out_ref[...] + part
            return carry

        if fresh and spans > 2:
            out_ref[...] = jnp.zeros_like(out_ref)
            fresh = False
        lax.fori_loop(0, spans // 2, one, 0, unroll=spans <= 2)

    def blocks_over(far):
        first = (my_side + far - 2 * my_side * far) * side
        return to_core(
            adj_recv.at[pl.ds(first, side)], adj_recv.at[pl.ds(trade_peers + first, side)],
            half_ss.at[far], half_rs.at[far],
        )

    def own_arrived(far):
        all_of(adj_recv, adj_ss.at[0], adj_rs.at[far], side - 1 + far).wait_recv()
        blocks_over(far).start()

    @pl.when(leads)
    def _():
        own_arrived(0)

    @pl.when(jnp.logical_not(leads))
    def _():
        blocks_over(0).wait_recv()

    backward(1 - my_core, 0, True)

    @pl.when(leads)
    def _():
        own_arrived(1)

    @pl.when(jnp.logical_not(leads))
    def _():
        own_arrived(0)

    backward(0, my_core)

    @pl.when(leads)
    def _():
        blocks_over(0).wait_recv()

    @pl.when(jnp.logical_not(leads))
    def _():
        blocks_over(1).wait_recv()

    backward(1, 1 - my_core)

    @pl.when(leads)
    def _():
        blocks_over(1).wait_recv()

    @pl.when(jnp.logical_not(leads))
    def _():
        own_arrived(1)

    backward(my_core, 1)

    all_of(code_send, code_ss.at[0], code_rs.at[0], 2 * others).wait_send()
    all_of(unit_recv, unit_ss.at[0], unit_rs.at[0], others).wait_send()
    all_of(adj_recv, adj_ss.at[0], adj_rs.at[0], others).wait_send()
    for copy in (code_over, unit_over, gain_over, basis_over, blocks_over(0), blocks_over(1)):
        copy.wait_send()


def on_device(
    trade_peers, date_peers,
    basis_values, coefficients, set_map, trade_type, type_gain, set_lags, thresholds,
):
    local_dates, path_count, basis_count = basis_values.shape
    trade_count = coefficients.shape[0]
    set_count = thresholds.shape[0]
    slots = 2 * trade_peers
    chunk = local_dates * path_count // slots
    half_rows = chunk * SPAN
    half = basis_count // 2
    loss_scale = 2.0 / math.sqrt(local_dates * date_peers * path_count)
    vmem_limit = min(60, 20 + 4 * local_dates * path_count // 512) * 1024 * 1024
    vmem = pl.BlockSpec(memory_space=pltpu.VMEM)
    dma = pltpu.SemaphoreType.DMA
    assert date_peers == 2 and trade_peers % GROUP == 0 and trade_peers % (2 * SPAN) == 0
    return pl.pallas_call(
        functools.partial(kernel, trade_peers, loss_scale),
        out_shape=jax.ShapeDtypeStruct((trade_count, half), jnp.float32),
        in_specs=[pl.BlockSpec(memory_space=pltpu.HBM)] * 7,
        out_specs=vmem,
        scratch_shapes=[
            pltpu.VMEM(type_gain.shape, jnp.float32),
            pltpu.VMEM(basis_values.shape, jnp.bfloat16),
            pltpu.VMEM(coefficients.shape, jnp.bfloat16),
            pltpu.VMEM((1, trade_count), jnp.int32),
            pltpu.VMEM((1, trade_count), jnp.int32),
            pltpu.VMEM((1, set_count), jnp.int32),
            pltpu.VMEM((1, set_count), jnp.float32),
            dma((7,)),
            pltpu.VMEM((slots, chunk, set_count), jnp.int16),
            pltpu.VMEM((trade_peers, chunk, set_count), jnp.int16),
            pltpu.VMEM((slots, chunk, set_count), jnp.int16),
            pltpu.VMEM((slots, 1, set_count), jnp.float32),
            pltpu.VMEM((2, trade_peers, 1, set_count), jnp.float32),
            pltpu.VMEM((trade_peers, 2, 1, set_count), jnp.float32),
            pltpu.VMEM(type_gain.shape, jnp.float32),
            pltpu.VMEM(basis_values.shape, jnp.bfloat16),
            pltpu.VMEM((2 * chunk, set_count), jnp.bfloat16),
            pltpu.VMEM((slots, 2 * chunk, set_count), jnp.bfloat16),
            pltpu.VMEM((trade_count, set_count), jnp.bfloat16),
            pltpu.VMEM((trade_count, 2 * half_rows), jnp.float32),
            pltpu.VMEM((slots // SPAN, SPAN, 2, chunk, half), jnp.bfloat16),
            dma((1,)), dma((1,)), dma((1,)), dma((1,)), dma((4,)), dma((4,)),
            dma((1,)), dma((2,)), dma((2,)), dma((2,)),
        ],
        compiler_params=pltpu.CompilerParams(
            collective_id=0, has_side_effects=True, vmem_limit_bytes=vmem_limit
        ),
    )(
        *[
            pltpu.with_memory_space_constraint(x, pltpu.HBM)
            for x in (
                type_gain, basis_values, coefficients, set_map.reshape(1, -1),
                trade_type.reshape(1, -1), set_lags.reshape(1, -1), thresholds.reshape(1, -1),
            )
        ]
    )


def solution(mesh):
    return jax.shard_map(
        functools.partial(on_device, mesh.shape["trades"], mesh.shape["dates"]),
        mesh=mesh,
        in_specs=(
            P("dates", "groups", None),
            P("trades", None),
            P("trades"),
            P("trades"),
            P("dates", None),
            P(),
            P(),
        ),
        out_specs=P(("groups", "trades"), "dates"),
        check_vma=False,
    )
```

```python
import functools
import math

import jax
import jax.numpy as jnp
from jax import lax
from jax.experimental import pallas as pl
from jax.experimental.pallas import tpu as pltpu
from jax.sharding import PartitionSpec as P

LAG_MAX = 2
GROUP = 8
SPAN = 4
CODE_MAX = 32767.0
NT = (((1,), (1,)), ((), ()))


def kernel(
    trade_peers, loss_scale,
    gain_in, basis_in, coef_in, set_in, type_in, lag_in, limit_in,
    out_ref,
    gain_ref, basis_ref, coef_ref, set_ref, type_ref, lag_ref, limit_ref, load_sem,
    code_send, code_pass, code_recv, unit_send, unit_both, unit_recv, gain_far, basis_far,
    adj_send, adj_recv, member_ref, gain_cols, basis_rows,
    code_ss, code_rs, unit_ss, unit_rs, pass_ss, pass_rs, adj_ss, adj_rs, half_ss, half_rs,
):
    my_trade = lax.axis_index("trades")
    my_core = lax.axis_index("dates")
    other_core = 1 - my_core
    local_dates, path_count, basis_count = basis_ref.shape
    trade_count = coef_ref.shape[0]
    set_count = limit_ref.shape[1]
    type_count = gain_ref.shape[1]
    others = trade_peers - 1
    core_paths = path_count // 2
    own_paths = core_paths // trade_peers
    core_groups = trade_peers // GROUP
    group_paths = GROUP * own_paths
    group_rows = local_dates * group_paths
    chunk_rows = local_dates * own_paths
    spans = trade_peers // SPAN
    span_paths = SPAN * own_paths
    half_rows = local_dates * span_paths
    half = basis_count // 2
    unroll = trade_peers <= 8

    def partner(step):
        trade = 0
        for bit in range(others.bit_length()):
            weight = 2 ** bit
            mine = (my_trade // weight) % 2
            flip = (step // weight) % 2
            trade += weight * (mine + flip - 2 * mine * flip)
        return trade

    barrier = pltpu.get_barrier_semaphore()

    def greet(step, carry):
        pl.semaphore_signal(
            barrier, inc=1, device_id={"trades": partner(trade_peers - step)},
            device_id_type=pl.DeviceIdType.MESH,
        )
        return carry

    lax.fori_loop(1, trade_peers, greet, 0, unroll=unroll)
    pl.semaphore_signal(
        barrier, inc=1, device_id={"dates": other_core}, device_id_type=pl.DeviceIdType.MESH
    )
    loads = [
        pltpu.make_async_copy(source, target, load_sem.at[i])
        for i, (source, target) in enumerate((
            (type_in, type_ref), (gain_in, gain_ref), (set_in, set_ref),
            (coef_in.at[:trade_count // 2], coef_ref.at[:trade_count // 2]),
            (coef_in.at[trade_count // 2:], coef_ref.at[trade_count // 2:]),
            (basis_in, basis_ref), (lag_in, lag_ref), (limit_in, limit_ref),
        ))
    ]
    for load in loads:
        load.start()
    for load in loads[:3]:
        load.wait()

    def to_trade(source, target, send_sem, recv_sem, trade):
        return pltpu.make_async_remote_copy(
            src_ref=source, dst_ref=target, send_sem=send_sem, recv_sem=recv_sem,
            device_id={"trades": trade}, device_id_type=pl.DeviceIdType.MESH,
        )

    def to_core(source, target, send_sem, recv_sem):
        return pltpu.make_async_remote_copy(
            src_ref=source, dst_ref=target, send_sem=send_sem, recv_sem=recv_sem,
            device_id={"dates": other_core}, device_id_type=pl.DeviceIdType.MESH,
        )

    def all_of(buffer, send_sem, recv_sem, count):
        slots = buffer.at[pl.ds(0, count)]
        return to_trade(slots, slots, send_sem, recv_sem, my_trade)

    types = type_ref[...]

    def gains_of(table):
        gains = []
        for d in range(local_dates):
            row = jnp.zeros_like(types, dtype=jnp.float32)
            for y in range(type_count):
                row = jnp.where(types == y, table[d:d + 1, y:y + 1], row)
            gains.append(row)
        return gains

    gains = gains_of(gain_ref[...])
    set_ids = lax.broadcasted_iota(jnp.int32, (set_count, trade_count), 0)
    member_wide = jnp.where(set_ids == set_ref[...], 1.0, 0.0)
    member = member_wide.astype(jnp.bfloat16)

    for load in loads[3:]:
        load.wait()

    def forward(group, carry):
        rows = basis_ref[:, pl.ds(pl.multiple_of(group * group_paths, group_paths), group_paths), :]
        raw = lax.dot_general(
            rows.reshape(group_rows, basis_count), coef_ref[...], NT,
            preferred_element_type=jnp.float32,
        )
        prices = jnp.concatenate(
            [raw[d * group_paths:(d + 1) * group_paths] * gains[d] for d in range(local_dates)], axis=0
        ).astype(jnp.bfloat16)
        part = lax.dot_general(prices, member, NT, preferred_element_type=jnp.float32)
        part = part.reshape(local_dates, GROUP, own_paths, set_count)
        for i in range(GROUP):
            chunk = part[:, i].reshape(chunk_rows, set_count)
            top = jnp.maximum(jnp.max(jnp.abs(chunk), axis=0, keepdims=True), 1e-30)
            codes = jnp.round(chunk * (CODE_MAX / top)).astype(jnp.int32)
            code_send[group * GROUP + i] = codes.astype(jnp.int16)
            unit_send[group * GROUP + i] = top * (1.0 / CODE_MAX)

        return carry

    lax.fori_loop(0, 2 * core_groups, forward, 0, unroll=core_groups <= 1)
    pl.semaphore_wait(barrier, trade_peers)
    theirs = pl.ds(other_core * trade_peers, trade_peers)
    code_over = to_core(code_send.at[theirs], code_pass, pass_ss.at[0], pass_rs.at[0])
    unit_over = to_core(
        unit_send.at[theirs], unit_both.at[my_core], pass_ss.at[1], pass_rs.at[1]
    )
    gain_over = to_core(gain_ref, gain_far, pass_ss.at[2], pass_rs.at[2])
    basis_over = to_core(basis_ref, basis_far, pass_ss.at[3], pass_rs.at[3])
    code_over.start()
    unit_over.start()

    def deal(codes, first, dates, units):
        def one(step, carry):
            trade = partner(trade_peers - step)
            slot = dates * trade_peers + my_trade
            to_trade(
                codes.at[first + trade], code_recv.at[slot], code_ss.at[0], code_rs.at[0], trade
            ).start()
            if units:
                to_trade(
                    unit_both.at[:, trade], unit_recv.at[my_trade], unit_ss.at[0], unit_rs.at[0], trade
                ).start()
            return carry

        lax.fori_loop(1, trade_peers, one, 0, unroll=unroll)

    leads = my_core == 1
    mine = my_core * trade_peers
    deal(code_send, mine, my_core, False)
    code_recv[mine + my_trade] = code_send[mine + my_trade]
    unit_both[my_core] = unit_send[pl.ds(mine, trade_peers)]
    member_ref[...] = jnp.transpose(member_wide).astype(jnp.bfloat16)
    code_over.wait_recv()
    unit_over.wait_recv()
    deal(code_pass, 0, other_core, True)
    code_recv[other_core * trade_peers + my_trade] = code_pass[my_trade]
    unit_recv[my_trade] = unit_both[:, my_trade]
    gain_over.start()
    basis_over.start()

    my_columns = pl.ds(pl.multiple_of(my_core * half, half), half)

    def order_rows(source, dates):
        def one(span, carry):
            start = my_core * core_paths + span * span_paths
            start -= (span // spans) * (2 * my_core * core_paths)
            rows = source[:, pl.ds(pl.multiple_of(start, span_paths), span_paths), my_columns]
            rows = rows.astype(jnp.float32)
            for i in range(SPAN):
                block = rows[:, i * own_paths:(i + 1) * own_paths].reshape(chunk_rows, half)
                basis_rows[span, i, dates] = block.astype(jnp.bfloat16)
            return carry

        lax.fori_loop(0, 2 * spans, one, 0, unroll=spans <= 2)

    side = trade_peers // 2
    my_side = my_trade // side
    order_rows(basis_ref, my_core)

    all_of(code_recv, code_ss.at[0], code_rs.at[0], 2 * others).wait_recv()
    all_of(unit_recv, unit_ss.at[0], unit_rs.at[0], others).wait_recv()

    def add(trade, totals):
        result = []
        for q in range(2):
            source = q * trade_peers + trade
            values = code_recv[source].astype(jnp.int32).astype(jnp.float32)
            result.append(totals[q] + values * unit_recv[trade, q])
        return tuple(result)

    totals = lax.fori_loop(
        0, trade_peers, add,
        tuple(jnp.zeros((chunk_rows, set_count), jnp.float32) for _ in range(2)), unroll=unroll,
    )
    netted = [
        totals[q][d * own_paths:(d + 1) * own_paths] for q in range(2) for d in range(local_dates)
    ]
    date_count = len(netted)
    lags = lag_ref[...]
    direct = []
    for d in range(date_count):
        value = netted[d]
        for lag in range(1, LAG_MAX + 1):
            if d >= lag:
                value = value - jnp.where(lags == lag, netted[d - lag], 0.0)
        direct.append(jnp.maximum(value - limit_ref[...], 0.0) * loss_scale)
    parts = []
    for d in range(date_count):
        value = direct[d]
        for lag in range(1, LAG_MAX + 1):
            if d + lag < date_count:
                value = value - jnp.where(lags == lag, direct[d + lag], 0.0)
        parts.append(value)
    adj_send[...] = jnp.concatenate(parts, axis=0).astype(jnp.bfloat16)

    def adj_copy(trade):
        far = my_side + trade // side - 2 * my_side * (trade // side)
        return to_trade(adj_send, adj_recv.at[my_trade], adj_ss.at[0], adj_rs.at[far], trade)

    quarter = trade_peers // 4
    is_last = my_trade // (3 * quarter)

    def spread_out(step, carry):
        part = step // quarter
        trade = step + is_last * quarter * ((part + 3) // 4 - 3 * (part // 3))

        @pl.when(trade != my_trade)
        def _():
            adj_copy(trade).start()

        return carry

    lax.fori_loop(0, trade_peers, spread_out, 0, unroll=unroll)
    adj_recv[my_trade] = adj_send[...]

    gain_over.wait_recv()
    basis_over.wait_recv()
    gains_far = gains_of(gain_far[...])
    gains_all = [jnp.where(my_core == 0, near, far) for near, far in zip(gains, gains_far)]
    gains_all += [jnp.where(my_core == 0, far, near) for near, far in zip(gains, gains_far)]
    wide = [jnp.broadcast_to(row, (own_paths, trade_count)) for row in gains_all]
    gain_cols[...] = jnp.transpose(jnp.concatenate(wide * SPAN, axis=0))
    order_rows(basis_far, other_core)

    def scaled_of(first):
        block = adj_recv[pl.ds(first, SPAN)].reshape(2 * half_rows, set_count)
        spread = lax.dot_general(member_ref[...], block, NT, preferred_element_type=jnp.float32)
        return (spread * gain_cols[...]).astype(jnp.bfloat16)

    def backward(system, far, fresh=False):
        which = my_side + far - 2 * my_side * far

        def one(step, carry):
            span = which * (spans // 2) + step
            rows = basis_rows[system * spans + span].reshape(2 * half_rows, half)
            scaled = scaled_of(system * trade_peers + span * SPAN)
            part = jnp.dot(scaled, rows, preferred_element_type=jnp.float32)
            out_ref[...] = part if fresh else out_ref[...] + part
            return carry

        if fresh and spans > 2:
            out_ref[...] = jnp.zeros_like(out_ref)
            fresh = False
        lax.fori_loop(0, spans // 2, one, 0, unroll=spans <= 2)

    def blocks_over(far):
        first = (my_side + far - 2 * my_side * far) * side
        return to_core(
            adj_recv.at[pl.ds(first, side)], adj_recv.at[pl.ds(trade_peers + first, side)],
            half_ss.at[far], half_rs.at[far],
        )

    def own_arrived(far):
        all_of(adj_recv, adj_ss.at[0], adj_rs.at[far], side - 1 + far).wait_recv()
        blocks_over(far).start()

    @pl.when(leads)
    def _():
        own_arrived(0)

    @pl.when(jnp.logical_not(leads))
    def _():
        blocks_over(0).wait_recv()

    backward(1 - my_core, 0, True)

    @pl.when(leads)
    def _():
        own_arrived(1)

    @pl.when(jnp.logical_not(leads))
    def _():
        own_arrived(0)

    backward(0, my_core)

    @pl.when(leads)
    def _():
        blocks_over(0).wait_recv()

    @pl.when(jnp.logical_not(leads))
    def _():
        blocks_over(1).wait_recv()

    backward(1, 1 - my_core)

    @pl.when(leads)
    def _():
        blocks_over(1).wait_recv()

    @pl.when(jnp.logical_not(leads))
    def _():
        own_arrived(1)

    backward(my_core, 1)

    all_of(code_send, code_ss.at[0], code_rs.at[0], 2 * others).wait_send()
    all_of(unit_recv, unit_ss.at[0], unit_rs.at[0], others).wait_send()
    all_of(adj_recv, adj_ss.at[0], adj_rs.at[0], others).wait_send()
    for copy in (code_over, unit_over, gain_over, basis_over, blocks_over(0), blocks_over(1)):
        copy.wait_send()


def on_device(
    trade_peers, date_peers,
    basis_values, coefficients, set_map, trade_type, type_gain, set_lags, thresholds,
):
    local_dates, path_count, basis_count = basis_values.shape
    trade_count = coefficients.shape[0]
    set_count = thresholds.shape[0]
    slots = 2 * trade_peers
    chunk = local_dates * path_count // slots
    half_rows = chunk * SPAN
    half = basis_count // 2
    loss_scale = 2.0 / math.sqrt(local_dates * date_peers * path_count)
    vmem_limit = min(60, 20 + 4 * local_dates * path_count // 512) * 1024 * 1024
    vmem = pl.BlockSpec(memory_space=pltpu.VMEM)
    dma = pltpu.SemaphoreType.DMA
    assert date_peers == 2 and trade_peers % GROUP == 0 and trade_peers % (2 * SPAN) == 0
    return pl.pallas_call(
        functools.partial(kernel, trade_peers, loss_scale),
        out_shape=jax.ShapeDtypeStruct((trade_count, half), jnp.float32),
        in_specs=[pl.BlockSpec(memory_space=pltpu.HBM)] * 7,
        out_specs=vmem,
        scratch_shapes=[
            pltpu.VMEM(type_gain.shape, jnp.float32),
            pltpu.VMEM(basis_values.shape, jnp.bfloat16),
            pltpu.VMEM(coefficients.shape, jnp.bfloat16),
            pltpu.VMEM((1, trade_count), jnp.int32),
            pltpu.VMEM((1, trade_count), jnp.int32),
            pltpu.VMEM((1, set_count), jnp.int32),
            pltpu.VMEM((1, set_count), jnp.float32),
            dma((8,)),
            pltpu.VMEM((slots, chunk, set_count), jnp.int16),
            pltpu.VMEM((trade_peers, chunk, set_count), jnp.int16),
            pltpu.VMEM((slots, chunk, set_count), jnp.int16),
            pltpu.VMEM((slots, 1, set_count), jnp.float32),
            pltpu.VMEM((2, trade_peers, 1, set_count), jnp.float32),
            pltpu.VMEM((trade_peers, 2, 1, set_count), jnp.float32),
            pltpu.VMEM(type_gain.shape, jnp.float32),
            pltpu.VMEM(basis_values.shape, jnp.bfloat16),
            pltpu.VMEM((2 * chunk, set_count), jnp.bfloat16),
            pltpu.VMEM((slots, 2 * chunk, set_count), jnp.bfloat16),
            pltpu.VMEM((trade_count, set_count), jnp.bfloat16),
            pltpu.VMEM((trade_count, 2 * half_rows), jnp.float32),
            pltpu.VMEM((slots // SPAN, SPAN, 2, chunk, half), jnp.bfloat16),
            dma((1,)), dma((1,)), dma((1,)), dma((1,)), dma((4,)), dma((4,)),
            dma((1,)), dma((2,)), dma((2,)), dma((2,)),
        ],
        compiler_params=pltpu.CompilerParams(
            collective_id=0, has_side_effects=True, vmem_limit_bytes=vmem_limit
        ),
    )(
        *[
            pltpu.with_memory_space_constraint(x, pltpu.HBM)
            for x in (
                type_gain, basis_values, coefficients, set_map.reshape(1, -1),
                trade_type.reshape(1, -1), set_lags.reshape(1, -1), thresholds.reshape(1, -1),
            )
        ]
    )


def solution(mesh):
    return jax.shard_map(
        functools.partial(on_device, mesh.shape["trades"], mesh.shape["dates"]),
        mesh=mesh,
        in_specs=(
            P("dates", "groups", None),
            P("trades", None),
            P("trades"),
            P("trades"),
            P("dates", None),
            P(),
            P(),
        ),
        out_specs=P(("groups", "trades"), "dates"),
        check_vma=False,
    )
```

```python
import functools
import math

import jax
import jax.numpy as jnp
from jax import lax
from jax.experimental import pallas as pl
from jax.experimental.pallas import tpu as pltpu
from jax.sharding import PartitionSpec as P

LAG_MAX = 2
GROUP = 8
SPAN = 4
CODE_MAX = 32767.0
NT = (((1,), (1,)), ((), ()))


def kernel(
    trade_peers, loss_scale,
    gain_in, basis_in, coef_in, set_in, type_in, lag_in, limit_in,
    out_ref,
    gain_ref, basis_ref, coef_ref, set_ref, type_ref, lag_ref, limit_ref, load_sem,
    code_send, code_pass, code_recv, unit_send, unit_both, unit_recv, gain_far, basis_far,
    adj_send, adj_recv, member_ref, gain_cols, basis_rows,
    code_ss, code_rs, unit_ss, unit_rs, pass_ss, pass_rs, adj_ss, adj_rs, half_ss, half_rs,
):
    my_trade = lax.axis_index("trades")
    my_core = lax.axis_index("dates")
    other_core = 1 - my_core
    local_dates, path_count, basis_count = basis_ref.shape
    trade_count = coef_ref.shape[0]
    set_count = limit_ref.shape[1]
    type_count = gain_ref.shape[1]
    others = trade_peers - 1
    core_paths = path_count // 2
    own_paths = core_paths // trade_peers
    core_groups = trade_peers // GROUP
    group_paths = GROUP * own_paths
    group_rows = local_dates * group_paths
    chunk_rows = local_dates * own_paths
    spans = trade_peers // SPAN
    span_paths = SPAN * own_paths
    half_rows = local_dates * span_paths
    half = basis_count // 2
    unroll = trade_peers <= 8

    def partner(step):
        trade = 0
        for bit in range(others.bit_length()):
            weight = 2 ** bit
            mine = (my_trade // weight) % 2
            flip = (step // weight) % 2
            trade += weight * (mine + flip - 2 * mine * flip)
        return trade

    barrier = pltpu.get_barrier_semaphore()

    def greet(step, carry):
        pl.semaphore_signal(
            barrier, inc=1, device_id={"trades": partner(trade_peers - step)},
            device_id_type=pl.DeviceIdType.MESH,
        )
        return carry

    lax.fori_loop(1, trade_peers, greet, 0, unroll=unroll)
    pl.semaphore_signal(
        barrier, inc=1, device_id={"dates": other_core}, device_id_type=pl.DeviceIdType.MESH
    )
    loads = [
        pltpu.make_async_copy(source, target, load_sem.at[i])
        for i, (source, target) in enumerate((
            (type_in, type_ref), (gain_in, gain_ref), (set_in, set_ref),
            (coef_in.at[:trade_count // 2], coef_ref.at[:trade_count // 2]),
            (coef_in.at[trade_count // 2:], coef_ref.at[trade_count // 2:]),
            (basis_in, basis_ref), (lag_in, lag_ref), (limit_in, limit_ref),
        ))
    ]
    for load in loads:
        load.start()
    for load in loads[:3]:
        load.wait()

    def to_trade(source, target, send_sem, recv_sem, trade):
        return pltpu.make_async_remote_copy(
            src_ref=source, dst_ref=target, send_sem=send_sem, recv_sem=recv_sem,
            device_id={"trades": trade}, device_id_type=pl.DeviceIdType.MESH,
        )

    def to_core(source, target, send_sem, recv_sem):
        return pltpu.make_async_remote_copy(
            src_ref=source, dst_ref=target, send_sem=send_sem, recv_sem=recv_sem,
            device_id={"dates": other_core}, device_id_type=pl.DeviceIdType.MESH,
        )

    def all_of(buffer, send_sem, recv_sem, count):
        slots = buffer.at[pl.ds(0, count)]
        return to_trade(slots, slots, send_sem, recv_sem, my_trade)

    types = type_ref[...]

    def gains_of(table):
        gains = []
        for d in range(local_dates):
            row = jnp.zeros_like(types, dtype=jnp.float32)
            for y in range(type_count):
                row = jnp.where(types == y, table[d:d + 1, y:y + 1], row)
            gains.append(row)
        return gains

    gains = gains_of(gain_ref[...])
    set_ids = lax.broadcasted_iota(jnp.int32, (set_count, trade_count), 0)
    member_wide = jnp.where(set_ids == set_ref[...], 1.0, 0.0)
    member = member_wide.astype(jnp.bfloat16)

    for load in loads[3:]:
        load.wait()

    def forward(group, carry):
        rows = basis_ref[:, pl.ds(pl.multiple_of(group * group_paths, group_paths), group_paths), :]
        raw = lax.dot_general(
            rows.reshape(group_rows, basis_count), coef_ref[...], NT,
            preferred_element_type=jnp.float32,
        )
        prices = jnp.concatenate(
            [raw[d * group_paths:(d + 1) * group_paths] * gains[d] for d in range(local_dates)], axis=0
        ).astype(jnp.bfloat16)
        part = lax.dot_general(prices, member, NT, preferred_element_type=jnp.float32)
        part = part.reshape(local_dates, GROUP, own_paths, set_count)
        for i in range(GROUP):
            chunk = part[:, i].reshape(chunk_rows, set_count)
            top = jnp.maximum(jnp.max(jnp.abs(chunk), axis=0, keepdims=True), 1e-30)
            codes = jnp.round(chunk * (CODE_MAX / top)).astype(jnp.int32)
            code_send[group * GROUP + i] = codes.astype(jnp.int16)
            unit_send[group * GROUP + i] = top * (1.0 / CODE_MAX)

        return carry

    lax.fori_loop(0, 2 * core_groups, forward, 0, unroll=core_groups <= 1)
    pl.semaphore_wait(barrier, trade_peers)
    theirs = pl.ds(other_core * trade_peers, trade_peers)
    code_over = to_core(code_send.at[theirs], code_pass, pass_ss.at[0], pass_rs.at[0])
    unit_over = to_core(
        unit_send.at[theirs], unit_both.at[my_core], pass_ss.at[1], pass_rs.at[1]
    )
    gain_over = to_core(gain_ref, gain_far, pass_ss.at[2], pass_rs.at[2])
    basis_over = to_core(basis_ref, basis_far, pass_ss.at[3], pass_rs.at[3])
    code_over.start()
    unit_over.start()

    def deal(codes, first, dates, units):
        def one(step, carry):
            trade = partner(trade_peers - step)
            slot = dates * trade_peers + my_trade
            to_trade(
                codes.at[first + trade], code_recv.at[slot], code_ss.at[0], code_rs.at[0], trade
            ).start()
            if units:
                to_trade(
                    unit_both.at[:, trade], unit_recv.at[my_trade], unit_ss.at[0], unit_rs.at[0], trade
                ).start()
            return carry

        lax.fori_loop(1, trade_peers, one, 0, unroll=unroll)

    leads = my_core == 1
    mine = my_core * trade_peers
    deal(code_send, mine, my_core, False)
    code_recv[mine + my_trade] = code_send[mine + my_trade]
    unit_both[my_core] = unit_send[pl.ds(mine, trade_peers)]
    member_ref[...] = jnp.transpose(member_wide).astype(jnp.bfloat16)
    code_over.wait_recv()
    unit_over.wait_recv()
    deal(code_pass, 0, other_core, True)
    code_recv[other_core * trade_peers + my_trade] = code_pass[my_trade]
    unit_recv[my_trade] = unit_both[:, my_trade]
    gain_over.start()
    basis_over.start()

    my_columns = pl.ds(pl.multiple_of(my_core * half, half), half)

    def order_rows(source, dates):
        def one(span, carry):
            start = my_core * core_paths + span * span_paths
            start -= (span // spans) * (2 * my_core * core_paths)
            rows = source[:, pl.ds(pl.multiple_of(start, span_paths), span_paths), my_columns]
            rows = rows.astype(jnp.float32)
            for i in range(SPAN):
                block = rows[:, i * own_paths:(i + 1) * own_paths].reshape(chunk_rows, half)
                basis_rows[span, i, dates] = block.astype(jnp.bfloat16)
            return carry

        lax.fori_loop(0, 2 * spans, one, 0, unroll=spans <= 2)

    side = trade_peers // 2
    my_side = my_trade // side
    order_rows(basis_ref, my_core)

    all_of(code_recv, code_ss.at[0], code_rs.at[0], 2 * others).wait_recv()
    all_of(unit_recv, unit_ss.at[0], unit_rs.at[0], others).wait_recv()

    def add(trade, totals):
        result = []
        for q in range(2):
            source = q * trade_peers + trade
            values = code_recv[source].astype(jnp.int32).astype(jnp.float32)
            result.append(totals[q] + values * unit_recv[trade, q])
        return tuple(result)

    totals = lax.fori_loop(
        0, trade_peers, add,
        tuple(jnp.zeros((chunk_rows, set_count), jnp.float32) for _ in range(2)), unroll=unroll,
    )
    netted = [
        totals[q][d * own_paths:(d + 1) * own_paths] for q in range(2) for d in range(local_dates)
    ]
    date_count = len(netted)
    lags = lag_ref[...]
    direct = []
    for d in range(date_count):
        value = netted[d]
        for lag in range(1, LAG_MAX + 1):
            if d >= lag:
                value = value - jnp.where(lags == lag, netted[d - lag], 0.0)
        direct.append(jnp.maximum(value - limit_ref[...], 0.0) * loss_scale)
    parts = []
    for d in range(date_count):
        value = direct[d]
        for lag in range(1, LAG_MAX + 1):
            if d + lag < date_count:
                value = value - jnp.where(lags == lag, direct[d + lag], 0.0)
        parts.append(value)
    adj_send[...] = jnp.concatenate(parts, axis=0).astype(jnp.bfloat16)

    outer = 1 - ((my_trade // (side // 2) + 1) // 2) % 2

    def adj_copy(trade):
        far = my_side + trade // side - 2 * my_side * (trade // side)
        return to_trade(adj_send, adj_recv.at[my_trade], adj_ss.at[0], adj_rs.at[far * (1 + outer)], trade)

    quarter = trade_peers // 4
    is_last = my_trade // (3 * quarter)

    def spread_out(step, carry):
        part = step // quarter
        trade = step + is_last * quarter * ((part + 3) // 4 - 3 * (part // 3))

        @pl.when(trade != my_trade)
        def _():
            adj_copy(trade).start()

        return carry

    lax.fori_loop(0, trade_peers, spread_out, 0, unroll=unroll)
    adj_recv[my_trade] = adj_send[...]

    gain_over.wait_recv()
    basis_over.wait_recv()
    gains_far = gains_of(gain_far[...])
    gains_all = [jnp.where(my_core == 0, near, far) for near, far in zip(gains, gains_far)]
    gains_all += [jnp.where(my_core == 0, far, near) for near, far in zip(gains, gains_far)]
    wide = [jnp.broadcast_to(row, (own_paths, trade_count)) for row in gains_all]
    gain_cols[...] = jnp.transpose(jnp.concatenate(wide * SPAN, axis=0))
    order_rows(basis_far, other_core)

    def scaled_of(first):
        block = adj_recv[pl.ds(first, SPAN)].reshape(2 * half_rows, set_count)
        spread = lax.dot_general(member_ref[...], block, NT, preferred_element_type=jnp.float32)
        return (spread * gain_cols[...]).astype(jnp.bfloat16)

    def backward(system, far, fresh=False):
        which = my_side + far - 2 * my_side * far

        def one(step, carry):
            span = which * (spans // 2) + step
            rows = basis_rows[system * spans + span].reshape(2 * half_rows, half)
            scaled = scaled_of(system * trade_peers + span * SPAN)
            part = jnp.dot(scaled, rows, preferred_element_type=jnp.float32)
            out_ref[...] = part if fresh else out_ref[...] + part
            return carry

        if fresh and spans > 2:
            out_ref[...] = jnp.zeros_like(out_ref)
            fresh = False
        lax.fori_loop(0, spans // 2, one, 0, unroll=spans <= 2)

    def blocks_over(level):
        first = (my_side * side, (2 - my_side) * (side // 2), (3 - 3 * my_side) * (side // 2))[level]
        count = side if level == 0 else side // 2
        return to_core(
            adj_recv.at[pl.ds(first, count)], adj_recv.at[pl.ds(trade_peers + first, count)],
            half_ss.at[level], half_rs.at[level],
        )

    def own_arrived(far):
        for level in (1, 2) if far else (0,):
            count = side // 2 if far else side - 1
            all_of(adj_recv, adj_ss.at[0], adj_rs.at[level], count).wait_recv()
            blocks_over(level).start()

    @pl.when(leads)
    def _():
        own_arrived(0)

    @pl.when(jnp.logical_not(leads))
    def _():
        blocks_over(0).wait_recv()

    backward(1 - my_core, 0, True)

    @pl.when(leads)
    def _():
        own_arrived(1)

    @pl.when(jnp.logical_not(leads))
    def _():
        own_arrived(0)

    backward(0, my_core)

    @pl.when(leads)
    def _():
        blocks_over(0).wait_recv()

    @pl.when(jnp.logical_not(leads))
    def _():
        blocks_over(1).wait_recv()
        blocks_over(2).wait_recv()

    backward(1, 1 - my_core)

    @pl.when(leads)
    def _():
        blocks_over(1).wait_recv()
        blocks_over(2).wait_recv()

    @pl.when(jnp.logical_not(leads))
    def _():
        own_arrived(1)

    backward(my_core, 1)

    all_of(code_send, code_ss.at[0], code_rs.at[0], 2 * others).wait_send()
    all_of(unit_recv, unit_ss.at[0], unit_rs.at[0], others).wait_send()
    all_of(adj_recv, adj_ss.at[0], adj_rs.at[0], others).wait_send()
    for copy in (code_over, unit_over, gain_over, basis_over, *map(blocks_over, range(3))):
        copy.wait_send()


def on_device(
    trade_peers, date_peers,
    basis_values, coefficients, set_map, trade_type, type_gain, set_lags, thresholds,
):
    local_dates, path_count, basis_count = basis_values.shape
    trade_count = coefficients.shape[0]
    set_count = thresholds.shape[0]
    slots = 2 * trade_peers
    chunk = local_dates * path_count // slots
    half_rows = chunk * SPAN
    half = basis_count // 2
    loss_scale = 2.0 / math.sqrt(local_dates * date_peers * path_count)
    vmem_limit = min(60, 20 + 4 * local_dates * path_count // 512) * 1024 * 1024
    vmem = pl.BlockSpec(memory_space=pltpu.VMEM)
    dma = pltpu.SemaphoreType.DMA
    assert date_peers == 2 and trade_peers % GROUP == 0 and trade_peers % (2 * SPAN) == 0
    return pl.pallas_call(
        functools.partial(kernel, trade_peers, loss_scale),
        out_shape=jax.ShapeDtypeStruct((trade_count, half), jnp.float32),
        in_specs=[pl.BlockSpec(memory_space=pltpu.HBM)] * 7,
        out_specs=vmem,
        scratch_shapes=[
            pltpu.VMEM(type_gain.shape, jnp.float32),
            pltpu.VMEM(basis_values.shape, jnp.bfloat16),
            pltpu.VMEM(coefficients.shape, jnp.bfloat16),
            pltpu.VMEM((1, trade_count), jnp.int32),
            pltpu.VMEM((1, trade_count), jnp.int32),
            pltpu.VMEM((1, set_count), jnp.int32),
            pltpu.VMEM((1, set_count), jnp.float32),
            dma((8,)),
            pltpu.VMEM((slots, chunk, set_count), jnp.int16),
            pltpu.VMEM((trade_peers, chunk, set_count), jnp.int16),
            pltpu.VMEM((slots, chunk, set_count), jnp.int16),
            pltpu.VMEM((slots, 1, set_count), jnp.float32),
            pltpu.VMEM((2, trade_peers, 1, set_count), jnp.float32),
            pltpu.VMEM((trade_peers, 2, 1, set_count), jnp.float32),
            pltpu.VMEM(type_gain.shape, jnp.float32),
            pltpu.VMEM(basis_values.shape, jnp.bfloat16),
            pltpu.VMEM((2 * chunk, set_count), jnp.bfloat16),
            pltpu.VMEM((slots, 2 * chunk, set_count), jnp.bfloat16),
            pltpu.VMEM((trade_count, set_count), jnp.bfloat16),
            pltpu.VMEM((trade_count, 2 * half_rows), jnp.float32),
            pltpu.VMEM((slots // SPAN, SPAN, 2, chunk, half), jnp.bfloat16),
            dma((1,)), dma((1,)), dma((1,)), dma((1,)), dma((4,)), dma((4,)),
            dma((1,)), dma((3,)), dma((3,)), dma((3,)),
        ],
        compiler_params=pltpu.CompilerParams(
            collective_id=0, has_side_effects=True, vmem_limit_bytes=vmem_limit
        ),
    )(
        *[
            pltpu.with_memory_space_constraint(x, pltpu.HBM)
            for x in (
                type_gain, basis_values, coefficients, set_map.reshape(1, -1),
                trade_type.reshape(1, -1), set_lags.reshape(1, -1), thresholds.reshape(1, -1),
            )
        ]
    )


def solution(mesh):
    return jax.shard_map(
        functools.partial(on_device, mesh.shape["trades"], mesh.shape["dates"]),
        mesh=mesh,
        in_specs=(
            P("dates", "groups", None),
            P("trades", None),
            P("trades"),
            P("trades"),
            P("dates", None),
            P(),
            P(),
        ),
        out_specs=P(("groups", "trades"), "dates"),
        check_vma=False,
    )
```
